128 devices in a mesh: expert: 16 (over x, z_hi, core), dp: 8 (over y, z_lo).
Axes of the slice: x: 4, y: 4, z: 4 (z_hi: 2, z_lo: 2; z = z_hi * 2 + z_lo), core: 2. Of those that a mesh axis runs over, the one named last changes fastest.
Arguments:
- rows_x: bfloat16 [4096, 4096], P('expert'), may hold values from -6 to 6
- rows_dy: bfloat16 [4096, 4096], P('expert'), may hold values from -2 to 2
- router_logits: float32 [4096, 16], P('expert'), may hold values from -7.5 to 307.5
- expert_of: int32 [4096, 1], P('expert'), may hold values from 0 to 15, as said below
- w_gate: bfloat16 [16, 1536, 4096], P('expert', 'dp'), may hold values from -0.09375 to 0.09375
- w_up: bfloat16 [16, 1536, 4096], P('expert', 'dp'), may hold values from -0.09375 to 0.09375
- w_down: bfloat16 [16, 1536, 4096], P('expert', 'dp'), may hold values from -0.15625 to 0.15625
Outputs:
- grad_rows: bfloat16 [4096, 4096], P('expert', 'dp')
- grad_logits: float32 [4096, 16], P('expert')
- grad_gate: float32 [16, 1536, 4096], P('expert', 'dp')
- grad_up: float32 [16, 1536, 4096], P('expert', 'dp')
- grad_down: float32 [16, 1536, 4096], P('expert', 'dp')
- grad_norm: float32 [], replicated
The draws below stay inside these ranges and needn't reach their ends.
Inputs may be any that keep to these rules, and one draw needn't show every extreme that they name: `expert_of`: one expert, the same in every aligned block of 256 rows, is named by exactly 64 rows of each block; a second expert, the same in every block, by exactly 32 rows of each block; every other expert by at most 32 rows of a block.
All inputs are finite; a program needn't handle non-finite values.
Results may differ from the reference program's by a relative error of at most 0.015.
Values may be sent and summed in bfloat16 or wider, within the bound.
A program may use at most 192 MiB of HBM per device.

```python
from functools import partial
import jax
import jax.numpy as jnp
from jax import lax

D = 4096
FF = 1536
R_DEV = 256
HOT = 1
EXPERTS = 16
CAP = 64
COLD_CAP = 32
ROWS = 4096
N_DP = 8


def draw_router_logits(key, part):
    base_key = jax.random.fold_in(jax.random.fold_in(key, 71), 0)
    scores = jnp.clip(1.5 * jax.random.normal(base_key, (ROWS, EXPERTS), jnp.float32), -7.5, 7.5)
    return scores


def draw_expert_of(key, part):
    base_key = jax.random.fold_in(key, 29)
    hot_key, full_key, block_key = jax.random.split(base_key, 3)
    hot_expert = jax.random.randint(hot_key, (), 0, EXPERTS).astype(jnp.int32)
    full_cold = jax.random.randint(full_key, (), 0, EXPERTS - 1).astype(jnp.int32)
    cold_slots = (EXPERTS - 1) * COLD_CAP
    cold_rows = R_DEV - CAP
    owner = jnp.repeat(jnp.arange(EXPERTS - 1, dtype=jnp.int32), COLD_CAP, total_repeat_length=cold_slots)

    def one_block(block_seed):
        pick_key, order_key = jax.random.split(block_seed)
        rank_key = jax.random.permutation(pick_key, cold_slots).astype(jnp.int32)
        priority = jnp.where(owner == full_cold, -1, rank_key)
        chosen = owner[jnp.argsort(priority, stable=True)[:cold_rows]]
        chosen = chosen + (chosen >= hot_expert).astype(jnp.int32)
        block = jnp.concatenate([jnp.full((CAP,), hot_expert, jnp.int32), chosen])
        return jax.random.permutation(order_key, block)
    blocks = jax.vmap(one_block)(jax.random.split(block_key, ROWS // R_DEV))
    return blocks.reshape(ROWS, 1).astype(jnp.int32)


def shard_levels(rng, shape, pieces, smallest, high):
    loudness = 1.0
    for axis_at, shards_of in pieces:
        steps = jax.random.uniform(jax.random.fold_in(jax.random.fold_in(rng, 6), axis_at), (shards_of,), jnp.float32, smallest / len(pieces), high / len(pieces))
        loudness = loudness * jnp.repeat(jnp.exp(steps), shape[axis_at] // shards_of).reshape((-1,) + (1,) * (len(shape) - 1 - axis_at))
    return loudness


def scatter_about(key, extent, deviation, limit, cuts=(), held_as=jnp.bfloat16):
    entries = jax.random.normal(key, extent, jnp.float32) * deviation
    if len(cuts) > 0:
        entries = shard_levels(key, extent, cuts, -0.22, 0.18) * entries
    return jnp.clip(entries, min=-limit, max=limit).astype(held_as)


def setup_inputs(seed: int = 0) -> dict:
    keys = jax.random.split(jax.random.key(seed), 8)
    return {
        "rows_x": scatter_about(keys[0], (ROWS, D), 1.0, 6.0, ((0, 16),)),
        "rows_dy": scatter_about(keys[1], (ROWS, D), 0.25, 2.0, ((0, 16),)),
        "router_logits": draw_router_logits(jax.random.fold_in(keys[7], 71), 0),
        "expert_of": draw_expert_of(jax.random.fold_in(keys[7], 71), 0),
        "w_gate": scatter_about(keys[4], (EXPERTS, FF, D), D ** -0.5, 0.09375, ((0, 16), (1, 8))),
        "w_up": scatter_about(keys[5], (EXPERTS, FF, D), D ** -0.5, 0.09375, ((0, 16), (1, 8))),
        "w_down": scatter_about(keys[6], (EXPERTS, FF, D), FF ** -0.5, 0.15625, ((0, 16), (1, 8))),
    }


aux_weight = 1.0

def rank_rows(expert_ids):
    onehot = (expert_ids[:, None] == jnp.arange(EXPERTS, dtype=jnp.int32)[None, :]).astype(jnp.int32)
    earlier = jnp.cumsum(onehot, axis=0) - onehot
    return lax.optimization_barrier(jnp.sum(earlier * onehot, axis=1)).astype(jnp.int32)

def place_rows(values, target, total):
    return jnp.zeros((total,) + values.shape[1:], values.dtype).at[target].set(values, mode='drop')

def take_rows(values, target):
    return values[jnp.minimum(target, values.shape[0] - 1)]

def expert_backward(rows_in, grads_in, gates_in, gate_weight, up_weight, down_weight):
    scaled = (gates_in.astype(jnp.float32)[:, None] * grads_in.astype(jnp.float32)).astype(jnp.bfloat16)
    gate_pre = lax.dot_general(rows_in, gate_weight, (((1,), (1,)), ((), ())), preferred_element_type=jnp.float32)
    up_pre = lax.dot_general(rows_in, up_weight, (((1,), (1,)), ((), ())), preferred_element_type=jnp.float32)
    sigmoid_gate = jax.nn.sigmoid(gate_pre)
    active = gate_pre * sigmoid_gate
    hidden = (active * up_pre).astype(jnp.bfloat16)
    output_part = jnp.dot(hidden, down_weight, preferred_element_type=jnp.float32)
    gate_part = lax.optimization_barrier(jnp.sum(grads_in.astype(jnp.float32) * output_part, axis=1))
    grad_hidden = lax.dot_general(scaled, down_weight, (((1,), (1,)), ((), ())), preferred_element_type=jnp.float32)
    grad_upper = (grad_hidden * active).astype(jnp.bfloat16)
    grad_pre = (grad_hidden * up_pre * sigmoid_gate * (1.0 + gate_pre * (1.0 - sigmoid_gate))).astype(jnp.bfloat16)
    down_grad_t = lax.dot_general(scaled, hidden, (((0,), (0,)), ((), ())), preferred_element_type=jnp.float32)
    gate_grad_w = lax.dot_general(grad_pre, rows_in, (((0,), (0,)), ((), ())), preferred_element_type=jnp.float32)
    up_grad_w = lax.dot_general(grad_upper, rows_in, (((0,), (0,)), ((), ())), preferred_element_type=jnp.float32)
    input_part = jnp.dot(grad_pre, gate_weight, preferred_element_type=jnp.float32)
    input_part = input_part + jnp.dot(grad_upper, up_weight, preferred_element_type=jnp.float32)
    rounded = lax.optimization_barrier(input_part.astype(jnp.bfloat16)).astype(jnp.float32)
    return (rounded, gate_part, gate_grad_w, up_grad_w, down_grad_t)

def one_expert(operands):
    rows_in, grads_in, gates_in, gate_weight, up_weight, down_weight = operands
    hidden_shard = FF // N_DP
    input_acc = jnp.zeros((rows_in.shape[0], D), jnp.float32)
    gate_acc = jnp.zeros((rows_in.shape[0],), jnp.float32)
    gate_list, up_list, down_list = ([], [], [])
    for shard_index in range(N_DP):
        row_start = shard_index * hidden_shard
        row_end = row_start + hidden_shard
        result = expert_backward(rows_in, grads_in, gates_in, gate_weight[row_start:row_end, :], up_weight[row_start:row_end, :], down_weight[row_start:row_end, :])
        input_acc = input_acc + result[0]
        gate_acc = gate_acc + result[1]
        gate_list.append(result[2])
        up_list.append(result[3])
        down_list.append(result[4].T)
    return (input_acc.astype(jnp.bfloat16), gate_acc.astype(jnp.bfloat16), jnp.concatenate(gate_list, axis=0), jnp.concatenate(up_list, axis=0), jnp.concatenate(down_list, axis=0))

def reference(rows_x, rows_dy, router_logits, expert_of, w_gate, w_up, w_down):
    blocks = ROWS // R_DEV
    router_probs = jax.nn.softmax(router_logits, axis=1)
    expert_ids = expert_of[:, 0]
    expert_iota = jnp.arange(EXPERTS, dtype=jnp.int32)
    onehot_int = (expert_ids[:, None] == expert_iota[None, :]).astype(jnp.int32)
    onehot_all = onehot_int.astype(jnp.float32)
    counts = lax.optimization_barrier(jnp.sum(onehot_int, axis=0))
    gate_b = lax.optimization_barrier(jnp.sum(router_probs * onehot_all, axis=1)).astype(jnp.bfloat16)
    scores = counts * EXPERTS + (EXPERTS - 1 - expert_iota)
    hot_ids = lax.top_k(scores, HOT)[1].astype(jnp.int32)
    block_ids = expert_ids.reshape(blocks, R_DEV)
    ranking = jax.vmap(rank_rows)(block_ids)
    row_hot = jnp.any(block_ids[:, :, None] == hot_ids[None, None, :], axis=2)
    cold_total = EXPERTS * COLD_CAP
    cold_target = jnp.where(row_hot, cold_total, block_ids * COLD_CAP + ranking).astype(jnp.int32)
    block_rows = rows_x.reshape(blocks, R_DEV, D)
    block_grads = rows_dy.reshape(blocks, R_DEV, D)
    block_gates = gate_b.reshape(blocks, R_DEV)
    place_cold = jax.vmap(partial(place_rows, total=cold_total))
    cold_rows = place_cold(block_rows, cold_target).reshape(blocks, EXPERTS, COLD_CAP, D).transpose(1, 0, 2, 3).reshape(EXPERTS, blocks * COLD_CAP, D)
    cold_grads = place_cold(block_grads, cold_target).reshape(blocks, EXPERTS, COLD_CAP, D).transpose(1, 0, 2, 3).reshape(EXPERTS, blocks * COLD_CAP, D)
    cold_gates = place_cold(block_gates, cold_target).reshape(blocks, EXPERTS, COLD_CAP).transpose(1, 0, 2).reshape(EXPERTS, blocks * COLD_CAP)
    results = lax.map(one_expert, (cold_rows, cold_grads, cold_gates, w_gate, w_up, w_down))
    grad_gate, grad_up, grad_down = (results[2], results[3], results[4])
    back_cold = results[0].reshape(EXPERTS, blocks, COLD_CAP, D).transpose(1, 0, 2, 3).reshape(blocks, cold_total, D)
    back_cold_gates = results[1].reshape(EXPERTS, blocks, COLD_CAP).transpose(1, 0, 2).reshape(blocks, cold_total)
    grad_rows = jax.vmap(take_rows)(back_cold, cold_target)
    gate_rows = jax.vmap(take_rows)(back_cold_gates, cold_target)
    place_hot = jax.vmap(partial(place_rows, total=CAP))
    for hot_index in range(HOT):
        hot_id = hot_ids[hot_index]
        on_hot = block_ids == hot_id
        hot_target = jnp.where(on_hot, ranking, CAP).astype(jnp.int32)
        hot_rows = place_hot(block_rows, hot_target).reshape(blocks * CAP, D)
        hot_grads = place_hot(block_grads, hot_target).reshape(blocks * CAP, D)
        hot_gates = place_hot(block_gates, hot_target).reshape(blocks * CAP)
        hot_result = one_expert((hot_rows, hot_grads, hot_gates, w_gate[hot_id], w_up[hot_id], w_down[hot_id]))
        grad_gate = grad_gate.at[hot_id].add(hot_result[2])
        grad_up = grad_up.at[hot_id].add(hot_result[3])
        grad_down = grad_down.at[hot_id].add(hot_result[4])
        hot_back = hot_result[0].reshape(blocks, CAP, D)
        hot_back_gates = hot_result[1].reshape(blocks, CAP)
        grad_rows = jnp.where(on_hot[:, :, None], jax.vmap(take_rows)(hot_back, hot_target), grad_rows)
        gate_rows = jnp.where(on_hot, jax.vmap(take_rows)(hot_back_gates, hot_target), gate_rows)
    grad_rows = grad_rows.reshape(ROWS, D)
    gate_rows = gate_rows.reshape(ROWS).astype(jnp.float32)
    fractions = counts.astype(jnp.float32) / ROWS
    pulls = onehot_all * gate_rows[:, None] + aux_weight * EXPERTS * fractions[None, :]
    grad_logits = router_probs * (pulls - lax.optimization_barrier(jnp.sum(router_probs * pulls, axis=1, keepdims=True)))
    squares = jnp.sum(grad_gate * grad_gate) + jnp.sum(grad_up * grad_up) + jnp.sum(grad_down * grad_down)
    return (grad_rows, grad_logits, grad_gate, grad_up, grad_down, jnp.sqrt(squares))
```

```python
import jax
import jax.numpy as jnp
from jax import lax
from jax.experimental import pallas as pl
from jax.experimental.pallas import tpu as pltpu
from jax.sharding import PartitionSpec as P

f32 = jnp.float32
bf16 = jnp.bfloat16
MESH = pl.DeviceIdType.MESH
ANY = pl.BlockSpec(memory_space=pl.ANY)
VM = pl.BlockSpec(memory_space=pltpu.VMEM)
SM = pl.BlockSpec(memory_space=pltpu.SMEM)

E = 16
NDP = 8
SLOT = 32
W = 512
ROWS = E * SLOT
LOCAL = 2 * SLOT
SLOTS = ROWS + SLOT
GW = 1280


def place():
    e = lax.axis_index("expert")
    d = lax.axis_index("dp")
    return e, d, e // 4, (e // 2) % 2, e % 2, d // 2, d % 2


def expert_at(x, zh, c):
    return (x * 2 + zh) * 2 + c


def to(e, d):
    return {"expert": e, "dp": d}


def row_facts(ids, experts):
    rows = ids.shape[1]
    onehot = (lax.broadcasted_iota(jnp.int32, (experts, rows), 0) == ids).astype(f32)
    before = lax.broadcasted_iota(jnp.int32, (rows, rows), 0) < lax.broadcasted_iota(
        jnp.int32, (rows, rows), 1
    )
    earlier = jnp.dot(onehot.astype(bf16), before.astype(bf16), preferred_element_type=f32)
    rank = jnp.sum(onehot * earlier, axis=0, keepdims=True).astype(jnp.int32)
    return onehot, rank


def soft(logits):
    top = jnp.max(logits, axis=0, keepdims=True)
    ex = jnp.exp(logits - top)
    return ex / jnp.sum(ex, axis=0, keepdims=True)


def nt(a, b):
    return lax.dot_general(a, b, (((1,), (1,)), ((), ())), preferred_element_type=f32)


def tn(a, b):
    return lax.dot_general(a, b, (((0,), (0,)), ((), ())), preferred_element_type=f32)


def slots_kernel(ids_ref, logits_ref, x_ref, dy_ref, s_ref, m_ref, perm):
    @pl.when(pl.program_id(0) == 0)
    def _():
        ids = ids_ref[...]
        onehot, rank = row_facts(ids, E)
        rows = ids.shape[1]
        target = jnp.where(rank < SLOT, ids * SLOT + rank, ROWS + rank - SLOT)
        slot = lax.broadcasted_iota(jnp.int32, (SLOTS, rows), 0)
        perm[...] = (slot == target).astype(f32).astype(bf16)
        gate = jnp.sum(soft(logits_ref[...]) * onehot, axis=0, keepdims=True).astype(bf16)
        gate = gate.astype(f32)
        lane = lax.broadcasted_iota(jnp.int32, (128, rows), 0)
        first = (lane == rank).astype(f32).astype(bf16)
        extra = (lane == rank - SLOT).astype(f32).astype(bf16)
        by_expert = (lane == ids).astype(f32).astype(bf16)
        cold = (onehot * gate * (rank < SLOT).astype(f32)).astype(bf16)
        cold = nt(cold, first)
        gate8 = jnp.broadcast_to(gate, (8, rows)).astype(bf16)
        hot = nt(gate8, extra)
        count = nt(jnp.ones((8, rows), bf16), by_expert)
        line = lax.broadcasted_iota(jnp.int32, (8, 128), 0)
        for e in range(E):
            mine = jnp.broadcast_to(cold[e : e + 1, :], (8, 128))
            m_ref[e] = jnp.where(line == 0, mine, jnp.where(line == 1, hot, count))

    p = perm[...]
    s_ref[0, 0] = jnp.dot(p, x_ref[...], preferred_element_type=f32).astype(bf16)
    s_ref[1, 0] = jnp.dot(p, dy_ref[...], preferred_element_type=f32).astype(bf16)


def lay_out(ids, logits, x, dy):
    rows = x.shape[0]
    return pl.pallas_call(
        slots_kernel,
        grid=(NDP,),
        in_specs=[
            pl.BlockSpec((1, rows), lambda j: (0, 0)),
            pl.BlockSpec((E, rows), lambda j: (0, 0)),
            pl.BlockSpec((rows, W), lambda j: (0, j)),
            pl.BlockSpec((rows, W), lambda j: (0, j)),
        ],
        out_specs=[
            pl.BlockSpec((2, 1, SLOTS, W), lambda j: (0, j, 0, 0)),
            pl.BlockSpec((E, 8, 128), lambda j: (0, 0, 0)),
        ],
        out_shape=[
            jax.ShapeDtypeStruct((2, NDP, SLOTS, W), bf16),
            jax.ShapeDtypeStruct((E, 8, 128), f32),
        ],
        scratch_shapes=[pltpu.VMEM((SLOTS, rows), bf16)],
        name="lay_out",
    )(ids, logits, x, dy)


class Gather:
    names = (
        "0oz", "0or", "0ol", "0lr", "0lz", "0rl", "0rz", "0dz", "0ez",
        "1oz", "1or", "1ol", "1zr", "1zl", "1lr", "1kr", "1rl", "1ql",
    )

    def __init__(self, own, piece, j, z, right, left, pair, ssem, rsem):
        self.own, self.piece, self.ssem, self.rsem = own, piece, ssem, rsem
        self.j, self.z = j, z
        self.jl, self.jr, self.jd = (j + 3) % 4, (j + 1) % 4, (j + 2) % 4
        self.right, self.left, self.pair = right, left, pair
        self.sent = []

    def send(self, name, src, dst, dev):
        i = self.names.index(name)
        copy = pltpu.make_async_remote_copy(
            src, dst, self.ssem.at[i], self.rsem.at[i], device_id=dev, device_id_type=MESH
        )
        copy.start()
        self.sent.append(copy)

    def pass_on(self, name, dev, *where):
        ref = self.piece(*where)
        self.send(name, ref, ref, dev)

    def got(self, name, *where):
        i = self.names.index(name)
        ref = self.piece(*where)
        pltpu.make_async_remote_copy(
            ref, ref, self.ssem.at[i], self.rsem.at[i], device_id=self.pair, device_id_type=MESH
        ).wait_recv()

    def start(self, a):
        for way, dev in (("z", self.pair), ("r", self.right), ("l", self.left)):
            self.send(f"{a}o{way}", self.own(a), self.piece(a, self.j, self.z, None), dev)

    def s2(self):
        self.got("0or", 0, self.jl, self.z, None)
        self.pass_on("0lr", self.right, 0, self.jl, self.z, 0)
        self.pass_on("0lz", self.pair, 0, self.jl, self.z, None)

    def s3(self):
        self.got("0ol", 0, self.jr, self.z, None)
        self.pass_on("0rl", self.left, 0, self.jr, self.z, 1)
        self.pass_on("0rz", self.pair, 0, self.jr, self.z, None)

    def s4(self):
        self.got("1oz", 1, self.j, 1 - self.z, None)
        self.pass_on("1zr", self.right, 1, self.j, 1 - self.z, None)
        self.pass_on("1zl", self.left, 1, self.j, 1 - self.z, None)

    def s5(self):
        self.got("1or", 1, self.jl, self.z, None)
        self.pass_on("1lr", self.right, 1, self.jl, self.z, 0)

    def s6(self):
        self.got("1ol", 1, self.jr, self.z, None)
        self.pass_on("1rl", self.left, 1, self.jr, self.z, 1)

    def s7(self):
        self.got("0lr", 0, self.jd, self.z, 0)
        self.pass_on("0dz", self.pair, 0, self.jd, self.z, 0)

    def s8(self):
        self.got("0rl", 0, self.jd, self.z, 1)
        self.pass_on("0ez", self.pair, 0, self.jd, self.z, 1)

    def s9(self):
        self.got("1zr", 1, self.jl, 1 - self.z, None)
        self.pass_on("1kr", self.right, 1, self.jl, 1 - self.z, 0)

    def s10(self):
        self.got("1zl", 1, self.jr, 1 - self.z, None)
        self.pass_on("1ql", self.left, 1, self.jr, 1 - self.z, 1)

    def end_of_1_d(self):
        self.got("1lr", 1, self.jd, self.z, 0)
        self.got("1rl", 1, self.jd, self.z, 1)

    def end_of_1_e(self):
        self.got("1kr", 1, self.jd, 1 - self.z, 0)
        self.got("1ql", 1, self.jd, 1 - self.z, 1)

    def end_of_0_d(self):
        self.got("0dz", 0, self.jd, 1 - self.z, 0)
        self.got("0ez", 0, self.jd, 1 - self.z, 1)

    def drain(self):
        for copy in self.sent:
            copy.wait_send()


def meet(partners):
    barrier = pltpu.get_barrier_semaphore()
    for dev in partners:
        pl.semaphore_signal(barrier, inc=1, device_id=dev, device_id_type=MESH)
    pl.semaphore_wait(barrier, len(partners))


def others(x, zh):
    for k in range(1, 8):
        dx, dz = k // 2, k % 2
        yield k, ((4 - dx) % 4) * 2 + dz, (x + dx) % 4, (zh + dz) % 2


def dispatch_kernel(
    s, ms, cold, extra, mr, bounce, mbounce,
    st_s, st_r, m_s, m_r, sib_s, sib_r, dp_s, dp_r, ex_s, ex_r, xs_s, xs_r, loc,
):
    e, d, x, zh, c, y, zl = place()
    dbar = y * 2 + 1 - zl
    sib = to(expert_at(x, zh, 1 - c), d)
    d_r, d_l = ((y + 1) % 4) * 2 + zl, ((y + 3) % 4) * 2 + zl
    peers = [
        (rel, back, expert_at(x2, zh2, c2), d if rel % 2 == 0 else dbar)
        for rel, back, x2, zh2 in others(x, zh)
        for c2 in (0, 1)
    ]
    x_r = to(expert_at((x + 1) % 4, zh, c), d)
    x_l = to(expert_at((x + 3) % 4, zh, c), d)
    z_p = to(expert_at(x, 1 - zh, c), dbar)
    meet([to(e2, d2) for _, _, e2, d2 in peers] + [sib, to(e, d_r), to(e, d_l), to(e, dbar)])

    sent, msent = [], []
    for a in (0, 1):
        for rel, back, e2, d2 in peers:
            copy = pltpu.make_async_remote_copy(
                s.at[a, d2, pl.ds(pl.multiple_of(e2 * SLOT, SLOT), SLOT), :],
                cold.at[a, d2, pl.ds(pl.multiple_of((back * 2 + c) * SLOT, SLOT), SLOT), :],
                st_s.at[a], st_r.at[a], device_id=to(e2, d2), device_id_type=MESH,
            )
            copy.start()
        if a == 0:
            own_in = [
                pltpu.make_async_copy(
                    s.at[:, :, pl.ds(pl.multiple_of(e * SLOT, SLOT), SLOT), :], bounce.at[0], loc.at[0]
                ),
                pltpu.make_async_copy(s.at[:, :, pl.ds(ROWS, SLOT), :], bounce.at[1], loc.at[1]),
                pltpu.make_async_copy(ms.at[e], mbounce, loc.at[2]),
            ]
            for copy in own_in:
                copy.start()
    for n, (rel, back, e2, d2) in enumerate(peers + [(0, 0, expert_at(x, zh, 1 - c), d)]):
        copy = pltpu.make_async_remote_copy(
            ms.at[e2], mr.at[back * 2 + c], m_s.at[n], m_r.at[back * 2 + c],
            device_id=to(e2, d2), device_id_type=MESH,
        )
        copy.start()
        msent.append(copy)
    sib_copy = pltpu.make_async_remote_copy(
        s.at[:, :, pl.ds(pl.multiple_of((e + 1 - 2 * c) * SLOT, SLOT), SLOT), :],
        cold.at[:, :, pl.ds(pl.multiple_of(c * SLOT, SLOT), SLOT), :],
        sib_s, sib_r, device_id=sib, device_id_type=MESH,
    )
    sib_copy.start()
    sent.append(sib_copy)
    for copy in own_in:
        copy.wait()
    own_out = [
        pltpu.make_async_copy(
            bounce.at[0], cold.at[:, :, pl.ds(pl.multiple_of(c * SLOT, SLOT), SLOT), :], loc.at[3]
        ),
        pltpu.make_async_copy(
            bounce.at[1], extra.at[:, :, pl.ds(pl.multiple_of(e * SLOT, SLOT), SLOT), :], loc.at[4]
        ),
        pltpu.make_async_copy(mbounce, mr.at[c], loc.at[5]),
    ]
    for copy in own_out:
        copy.start()

    half = (ROWS - LOCAL) // 2

    def dp_piece(a, j, z, h):
        rows = {None: (LOCAL, 2 * half), 0: (LOCAL, half), 1: (LOCAL + half, half)}[h]
        return cold.at[a, j * 2 + z, pl.ds(*rows), :]

    def ex_piece_of(core):
        def piece(a, j, z, h):
            chunks = {None: (0, NDP), 0: (0, NDP // 2), 1: (NDP // 2, NDP // 2)}[h]
            at = pl.multiple_of(expert_at(j, z, core) * SLOT, SLOT)
            return extra.at[a, pl.ds(*chunks), pl.ds(at, SLOT), :]
        return piece

    ex_piece, ex_other = ex_piece_of(c), ex_piece_of(1 - c)

    dp = Gather(
        lambda a: dp_piece(a, y, zl, None), dp_piece, y, zl,
        to(e, d_r), to(e, d_l), to(e, dbar), dp_s, dp_r,
    )
    ex = Gather(
        lambda a: s.at[a, :, pl.ds(ROWS, SLOT), :], ex_piece, x, zh, x_r, x_l, z_p, ex_s, ex_r,
    )
    shares = []

    def share(a, j, z, src=None):
        i = len(shares)
        dst = ex_piece(a, j, z, None)
        copy = pltpu.make_async_remote_copy(
            dst if src is None else src, dst, xs_s.at[i], xs_r.at[i],
            device_id=sib, device_id_type=MESH,
        )
        copy.start()
        shares.append((copy, (a, j, z)))

    def whole(a):
        ref = cold.at[a, d, pl.ds(LOCAL, ROWS - LOCAL), :]
        return pltpu.make_async_remote_copy(
            ref, ref, st_s.at[a], st_r.at[a], device_id=sib, device_id_type=MESH
        )

    whole(0).wait_recv()
    dp.start(0)
    ex.start(0)
    whole(1).wait_recv()
    dp.start(1)
    ex.start(1)
    share(0, x, zh, s.at[0, :, pl.ds(ROWS, SLOT), :])
    share(1, x, zh, s.at[1, :, pl.ds(ROWS, SLOT), :])
    ex.s2()
    ex.s3()
    dp.s2()
    dp.s3()
    ex.s4()
    ex.s5()
    ex.s6()
    for a, j, z in ((0, ex.jl, zh), (0, ex.jr, zh), (1, x, 1 - zh), (1, ex.jl, zh), (1, ex.jr, zh)):
        share(a, j, z)
    ex.s7()
    ex.s8()
    share(0, ex.jd, zh)
    dp.s4()
    dp.s5()
    dp.s6()
    ex.s9()
    ex.s10()
    share(1, ex.jl, 1 - zh)
    share(1, ex.jr, 1 - zh)
    dp.s7()
    dp.s8()
    dp.s9()
    dp.s10()
    ex.got("0oz", 0, x, 1 - zh, None)
    share(0, x, 1 - zh)
    ex.got("0lz", 0, ex.jl, 1 - zh, None)
    share(0, ex.jl, 1 - zh)
    ex.got("0rz", 0, ex.jr, 1 - zh, None)
    share(0, ex.jr, 1 - zh)
    ex.end_of_1_d()
    share(1, ex.jd, zh)
    ex.end_of_1_e()
    share(1, ex.jd, 1 - zh)
    ex.end_of_0_d()
    share(0, ex.jd, 1 - zh)
    for i, (copy, where) in enumerate(shares):
        ref = ex_other(*where, None)
        pltpu.make_async_remote_copy(
            ref, ref, xs_s.at[i], xs_r.at[i], device_id=sib, device_id_type=MESH
        ).wait_recv()
    dp.end_of_1_d()
    dp.end_of_1_e()
    dp.got("0oz", 0, y, 1 - zl, None)
    dp.got("0lz", 0, dp.jl, 1 - zl, None)
    dp.got("0rz", 0, dp.jr, 1 - zl, None)
    dp.end_of_0_d()
    for i in [1 - c] + list(range(2, E)):
        pltpu.make_async_remote_copy(
            ms.at[0], mr.at[i], m_s.at[0], m_r.at[i], device_id=sib, device_id_type=MESH
        ).wait_recv()
    for copy in sent:
        copy.wait()
    for copy in msent:
        copy.wait_send()
    whole(0).wait_send()
    whole(1).wait_send()
    for copy in own_out:
        copy.wait()
    for copy, _ in shares:
        copy.wait_send()
    dp.drain()
    ex.drain()


def dispatch(s, m):
    D = pltpu.SemaphoreType.DMA
    return pl.pallas_call(
        dispatch_kernel,
        in_specs=[ANY, ANY],
        out_specs=[ANY, ANY, ANY],
        out_shape=[
            jax.ShapeDtypeStruct((2, NDP, ROWS, W), bf16),
            jax.ShapeDtypeStruct((2, NDP, ROWS, W), bf16),
            jax.ShapeDtypeStruct((E, 8, 128), f32),
        ],
        scratch_shapes=[
            pltpu.VMEM((2, 2, NDP, SLOT, W), bf16),
            pltpu.VMEM((8, 128), f32),
            D((2,)), D((2,)), D((15,)), D((16,)), D, D,
            D((18,)), D((18,)), D((18,)), D((18,)), D((16,)), D((16,)), D((6,)),
        ],
        compiler_params=pltpu.CompilerParams(collective_id=1, has_side_effects=True),
        name="dispatch",
    )(s, m)


def sigmoid(v):
    return 1.0 / (1.0 + jnp.exp(-v))


def experts_kernel(
    hot_ref, gates_ref, cold, extra_hbm, wg, wu, wd,
    dxc, dxh, gp, gg, gu, gd,
    extra, acc, lhs, rhs, stage, sem, osem,
):
    hot = hot_ref[0] > 0
    FFL = wg.shape[0]

    @pl.when(hot)
    def _():
        pltpu.make_async_copy(extra_hbm, extra, sem).start()

    def cols(j):
        return pl.ds(pl.multiple_of(j * W, W), W)

    def forward(rows_ref, t):
        acc[...] = jnp.zeros_like(acc)

        def step(j, _):
            xj, dj = rows_ref[0, j], rows_ref[1, j]
            acc[0] += nt(wg[:, cols(j)], xj)
            acc[1] += nt(wu[:, cols(j)], xj)
            acc[2] += nt(wd[:, cols(j)], dj)
            return 0

        lax.fori_loop(0, NDP, step, 0)
        gate = gates_ref[t : t + 1, :]
        pre, up, g = acc[0], acc[1], acc[2]
        s = sigmoid(pre)
        active = pre * s
        hidden = (active * up).astype(bf16).astype(f32)
        gp[0:1, t * ROWS : (t + 1) * ROWS] = jnp.sum(hidden * g, axis=0, keepdims=True)
        gh = g * gate
        d_up = gh * active
        d_pre = gh * up * s * (1.0 + pre * (1.0 - s))
        lhs[t, 0] = d_pre.astype(bf16)
        lhs[t, 1] = d_up.astype(bf16)
        lhs[t, 2] = (hidden * gate).astype(bf16)
        rhs[t, :, 0:FFL] = d_pre.T.astype(bf16)
        rhs[t, :, FFL : 2 * FFL] = d_up.T.astype(bf16)

    forward(cold, 0)

    @pl.when(hot)
    def _():
        pltpu.make_async_copy(extra_hbm, extra, sem).wait()
        forward(extra, 1)

    @pl.when(jnp.logical_not(hot))
    def _():
        gp[0:1, ROWS : 2 * ROWS] = jnp.zeros((1, ROWS), f32)

    outs = (gg, gu, gd)

    def put(j, slot, i):
        return pltpu.make_async_copy(
            stage.at[slot, i], outs[i].at[:, cols(j)], osem.at[slot, i]
        )

    def step(j, sq):
        slot = j % 2

        @pl.when(j >= 2)
        def _():
            for i in range(3):
                put(j - 2, slot, i).wait()

        w2 = (wg[:, cols(j)], wu[:, cols(j)])

        def back(t, out):
            r = jnp.dot(rhs[t, :, 0:FFL], w2[0], preferred_element_type=f32)
            r += jnp.dot(rhs[t, :, FFL : 2 * FFL], w2[1], preferred_element_type=f32)
            out[j] = r.astype(bf16)

        back(0, dxc)
        for i in range(3):
            stage[slot, i] = jnp.dot(lhs[0, i], cold[i // 2, j], preferred_element_type=f32)

        @pl.when(hot)
        def _():
            back(1, dxh)
            for i in range(3):
                stage[slot, i] += jnp.dot(lhs[1, i], extra[i // 2, j], preferred_element_type=f32)

        @pl.when(jnp.logical_not(hot))
        def _():
            dxh[j] = jnp.zeros((ROWS, W), bf16)

        for i in range(3):
            v = stage[slot, i]
            sq = sq + jnp.sum((v * v).reshape(-1, 8, W), axis=0)
            put(j, slot, i).start()
        return sq

    sq = lax.fori_loop(0, NDP, step, jnp.zeros((8, W), f32))
    total = jnp.sum(jnp.sum(sq, axis=0, keepdims=True), axis=1, keepdims=True)
    gp[0:1, 2 * ROWS :] = jnp.broadcast_to(total, (1, GW - 2 * ROWS))
    for j in (NDP - 2, NDP - 1):
        for i in range(3):
            put(j, j % 2, i).wait()


def experts(hot, gates, cold, extra, wg, wu, wd):
    FFL, D = wg.shape
    return pl.pallas_call(
        experts_kernel,
        in_specs=[SM, VM, VM, ANY, VM, VM, VM],
        out_specs=[VM, VM, VM, ANY, ANY, ANY],
        out_shape=[
            jax.ShapeDtypeStruct((NDP, ROWS, W), bf16),
            jax.ShapeDtypeStruct((NDP, ROWS, W), bf16),
            jax.ShapeDtypeStruct((1, GW), f32),
        ]
        + [jax.ShapeDtypeStruct((FFL, D), f32)] * 3,
        scratch_shapes=[
            pltpu.VMEM((2, NDP, ROWS, W), bf16),
            pltpu.VMEM((3, FFL, ROWS), f32),
            pltpu.VMEM((2, 3, FFL, ROWS), bf16),
            pltpu.VMEM((2, ROWS, 2 * FFL), bf16),
            pltpu.VMEM((2, 3, FFL, W), f32),
            pltpu.SemaphoreType.DMA,
            pltpu.SemaphoreType.DMA((2, 3)),
        ],
        compiler_params=pltpu.CompilerParams(vmem_limit_bytes=60 * 1024 * 1024),
        name="experts",
    )(hot, gates, cold, extra, wg, wu, wd)


def add_rows(out, terms, rows):
    def step(i, _):
        r = pl.ds(pl.multiple_of(i * 32, 32), 32)
        total = terms[0][r, :].astype(f32)
        for term in terms[1:]:
            total = total + term[r, :].astype(f32)
        out[r, :] = total.astype(out.dtype)
        return 0

    lax.fori_loop(0, rows // 32, step, 0)


C_NAMES = (
    "c_rr", "c_rl", "c_dr", "c_dl", "c_sr", "c_sl", "c_z",
    "h_z2", "h_zr", "h_zl", "h_z0", "h_rr", "h_rl", "h_dr", "h_dl", "h_sr", "h_sl",
)


def combine_kernel(
    dxc, dxh, gp, back, gback,
    cr_l, cr_r, cs_r, cs_l, cf_l, cf_r, cz_s, cz_r, own,
    hz, hw, hr_l, hr_r, hf_l, hf_r, rc, rh, gall, gsum,
    ssem, rsem, g_s, g_r, b_s, b_r, gb_s, gb_r,
):
    e, d, x, zh, c, y, zl = place()
    zo = 1 - zl
    yr, yl, y2 = (y + 1) % 4, (y + 3) % 4, (y + 2) % 4
    right, left, pair = to(e, yr * 2 + zl), to(e, yl * 2 + zl), to(e, y * 2 + zo)
    peers, places, mine = [(0, expert_at(x, zh, 1 - c))], [1 - c], [c]
    for rel, seen, x2, zh2 in others(x, zh):
        for c2 in (0, 1):
            peers.append((rel, expert_at(x2, zh2, c2)))
            places.append(rel * 2 + c2)
            mine.append(seen * 2 + c)
    dps = [(d + k) % NDP for k in range(1, NDP)]
    meet([to(e2, d) for _, e2 in peers] + [to(e, d2) for d2 in dps])

    sent = []

    def send(name, src, dst, dev):
        i = C_NAMES.index(name)
        copy = pltpu.make_async_remote_copy(
            src, dst, ssem.at[i], rsem.at[i], device_id=dev, device_id_type=MESH
        )
        copy.start()
        sent.append(copy)

    def got(name, ref):
        i = C_NAMES.index(name)
        pltpu.make_async_remote_copy(
            ref, ref, ssem.at[i], rsem.at[i], device_id=pair, device_id_type=MESH
        ).wait_recv()

    H = ROWS // 2
    top, low = pl.ds(0, H), pl.ds(H, H)

    def both(j):
        return pl.ds(j * 2, 2)

    send("c_rr", dxc.at[both(y2), top], cr_l, right)
    send("c_rl", dxc.at[both(y2), low], cr_r, left)
    send("h_z2", dxh.at[y2 * 2 + zo], hz.at[y2], pair)
    send("h_zr", dxh.at[yr * 2 + zo], hz.at[yr], pair)
    send("h_zl", dxh.at[yl * 2 + zo], hz.at[yl], pair)
    send("h_z0", dxh.at[y * 2 + zo], hz.at[y], pair)
    gsends = []
    for k, d2 in enumerate(dps):
        copy = pltpu.make_async_remote_copy(
            gp, gall.at[d], g_s.at[k], g_r.at[k], device_id=to(e, d2), device_id_type=MESH
        )
        copy.start()
        gsends.append(copy)
    gall[d] = gp[...]
    send("c_dr", dxc.at[both(yr), low], cf_l.at[:, low], right)
    send("c_dl", dxc.at[both(yl), top], cf_r.at[:, top], left)

    for k in range(NDP - 1):
        src = (d + NDP - 1 - k) % NDP
        pltpu.make_async_remote_copy(
            gall.at[src], gall.at[src], g_s.at[k], g_r.at[k], device_id=pair, device_id_type=MESH
        ).wait_recv()
    total = gall[0]
    for k in range(1, NDP):
        total = total + gall[k]
    gsum[...] = total
    gback[e] = total
    for n, (_, e2) in enumerate(peers):
        copy = pltpu.make_async_remote_copy(
            gsum, gback.at[e], gb_s.at[n], gb_r.at[mine[n]], device_id=to(e2, d), device_id_type=MESH
        )
        copy.start()
        gsends.append(copy)

    got("c_rr", cr_l)
    for i in (0, 1):
        add_rows(cs_r.at[i], (dxc.at[yr * 2 + i, top], cr_l.at[i]), H)
    send("c_sr", cs_r, cf_l.at[:, top], right)
    got("c_rl", cr_r)
    for i in (0, 1):
        add_rows(cs_l.at[i], (dxc.at[yl * 2 + i, low], cr_r.at[i]), H)
    send("c_sl", cs_l, cf_r.at[:, low], left)

    got("h_z2", hz.at[y2])
    add_rows(hw.at[y2], (dxh.at[y2 * 2 + zl], hz.at[y2]), ROWS)
    send("h_rr", hw.at[y2, top], hr_l, right)
    send("h_rl", hw.at[y2, low], hr_r, left)
    got("h_zr", hz.at[yr])
    add_rows(hw.at[yr, low], (dxh.at[yr * 2 + zl, low], hz.at[yr, low]), H)
    send("h_dr", hw.at[yr, low], hf_l.at[low], right)
    got("h_zl", hz.at[yl])
    add_rows(hw.at[yl, top], (dxh.at[yl * 2 + zl, top], hz.at[yl, top]), H)
    send("h_dl", hw.at[yl, top], hf_r.at[top], left)
    got("h_rr", hr_l)
    add_rows(hw.at[yr, top], (dxh.at[yr * 2 + zl, top], hz.at[yr, top], hr_l), H)
    send("h_sr", hw.at[yr, top], hf_l.at[top], right)
    got("h_rl", hr_r)
    add_rows(hw.at[yl, low], (dxh.at[yl * 2 + zl, low], hz.at[yl, low], hr_r), H)
    send("h_sl", hw.at[yl, low], hf_r.at[low], left)

    got("c_dr", cf_l.at[:, low])
    got("c_dl", cf_r.at[:, top])
    got("c_sr", cf_l.at[:, top])
    got("c_sl", cf_r.at[:, low])
    add_rows(cz_s, (dxc.at[y * 2 + zo], cf_l.at[zo], cf_r.at[zo]), ROWS)
    send("c_z", cz_s, cz_r, pair)
    add_rows(own, (dxc.at[y * 2 + zl], cf_l.at[zl], cf_r.at[zl]), ROWS)

    def give(refs, half):
        for n, (_, e2) in enumerate(peers):
            at = places[n] if half == 0 else e2
            copy = pltpu.make_async_remote_copy(
                refs.at[pl.ds(pl.multiple_of(at * SLOT, SLOT), SLOT), :],
                back.at[e, pl.ds(half * SLOT, SLOT), :],
                b_s.at[half * 15 + n], b_r.at[half * E + mine[n]],
                device_id=to(e2, d), device_id_type=MESH,
            )
            copy.start()
            gsends.append(copy)
        at = c if half == 0 else e
        back[e, half * SLOT : (half + 1) * SLOT, :] = refs[
            pl.ds(pl.multiple_of(at * SLOT, SLOT), SLOT), :
        ]

    got("h_z0", hz.at[y])
    got("h_dr", hf_l.at[low])
    got("h_dl", hf_r.at[top])
    got("h_sr", hf_l.at[top])
    got("h_sl", hf_r.at[low])
    add_rows(rh, (dxh.at[y * 2 + zl], hz.at[y], hf_l, hf_r), ROWS)
    give(rh, 1)
    got("c_z", cz_r)
    add_rows(rc, (own, cz_r), ROWS)
    give(rc, 0)

    for i in [1 - c] + list(range(2, E)):
        for half in (0, 1):
            ref = back.at[0, pl.ds(half * SLOT, SLOT), :]
            pltpu.make_async_remote_copy(
                ref, ref, b_s.at[0], b_r.at[half * E + i], device_id=pair, device_id_type=MESH
            ).wait_recv()
        pltpu.make_async_remote_copy(
            gsum, gback.at[0], gb_s.at[0], gb_r.at[i], device_id=pair, device_id_type=MESH
        ).wait_recv()
    for copy in gsends + sent:
        copy.wait_send()


def combine(dxc, dxh, gp):
    D = pltpu.SemaphoreType.DMA
    H = ROWS // 2
    return pl.pallas_call(
        combine_kernel,
        in_specs=[VM, VM, VM],
        out_specs=[VM, VM],
        out_shape=[
            jax.ShapeDtypeStruct((E, 2 * SLOT, W), bf16),
            jax.ShapeDtypeStruct((E, 1, GW), f32),
        ],
        scratch_shapes=[
            pltpu.VMEM((2, H, W), bf16), pltpu.VMEM((2, H, W), bf16),
            pltpu.VMEM((2, H, W), bf16), pltpu.VMEM((2, H, W), bf16),
            pltpu.VMEM((2, ROWS, W), bf16), pltpu.VMEM((2, ROWS, W), bf16),
            pltpu.VMEM((ROWS, W), bf16), pltpu.VMEM((ROWS, W), bf16),
            pltpu.VMEM((ROWS, W), f32),
            pltpu.VMEM((4, ROWS, W), bf16), pltpu.VMEM((4, ROWS, W), bf16),
            pltpu.VMEM((H, W), bf16), pltpu.VMEM((H, W), bf16),
            pltpu.VMEM((ROWS, W), bf16), pltpu.VMEM((ROWS, W), bf16),
            pltpu.VMEM((ROWS, W), bf16), pltpu.VMEM((ROWS, W), bf16),
            pltpu.VMEM((NDP, 1, GW), f32), pltpu.VMEM((1, GW), f32),
            D((17,)), D((17,)), D((7,)), D((7,)), D((30,)), D((32,)), D((15,)), D((16,)),
        ],
        compiler_params=pltpu.CompilerParams(
            collective_id=2, has_side_effects=True, vmem_limit_bytes=60 * 1024 * 1024
        ),
        name="combine",
    )(dxc, dxh, gp)


def finish_kernel(ids_ref, logits_ref, back, gback, mr, rows_ref, gl_ref, norm_ref):
    e, _, x, zh, c, _, _ = place()
    ids = ids_ref[...]
    onehot, rank = row_facts(ids, E)
    probs = soft(logits_ref[...])
    n = ids.shape[1]
    slot = lax.broadcasted_iota(jnp.int32, (E * 2 * SLOT, n), 0)
    pick = (slot == ids * (2 * SLOT) + rank).astype(f32).astype(bf16)
    flat = back[...].reshape(E * 2 * SLOT, W)
    rows_ref[...] = tn(pick, flat).astype(bf16)
    rel = (((x - (ids >> 2)) & 3) * 2 + (zh ^ ((ids >> 1) & 1))) * 2 + c
    lane = jnp.where(rank < SLOT, rel * SLOT + rank, ROWS + e * SLOT + rank - SLOT)
    here = (slot == lane).astype(f32).astype(bf16)
    found = jnp.dot(gback[:, 0, 0 : 2 * ROWS].astype(bf16), here, preferred_element_type=f32)
    dgate = jnp.sum(onehot * found, axis=0, keepdims=True)
    count = jnp.sum(mr[...], axis=0)[2:3, :]
    across = lax.broadcasted_iota(jnp.int32, (E, 128), 0)
    diag = across == lax.broadcasted_iota(jnp.int32, (E, 128), 1)
    column = jnp.sum(jnp.where(diag, jnp.broadcast_to(count, (E, 128)), 0.0), axis=1, keepdims=True)
    pulls = onehot * dgate + 1.0 * E * (column / (E * n))
    gl_ref[...] = probs * (pulls - jnp.sum(probs * pulls, axis=0, keepdims=True))
    norm_ref[...] = jnp.sqrt(jnp.sum(gback[:, 0, 2 * ROWS : 2 * ROWS + 128], axis=0, keepdims=True))


def finish(ids, logits, back, gback, mr):
    n = ids.shape[1]
    return pl.pallas_call(
        finish_kernel,
        in_specs=[VM] * 5,
        out_specs=[VM] * 3,
        out_shape=[
            jax.ShapeDtypeStruct((n, W), bf16),
            jax.ShapeDtypeStruct((E, n), f32),
            jax.ShapeDtypeStruct((1, 128), f32),
        ],
        name="finish",
    )(ids, logits, back, gback, mr)


def local(rows_x, rows_dy, router_logits, expert_of, w_gate, w_up, w_down):
    e, _, x, zh, _, _, _ = place()
    ids = expert_of.reshape(1, -1)
    logits = router_logits.T
    s, m = lay_out(ids, logits, rows_x, rows_dy)
    cold, extra, mr = dispatch(s, m)
    b = jnp.arange(E, dtype=jnp.int32)
    rel = (((b >> 2) - x) & 3) * 4 + (((b >> 1) & 1) ^ zh) * 2 + (b & 1)
    order = (rel[:, None] == jnp.arange(E, dtype=jnp.int32)[None, :]).astype(f32)
    gates = jnp.stack(
        [mr[:, 0, :SLOT].reshape(ROWS), jnp.dot(order, mr[:, 1, :SLOT]).reshape(ROWS)]
    )
    hot = (m[e, 2, e] > SLOT).astype(jnp.int32).reshape(1)
    dxc, dxh, gp, gg, gu, gd = experts(hot, gates, cold, extra, w_gate[0], w_up[0], w_down[0])
    back, gback = combine(dxc, dxh, gp)
    grad_rows, grad_logits, norm = finish(ids, logits, back, gback, mr)
    return grad_rows, grad_logits.T, gg[None], gu[None], gd[None], norm[0, 0]


def solution(mesh):
    rows = P("expert", None)
    weights = P("expert", "dp", None)
    return jax.shard_map(
        local,
        mesh=mesh,
        in_specs=(rows, rows, rows, rows, weights, weights, weights),
        out_specs=(P("expert", "dp"), rows, weights, weights, weights, P()),
        check_vma=False,
    )
```

```python
import jax
import jax.numpy as jnp
from jax import lax
from jax.experimental import pallas as pl
from jax.experimental.pallas import tpu as pltpu
from jax.sharding import PartitionSpec as P

f32 = jnp.float32
bf16 = jnp.bfloat16
MESH = pl.DeviceIdType.MESH
ANY = pl.BlockSpec(memory_space=pl.ANY)
VM = pl.BlockSpec(memory_space=pltpu.VMEM)
SM = pl.BlockSpec(memory_space=pltpu.SMEM)

E = 16
NDP = 8
SLOT = 32
W = 512
ROWS = E * SLOT
LOCAL = 2 * SLOT
GW = 1280


def place():
    e = lax.axis_index("expert")
    d = lax.axis_index("dp")
    return e, d, e // 4, (e // 2) % 2, e % 2, d // 2, d % 2


def expert_at(x, zh, c):
    return (x * 2 + zh) * 2 + c


def to(e, d):
    return {"expert": e, "dp": d}


def row_facts(ids, experts):
    rows = ids.shape[1]
    onehot = (lax.broadcasted_iota(jnp.int32, (experts, rows), 0) == ids).astype(f32)
    before = lax.broadcasted_iota(jnp.int32, (rows, rows), 0) < lax.broadcasted_iota(
        jnp.int32, (rows, rows), 1
    )
    earlier = jnp.dot(onehot.astype(bf16), before.astype(bf16), preferred_element_type=f32)
    rank = jnp.sum(onehot * earlier, axis=0, keepdims=True).astype(jnp.int32)
    return onehot, rank


def soft(logits):
    top = jnp.max(logits, axis=0, keepdims=True)
    ex = jnp.exp(logits - top)
    return ex / jnp.sum(ex, axis=0, keepdims=True)


def nt(a, b):
    return lax.dot_general(a, b, (((1,), (1,)), ((), ())), preferred_element_type=f32)


def tn(a, b):
    return lax.dot_general(a, b, (((0,), (0,)), ((), ())), preferred_element_type=f32)


def seen_from(ids, x, zh, c):
    return (((x - (ids >> 2)) & 3) * 2 + (zh ^ ((ids >> 1) & 1))) * 2 + c


def slots_kernel(ids_ref, logits_ref, x_ref, dy_ref, s1_ref, s2_ref, m_ref):
    e, d, x, zh, c, y, zl = place()
    ids = ids_ref[...]
    onehot, rank = row_facts(ids, E)
    rows = ids.shape[1]
    none = -1

    def perm(slots, target):
        slot = lax.broadcasted_iota(jnp.int32, (slots, rows), 0)
        return (slot == target).astype(f32).astype(bf16)

    far = (zh ^ ((ids >> 1) & 1)) == 1
    first = rank < SLOT
    chip = ((ids >> 2) * 2 + (ids & 1)) * SLOT + rank
    for g, ours in ((0, jnp.logical_not(far)), (1, far)):
        p = perm(ROWS // 2, jnp.where(first & ours, chip, none))
        at = pl.ds(pl.multiple_of((d if g == 0 else y * 2 + 1 - zl) * W, W), W)
        s1_ref[0, g] = jnp.dot(p, x_ref[:, at], preferred_element_type=f32).astype(bf16)
        s1_ref[1, g] = jnp.dot(p, dy_ref[:, at], preferred_element_type=f32).astype(bf16)
    home = jnp.where(ids == e, rank, jnp.where(ids == e + 1 - 2 * c, SLOT + rank, none))
    p = perm(3 * SLOT, jnp.where(first, home, SLOT + rank))
    for j in range(NDP):
        at = slice(j * W, (j + 1) * W)
        s2_ref[0, j] = jnp.dot(p, x_ref[:, at], preferred_element_type=f32).astype(bf16)
        s2_ref[1, j] = jnp.dot(p, dy_ref[:, at], preferred_element_type=f32).astype(bf16)

    gate = jnp.sum(soft(logits_ref[...]) * onehot, axis=0, keepdims=True).astype(bf16).astype(f32)
    lane = lax.broadcasted_iota(jnp.int32, (128, rows), 0)
    spot = (seen_from(ids, x, zh, c) & 3) * SLOT + rank
    cold = (onehot * gate * first.astype(f32)).astype(bf16)
    cold = nt(cold, (lane == spot).astype(f32).astype(bf16))
    gate8 = jnp.broadcast_to(gate, (8, rows)).astype(bf16)
    spot = jnp.where(first, none, (e & 3) * SLOT + rank - SLOT)
    hot = nt(gate8, (lane == spot).astype(f32).astype(bf16))
    count = nt(jnp.ones((8, rows), bf16), (lane == ids).astype(f32).astype(bf16))
    line = lax.broadcasted_iota(jnp.int32, (8, 128), 0)
    for k in range(E):
        mine = jnp.broadcast_to(cold[k : k + 1, :], (8, 128))
        busy = (jnp.sum(onehot[k : k + 1, :], axis=1, keepdims=True) > SLOT).astype(f32)
        rest = jnp.where(line == 2, count, jnp.broadcast_to(busy, (8, 128)))
        m_ref[k] = jnp.where(line == 0, mine, jnp.where(line == 1, hot, rest))


def lay_out(ids, logits, x, dy):
    return pl.pallas_call(
        slots_kernel,
        in_specs=[VM] * 4,
        out_specs=[VM] * 3,
        out_shape=[
            jax.ShapeDtypeStruct((2, 2, ROWS // 2, W), bf16),
            jax.ShapeDtypeStruct((2, NDP, 3 * SLOT, W), bf16),
            jax.ShapeDtypeStruct((E, 8, 128), f32),
        ],
        name="lay_out",
    )(ids, logits, x, dy)


class Gather:
    names = (
        "0oz", "0or", "0ol", "0lr", "0lz", "0rl", "0rz", "0dz", "0ez",
        "1oz", "1or", "1ol", "1zr", "1zl", "1lr", "1kr", "1rl", "1ql",
    )

    def __init__(self, own, piece, j, z, right, left, pair, ssem, rsem):
        self.own, self.piece, self.ssem, self.rsem = own, piece, ssem, rsem
        self.j, self.z = j, z
        self.jl, self.jr, self.jd = (j + 3) % 4, (j + 1) % 4, (j + 2) % 4
        self.right, self.left, self.pair = right, left, pair
        self.sent = []

    def send(self, name, src, dst, dev):
        i = self.names.index(name)
        copy = pltpu.make_async_remote_copy(
            src, dst, self.ssem.at[i], self.rsem.at[i], device_id=dev, device_id_type=MESH
        )
        copy.start()
        self.sent.append(copy)

    def pass_on(self, name, dev, *where):
        ref = self.piece(*where)
        self.send(name, ref, ref, dev)

    def got(self, name, *where):
        i = self.names.index(name)
        ref = self.piece(*where)
        pltpu.make_async_remote_copy(
            ref, ref, self.ssem.at[i], self.rsem.at[i], device_id=self.pair, device_id_type=MESH
        ).wait_recv()

    def start(self, a):
        for way, dev in (("z", self.pair), ("r", self.right), ("l", self.left)):
            self.send(f"{a}o{way}", self.own(a), self.piece(a, self.j, self.z, None), dev)

    def s2(self):
        self.got("0or", 0, self.jl, self.z, None)
        self.pass_on("0lr", self.right, 0, self.jl, self.z, 0)
        self.pass_on("0lz", self.pair, 0, self.jl, self.z, None)

    def s3(self):
        self.got("0ol", 0, self.jr, self.z, None)
        self.pass_on("0rl", self.left, 0, self.jr, self.z, 1)
        self.pass_on("0rz", self.pair, 0, self.jr, self.z, None)

    def s4(self):
        self.got("1oz", 1, self.j, 1 - self.z, None)
        self.pass_on("1zr", self.right, 1, self.j, 1 - self.z, None)
        self.pass_on("1zl", self.left, 1, self.j, 1 - self.z, None)

    def s5(self):
        self.got("1or", 1, self.jl, self.z, None)
        self.pass_on("1lr", self.right, 1, self.jl, self.z, 0)

    def s6(self):
        self.got("1ol", 1, self.jr, self.z, None)
        self.pass_on("1rl", self.left, 1, self.jr, self.z, 1)

    def s7(self):
        self.got("0lr", 0, self.jd, self.z, 0)
        self.pass_on("0dz", self.pair, 0, self.jd, self.z, 0)

    def s8(self):
        self.got("0rl", 0, self.jd, self.z, 1)
        self.pass_on("0ez", self.pair, 0, self.jd, self.z, 1)

    def s9(self):
        self.got("1zr", 1, self.jl, 1 - self.z, None)
        self.pass_on("1kr", self.right, 1, self.jl, 1 - self.z, 0)

    def s10(self):
        self.got("1zl", 1, self.jr, 1 - self.z, None)
        self.pass_on("1ql", self.left, 1, self.jr, 1 - self.z, 1)

    def end_of_1_d(self):
        self.got("1lr", 1, self.jd, self.z, 0)
        self.got("1rl", 1, self.jd, self.z, 1)

    def end_of_1_e(self):
        self.got("1kr", 1, self.jd, 1 - self.z, 0)
        self.got("1ql", 1, self.jd, 1 - self.z, 1)

    def end_of_0_d(self):
        self.got("0dz", 0, self.jd, 1 - self.z, 0)
        self.got("0ez", 0, self.jd, 1 - self.z, 1)

    def drain(self):
        for copy in self.sent:
            copy.wait_send()


def meet(partners):
    barrier = pltpu.get_barrier_semaphore()
    for dev in partners:
        pl.semaphore_signal(barrier, inc=1, device_id=dev, device_id_type=MESH)
    pl.semaphore_wait(barrier, len(partners))


def others(x, zh):
    for k in range(1, 8):
        dx, dz = k // 2, k % 2
        yield k, ((4 - dx) % 4) * 2 + dz, (x + dx) % 4, (zh + dz) % 2


def dispatch_kernel(
    s1, s2, ms, cold, extra, mr, bounce, mbounce,
    st_s, st_r, m_s, m_r, sib_s, sib_r, dp_s, dp_r, ex_s, ex_r, xs_s, xs_r, loc,
):
    e, d, x, zh, c, y, zl = place()
    dbar = y * 2 + 1 - zl
    sib = to(expert_at(x, zh, 1 - c), d)
    d_r, d_l = ((y + 1) % 4) * 2 + zl, ((y + 3) % 4) * 2 + zl
    peers = [
        (rel, back, expert_at(x2, zh2, c2), d if rel % 2 == 0 else dbar, x2 * 2 + c2)
        for rel, back, x2, zh2 in others(x, zh)
        for c2 in (0, 1)
    ]
    x_r = to(expert_at((x + 1) % 4, zh, c), d)
    x_l = to(expert_at((x + 3) % 4, zh, c), d)
    z_p = to(expert_at(x, 1 - zh, c), dbar)
    meet([to(p[2], p[3]) for p in peers] + [sib, to(e, d_r), to(e, d_l), to(e, dbar)])

    sent, msent = [], []
    for a in (0, 1):
        for rel, back, e2, d2, q in peers:
            copy = pltpu.make_async_remote_copy(
                s1.at[a, rel % 2, pl.ds(pl.multiple_of(q * SLOT, SLOT), SLOT), :],
                cold.at[a, d2, pl.ds(pl.multiple_of((back * 2 + c) * SLOT, SLOT), SLOT), :],
                st_s.at[a], st_r.at[a], device_id=to(e2, d2), device_id_type=MESH,
            )
            copy.start()
        if a == 0:
            own_in = [
                pltpu.make_async_copy(s2.at[:, :, 0:SLOT, :], bounce.at[0], loc.at[0]),
                pltpu.make_async_copy(s2.at[:, :, 2 * SLOT :, :], bounce.at[1], loc.at[1]),
                pltpu.make_async_copy(ms.at[e], mbounce, loc.at[2]),
            ]
            for copy in own_in:
                copy.start()
    for n, (_, back, e2, d2, _) in enumerate(peers + [(0, 0, expert_at(x, zh, 1 - c), d, 0)]):
        copy = pltpu.make_async_remote_copy(
            ms.at[e2], mr.at[back * 2 + c], m_s.at[n], m_r.at[back * 2 + c],
            device_id=to(e2, d2), device_id_type=MESH,
        )
        copy.start()
        msent.append(copy)
    sib_copy = pltpu.make_async_remote_copy(
        s2.at[:, :, SLOT : 2 * SLOT, :],
        cold.at[:, :, pl.ds(pl.multiple_of(c * SLOT, SLOT), SLOT), :],
        sib_s, sib_r, device_id=sib, device_id_type=MESH,
    )
    sib_copy.start()
    sent.append(sib_copy)
    for copy in own_in:
        copy.wait()
    own_out = [
        pltpu.make_async_copy(
            bounce.at[0], cold.at[:, :, pl.ds(pl.multiple_of(c * SLOT, SLOT), SLOT), :], loc.at[3]
        ),
        pltpu.make_async_copy(
            bounce.at[1], extra.at[:, :, pl.ds(pl.multiple_of(e * SLOT, SLOT), SLOT), :], loc.at[4]
        ),
        pltpu.make_async_copy(mbounce, mr.at[c], loc.at[5]),
    ]
    for copy in own_out:
        copy.start()

    half = (ROWS - LOCAL) // 2

    def dp_piece(a, j, z, h):
        rows = {None: (LOCAL, 2 * half), 0: (LOCAL, half), 1: (LOCAL + half, half)}[h]
        return cold.at[a, j * 2 + z, pl.ds(*rows), :]

    def ex_piece_of(core):
        def piece(a, j, z, h):
            chunks = {None: (0, NDP), 0: (0, NDP // 2), 1: (NDP // 2, NDP // 2)}[h]
            at = pl.multiple_of(expert_at(j, z, core) * SLOT, SLOT)
            return extra.at[a, pl.ds(*chunks), pl.ds(at, SLOT), :]
        return piece

    ex_piece, ex_other = ex_piece_of(c), ex_piece_of(1 - c)

    dp = Gather(
        lambda a: dp_piece(a, y, zl, None), dp_piece, y, zl,
        to(e, d_r), to(e, d_l), to(e, dbar), dp_s, dp_r,
    )
    ex = Gather(
        lambda a: s2.at[a, :, 2 * SLOT :, :], ex_piece, x, zh, x_r, x_l, z_p, ex_s, ex_r,
    )
    shares = []

    def share(a, j, z, src=None):
        i = len(shares)
        dst = ex_piece(a, j, z, None)
        copy = pltpu.make_async_remote_copy(
            dst if src is None else src, dst, xs_s.at[i], xs_r.at[i],
            device_id=sib, device_id_type=MESH,
        )
        copy.start()
        shares.append((copy, (a, j, z)))

    def whole(a):
        ref = cold.at[a, d, pl.ds(LOCAL, ROWS - LOCAL), :]
        return pltpu.make_async_remote_copy(
            ref, ref, st_s.at[a], st_r.at[a], device_id=sib, device_id_type=MESH
        )

    whole(0).wait_recv()
    dp.start(0)
    ex.start(0)
    whole(1).wait_recv()
    dp.start(1)
    ex.start(1)
    share(0, x, zh, s2.at[0, :, 2 * SLOT :, :])
    share(1, x, zh, s2.at[1, :, 2 * SLOT :, :])
    ex.s2()
    ex.s3()
    dp.s2()
    dp.s3()
    ex.s4()
    ex.s5()
    ex.s6()
    for a, j, z in ((0, ex.jl, zh), (0, ex.jr, zh), (1, x, 1 - zh), (1, ex.jl, zh), (1, ex.jr, zh)):
        share(a, j, z)
    ex.s7()
    ex.s8()
    share(0, ex.jd, zh)
    dp.s4()
    dp.s5()
    dp.s6()
    ex.s9()
    ex.s10()
    share(1, ex.jl, 1 - zh)
    share(1, ex.jr, 1 - zh)
    dp.s7()
    dp.s8()
    dp.s9()
    dp.s10()
    ex.got("0oz", 0, x, 1 - zh, None)
    share(0, x, 1 - zh)
    ex.got("0lz", 0, ex.jl, 1 - zh, None)
    share(0, ex.jl, 1 - zh)
    ex.got("0rz", 0, ex.jr, 1 - zh, None)
    share(0, ex.jr, 1 - zh)
    ex.end_of_1_d()
    share(1, ex.jd, zh)
    ex.end_of_1_e()
    share(1, ex.jd, 1 - zh)
    ex.end_of_0_d()
    share(0, ex.jd, 1 - zh)
    for i, (copy, where) in enumerate(shares):
        ref = ex_other(*where, None)
        pltpu.make_async_remote_copy(
            ref, ref, xs_s.at[i], xs_r.at[i], device_id=sib, device_id_type=MESH
        ).wait_recv()
    dp.end_of_1_d()
    dp.end_of_1_e()
    dp.got("0oz", 0, y, 1 - zl, None)
    dp.got("0lz", 0, dp.jl, 1 - zl, None)
    dp.got("0rz", 0, dp.jr, 1 - zl, None)
    dp.end_of_0_d()
    for i in [1 - c] + list(range(2, E)):
        pltpu.make_async_remote_copy(
            ms.at[0], mr.at[i], m_s.at[0], m_r.at[i], device_id=sib, device_id_type=MESH
        ).wait_recv()
    for copy in sent:
        copy.wait()
    for copy in msent:
        copy.wait_send()
    whole(0).wait_send()
    whole(1).wait_send()
    for copy in own_out:
        copy.wait()
    for copy, _ in shares:
        copy.wait_send()
    dp.drain()
    ex.drain()


def dispatch(s1, s2, m):
    D = pltpu.SemaphoreType.DMA
    return pl.pallas_call(
        dispatch_kernel,
        in_specs=[ANY, ANY, ANY],
        out_specs=[ANY, ANY, ANY],
        out_shape=[
            jax.ShapeDtypeStruct((2, NDP, ROWS, W), bf16),
            jax.ShapeDtypeStruct((2, NDP, ROWS, W), bf16),
            jax.ShapeDtypeStruct((E, 8, 128), f32),
        ],
        scratch_shapes=[
            pltpu.VMEM((2, 2, NDP, SLOT, W), bf16),
            pltpu.VMEM((8, 128), f32),
            D((2,)), D((2,)), D((15,)), D((16,)), D, D,
            D((18,)), D((18,)), D((18,)), D((18,)), D((16,)), D((16,)), D((6,)),
        ],
        compiler_params=pltpu.CompilerParams(collective_id=1, has_side_effects=True),
        name="dispatch",
    )(s1, s2, m)


def sigmoid(v):
    return 1.0 / (1.0 + jnp.exp(-v))


def gate_row(mr, t):
    _, _, x, _, c, _, _ = place()
    parts = []
    for g in range(E // 4):
        at = g * 4 if t == 0 else ((g - x) & 3) * 4
        part = mr[at, t : t + 1, :]
        for i in range(1, 4):
            part = part + mr[at + i, t : t + 1, :]
        parts.append(part if t == 0 else part * mr[c, 3:4, :])
    return jnp.concatenate(parts, axis=1)


def experts_kernel(
    hot_ref, mr, cold, extra_hbm, wg, wu, wd,
    dxc, dxh, gp, gg, gu, gd,
    extra, acc, lhs, rhs, stage, sem, osem,
):
    hot = hot_ref[0] > 0
    FFL = wg.shape[0]

    @pl.when(hot)
    def _():
        pltpu.make_async_copy(extra_hbm, extra, sem).start()

    def cols(j):
        return pl.ds(pl.multiple_of(j * W, W), W)

    def forward(rows_ref, t):
        acc[...] = jnp.zeros_like(acc)

        def step(j, _):
            xj, dj = rows_ref[0, j], rows_ref[1, j]
            acc[0] += nt(wg[:, cols(j)], xj)
            acc[1] += nt(wu[:, cols(j)], xj)
            acc[2] += nt(wd[:, cols(j)], dj)
            return 0

        lax.fori_loop(0, NDP, step, 0)
        gate = gate_row(mr, t)
        pre, up, g = acc[0], acc[1], acc[2]
        s = sigmoid(pre)
        active = pre * s
        hidden = (active * up).astype(bf16).astype(f32)
        gp[0:1, t * ROWS : (t + 1) * ROWS] = jnp.sum(hidden * g, axis=0, keepdims=True)
        gh = g * gate
        d_up = gh * active
        d_pre = gh * up * s * (1.0 + pre * (1.0 - s))
        lhs[t, 0] = d_pre.astype(bf16)
        lhs[t, 1] = d_up.astype(bf16)
        lhs[t, 2] = (hidden * gate).astype(bf16)
        rhs[t, :, 0:FFL] = d_pre.T.astype(bf16)
        rhs[t, :, FFL : 2 * FFL] = d_up.T.astype(bf16)

    forward(cold, 0)

    @pl.when(hot)
    def _():
        pltpu.make_async_copy(extra_hbm, extra, sem).wait()
        forward(extra, 1)

    @pl.when(jnp.logical_not(hot))
    def _():
        gp[0:1, ROWS : 2 * ROWS] = jnp.zeros((1, ROWS), f32)

    outs = (gg, gu, gd)

    def put(j, slot, i):
        return pltpu.make_async_copy(
            stage.at[slot, i], outs[i].at[:, cols(j)], osem.at[slot, i]
        )

    def step(j, sq):
        slot = j % 2

        @pl.when(j >= 2)
        def _():
            for i in range(3):
                put(j - 2, slot, i).wait()

        w2 = (wg[:, cols(j)], wu[:, cols(j)])

        def back(t, out):
            r = jnp.dot(rhs[t, :, 0:FFL], w2[0], preferred_element_type=f32)
            r += jnp.dot(rhs[t, :, FFL : 2 * FFL], w2[1], preferred_element_type=f32)
            out[j] = r.astype(bf16)

        back(0, dxc)
        for i in range(3):
            stage[slot, i] = jnp.dot(lhs[0, i], cold[i // 2, j], preferred_element_type=f32)

        @pl.when(hot)
        def _():
            back(1, dxh)
            for i in range(3):
                stage[slot, i] += jnp.dot(lhs[1, i], extra[i // 2, j], preferred_element_type=f32)

        @pl.when(jnp.logical_not(hot))
        def _():
            dxh[j] = jnp.zeros((ROWS, W), bf16)

        for i in range(3):
            v = stage[slot, i]
            sq = sq + jnp.sum((v * v).reshape(-1, 8, W), axis=0)
            put(j, slot, i).start()
        return sq

    sq = lax.fori_loop(0, NDP, step, jnp.zeros((8, W), f32))
    total = jnp.sum(jnp.sum(sq, axis=0, keepdims=True), axis=1, keepdims=True)
    gp[0:1, 2 * ROWS :] = jnp.broadcast_to(total, (1, GW - 2 * ROWS))
    for j in (NDP - 2, NDP - 1):
        for i in range(3):
            put(j, j % 2, i).wait()


def experts(hot, mr, cold, extra, wg, wu, wd):
    FFL, D = wg.shape
    return pl.pallas_call(
        experts_kernel,
        in_specs=[SM, VM, VM, ANY, VM, VM, VM],
        out_specs=[VM, VM, VM, ANY, ANY, ANY],
        out_shape=[
            jax.ShapeDtypeStruct((NDP, ROWS, W), bf16),
            jax.ShapeDtypeStruct((NDP, ROWS, W), bf16),
            jax.ShapeDtypeStruct((1, GW), f32),
        ]
        + [jax.ShapeDtypeStruct((FFL, D), f32)] * 3,
        scratch_shapes=[
            pltpu.VMEM((2, NDP, ROWS, W), bf16),
            pltpu.VMEM((3, FFL, ROWS), f32),
            pltpu.VMEM((2, 3, FFL, ROWS), bf16),
            pltpu.VMEM((2, ROWS, 2 * FFL), bf16),
            pltpu.VMEM((2, 3, FFL, W), f32),
            pltpu.SemaphoreType.DMA,
            pltpu.SemaphoreType.DMA((2, 3)),
        ],
        compiler_params=pltpu.CompilerParams(vmem_limit_bytes=60 * 1024 * 1024),
        name="experts",
    )(hot, mr, cold, extra, wg, wu, wd)


def add_into(out, *terms):
    n, rows, _ = out.shape
    step_rows = min(rows, 64)
    for i in range(n):

        def step(k, _):
            r = pl.ds(pl.multiple_of(k * step_rows, step_rows), step_rows)
            total = terms[0][i, r, :].astype(f32)
            for term in terms[1:]:
                total = total + term[i, r, :].astype(f32)
            out[i, r, :] = total.astype(out.dtype)
            return 0

        if rows == step_rows:
            step(0, 0)
        else:
            lax.fori_loop(0, rows // step_rows, step, 0)


class Scatter:
    names = (
        "ar0", "ar1", "al0", "al1", "br0", "br1", "bl0", "bl1", "cr0", "cr1", "cl0", "cl1", "p",
        "zd", "zr", "zl", "z0", "hr", "hl", "ir", "il", "kr", "kl",
    )

    @staticmethod
    def scratch(piece, half):
        V = pltpu.VMEM
        return [
            V((2,) + half, bf16), V((2,) + half, bf16), V((2,) + half, bf16), V((2,) + half, bf16),
            V((2,) + piece, bf16), V((2,) + piece, bf16),
            V(piece, bf16), V(piece, bf16), V(piece, f32),
            V((4,) + piece, bf16), V((4,) + piece, bf16),
            V(half, bf16), V(half, bf16), V(piece, bf16), V(piece, bf16),
            pltpu.SemaphoreType.DMA((23,)), pltpu.SemaphoreType.DMA((23,)),
        ]

    def __init__(self, chunk, cut, j, z, right, left, pair, refs):
        self.chunk, self.cut, self.j, self.z = chunk, cut, j, z
        self.jl, self.jr, self.jd = (j + 3) % 4, (j + 1) % 4, (j + 2) % 4
        self.right, self.left, self.pair = right, left, pair
        (
            self.rl, self.rr, self.tr, self.tl, self.fl, self.fr, self.zs, self.zin, self.own,
            self.hz, self.hw, self.hrl, self.hrr, self.hfl, self.hfr, self.ssem, self.rsem,
        ) = refs
        self.sent = []

    def send(self, name, src, dst, dev):
        i = self.names.index(name)
        copy = pltpu.make_async_remote_copy(
            src, dst, self.ssem.at[i], self.rsem.at[i], device_id=dev, device_id_type=MESH
        )
        copy.start()
        self.sent.append(copy)

    def got(self, name, ref):
        i = self.names.index(name)
        pltpu.make_async_remote_copy(
            ref, ref, self.ssem.at[i], self.rsem.at[i], device_id=self.pair, device_id_type=MESH
        ).wait_recv()

    def start0_far(self):
        for k in (0, 1):
            far = self.chunk(0, self.jd, k)
            self.send(f"ar{k}", self.cut(far, 0), self.rl.at[k], self.right)
            self.send(f"al{k}", self.cut(far, 1), self.rr.at[k], self.left)

    def start0_near(self):
        for k in (0, 1):
            right, left = self.chunk(0, self.jr, k), self.chunk(0, self.jl, k)
            self.send(f"br{k}", self.cut(right, 1), self.cut(self.fl.at[k], 1), self.right)
            self.send(f"bl{k}", self.cut(left, 0), self.cut(self.fr.at[k], 0), self.left)

    def start1(self):
        for way, j in (("d", self.jd), ("r", self.jr), ("l", self.jl), ("0", self.j)):
            self.send("z" + way, self.chunk(1, j, 1 - self.z), self.hz.at[j], self.pair)

    def relay0(self):
        for k in (0, 1):
            self.got(f"ar{k}", self.rl.at[k])
            add_into(self.tr.at[k], self.cut(self.chunk(0, self.jr, k), 0), self.rl.at[k])
            self.send(f"cr{k}", self.tr.at[k], self.cut(self.fl.at[k], 0), self.right)
            self.got(f"al{k}", self.rr.at[k])
            add_into(self.tl.at[k], self.cut(self.chunk(0, self.jl, k), 1), self.rr.at[k])
            self.send(f"cl{k}", self.tl.at[k], self.cut(self.fr.at[k], 1), self.left)

    def pair0(self):
        for k in (0, 1):
            for n, ref, h in (("br", self.fl, 1), ("bl", self.fr, 0), ("cr", self.fl, 0), ("cl", self.fr, 1)):
                self.got(f"{n}{k}", self.cut(ref.at[k], h))
        k = 1 - self.z
        add_into(self.zs, self.chunk(0, self.j, k), self.fl.at[k], self.fr.at[k])
        self.send("p", self.zs, self.zin, self.pair)
        k = self.z
        add_into(self.own, self.chunk(0, self.j, k), self.fl.at[k], self.fr.at[k])

    def end0(self, out):
        self.got("p", self.zin)
        add_into(out, self.own, self.zin)

    def relay1_far(self):
        self.got("zd", self.hz.at[self.jd])
        w = self.hw.at[self.jd]
        add_into(w, self.chunk(1, self.jd, self.z), self.hz.at[self.jd])
        self.send("hr", self.cut(w, 0), self.hrl, self.right)
        self.send("hl", self.cut(w, 1), self.hrr, self.left)

    def relay1_near(self):
        for way, j, h, ref, dev in (
            ("r", self.jr, 1, self.hfl, self.right), ("l", self.jl, 0, self.hfr, self.left)
        ):
            self.got("z" + way, self.hz.at[j])
            w = self.cut(self.hw.at[j], h)
            add_into(w, self.cut(self.chunk(1, j, self.z), h), self.cut(self.hz.at[j], h))
            self.send("i" + way, w, self.cut(ref, h), dev)

    def relay1_last(self):
        for way, j, h, inp, ref, dev in (
            ("r", self.jr, 0, self.hrl, self.hfl, self.right),
            ("l", self.jl, 1, self.hrr, self.hfr, self.left),
        ):
            self.got("h" + way, inp)
            w = self.cut(self.hw.at[j], h)
            add_into(w, self.cut(self.chunk(1, j, self.z), h), self.cut(self.hz.at[j], h), inp)
            self.send("k" + way, w, self.cut(ref, h), dev)

    def end1(self, out):
        self.got("z0", self.hz.at[self.j])
        self.got("ir", self.cut(self.hfl, 1))
        self.got("il", self.cut(self.hfr, 0))
        self.got("kr", self.cut(self.hfl, 0))
        self.got("kl", self.cut(self.hfr, 1))
        add_into(out, self.chunk(1, self.j, self.z), self.hz.at[self.j], self.hfl, self.hfr)

    def drain(self):
        for copy in self.sent:
            copy.wait_send()


HR = ROWS // 2
C_PIECE, C_HALF = (1, HR, W), (1, HR // 2, W)
H_PIECE, H_HALF = (NDP // 2, SLOT, W), (NDP // 4, SLOT, W)


def combine_kernel(dxc, dxh, gp, back, backh, gback, *refs):
    e, d, x, zh, c, y, zl = place()
    c_refs, refs = refs[:17], refs[17:]
    h_refs, refs = refs[:17], refs[17:]
    rc, hs, hin, outh, hp, gall, gsum, g_s, g_r, b_s, b_r, gb_s, gb_r, x_s, x_r, q_s, q_r = refs
    dbar = y * 2 + 1 - zl
    sib = to(expert_at(x, zh, 1 - c), d)
    peers, places, mine = [expert_at(x, zh, 1 - c)], [1 - c], [c]
    for rel, seen, x2, zh2 in others(x, zh):
        for c2 in (0, 1):
            peers.append(expert_at(x2, zh2, c2))
            places.append(rel * 2 + c2)
            mine.append(seen * 2 + c)
    dps = [(d + k) % NDP for k in range(1, NDP)]
    z_p = to(expert_at(x, 1 - zh, c), dbar)
    meet([to(e2, d) for e2 in peers] + [to(e, d2) for d2 in dps] + [z_p])

    C = Scatter(
        lambda a, j, z: dxc.at[pl.ds(j * 2 + z, 1), pl.ds(a * HR, HR)],
        lambda ref, h: ref.at[:, pl.ds(h * (HR // 2), HR // 2)],
        y, zl, to(e, ((y + 1) % 4) * 2 + zl), to(e, ((y + 3) % 4) * 2 + zl), to(e, dbar), c_refs,
    )
    X = Scatter(
        lambda a, j, z: hs.at[j * 2 + z, pl.ds(a * (NDP // 2), NDP // 2)],
        lambda ref, h: ref.at[pl.ds(h * (NDP // 4), NDP // 4)],
        x, zh, to(expert_at((x + 1) % 4, zh, c), d), to(expert_at((x + 3) % 4, zh, c), d), z_p,
        h_refs,
    )
    far = [X.jd * 2, X.jd * 2 + 1, X.jr * 2, X.jl * 2, X.jr * 2 + 1, X.jl * 2 + 1, x * 2, x * 2 + 1]

    def h_rows(chip, core):
        return pl.ds(pl.multiple_of((chip * 2 + core) * SLOT, SLOT), SLOT)

    rest = []

    def send(src, dst, ssem, rsem, dev):
        copy = pltpu.make_async_remote_copy(
            src, dst, ssem, rsem, device_id=dev, device_id_type=MESH
        )
        copy.start()
        rest.append(copy)

    def wait(ref, ssem, rsem):
        pltpu.make_async_remote_copy(
            ref, ref, ssem, rsem, device_id=sib, device_id_type=MESH
        ).wait_recv()

    C.start0_far()
    C.start1()
    for i, chip in enumerate(far):
        send(dxh.at[:, h_rows(chip, 1 - c)], hin.at[chip], x_s.at[i], x_r.at[i], sib)
    C.start0_near()
    for k, d2 in enumerate(dps):
        send(gp, gall.at[d], g_s.at[k], g_r.at[k], to(e, d2))
    gall[d] = gp[...]
    for i, chip in enumerate(far):
        wait(hin.at[chip], x_s.at[i], x_r.at[i])
        add_into(hs.at[chip], dxh.at[:, h_rows(chip, c)], hin.at[chip])
        if i == 1:
            X.start0_far()
        if i == 5:
            X.start0_near()
    X.start1()

    for k in range(NDP - 1):
        wait(gall.at[(d + NDP - 1 - k) % NDP], g_s.at[k], g_r.at[k])
    total = gall[0]
    for k in range(1, NDP):
        total = total + gall[k]
    gsum[...] = total
    gback[e] = total
    for n, e2 in enumerate(peers):
        send(gsum, gback.at[e], gb_s.at[n], gb_r.at[mine[n]], to(e2, d))

    C.relay0()
    C.relay1_far()
    X.relay0()
    X.relay1_far()
    X.relay1_near()
    C.relay1_near()
    X.relay1_last()
    X.pair0()
    C.relay1_last()
    C.pair0()
    X.end1(outh.at[pl.ds(NDP // 2, NDP // 2)])
    X.end0(outh.at[pl.ds(0, NDP // 2)])
    for k, d2 in enumerate(dps):
        send(outh.at[d2], hp.at[d], q_s.at[k], q_r.at[k], to(e, d2))
    hp[d] = outh[d]

    def give(a):
        for n, e2 in enumerate(peers):
            if (n >= 7) == (a == 1):
                send(
                    rc.at[0, pl.ds(pl.multiple_of(places[n] * SLOT, SLOT), SLOT), :],
                    back.at[e], b_s.at[n], b_r.at[mine[n]], to(e2, d),
                )

    C.end1(rc.at[:, pl.ds(HR, HR)])
    give(1)
    C.end0(rc.at[:, pl.ds(0, HR)])
    give(0)
    back[e] = rc[0, pl.ds(pl.multiple_of(c * SLOT, SLOT), SLOT), :]
    for k in range(NDP - 1):
        wait(hp.at[(d + NDP - 1 - k) % NDP], q_s.at[k], q_r.at[k])
    total = hp[0].astype(f32)
    for k in range(1, NDP):
        total = total + hp[k].astype(f32)
    backh[...] = total.astype(bf16)

    for i in [1 - c] + list(range(2, E)):
        wait(back.at[0], b_s.at[0], b_r.at[i])
        wait(gback.at[0], gb_s.at[0], gb_r.at[i])
    for copy in rest:
        copy.wait_send()
    C.drain()
    X.drain()


def combine(dxc, dxh, gp):
    D = pltpu.SemaphoreType.DMA
    V = pltpu.VMEM
    return pl.pallas_call(
        combine_kernel,
        in_specs=[VM, VM, VM],
        out_specs=[VM, VM, VM],
        out_shape=[
            jax.ShapeDtypeStruct((E, SLOT, W), bf16),
            jax.ShapeDtypeStruct((SLOT, W), bf16),
            jax.ShapeDtypeStruct((E, 1, GW), f32),
        ],
        scratch_shapes=Scatter.scratch(C_PIECE, C_HALF)
        + Scatter.scratch(H_PIECE, H_HALF)
        + [
            V((1, ROWS, W), bf16),
            V((NDP, NDP, SLOT, W), bf16), V((NDP, NDP, SLOT, W), bf16),
            V((NDP, SLOT, W), bf16), V((NDP, SLOT, W), bf16),
            V((NDP, 1, GW), f32), V((1, GW), f32),
            D((7,)), D((7,)), D((15,)), D((16,)), D((15,)), D((16,)),
            D((8,)), D((8,)), D((7,)), D((7,)),
        ],
        compiler_params=pltpu.CompilerParams(
            collective_id=2, has_side_effects=True, vmem_limit_bytes=60 * 1024 * 1024
        ),
        name="combine",
    )(dxc, dxh, gp)


def finish_kernel(ids_ref, logits_ref, back, backh, gback, mr, rows_ref, gl_ref, norm_ref):
    e, _, x, zh, c, _, _ = place()
    ids = ids_ref[...]
    onehot, rank = row_facts(ids, E)
    probs = soft(logits_ref[...])
    n = ids.shape[1]
    first = rank < SLOT
    slot = lax.broadcasted_iota(jnp.int32, (ROWS, n), 0)
    pick = (slot == jnp.where(first, ids * SLOT + rank, -1)).astype(f32).astype(bf16)
    slot = lax.broadcasted_iota(jnp.int32, (SLOT, n), 0)
    pickh = (slot == rank - SLOT).astype(f32).astype(bf16)
    got = tn(pick, back[...].reshape(ROWS, W)) + tn(pickh, backh[...])
    rows_ref[...] = got.astype(bf16)
    rel = seen_from(ids, x, zh, c)
    lane = jnp.where(first, rel * SLOT + rank, ROWS + e * SLOT + rank - SLOT)
    slot = lax.broadcasted_iota(jnp.int32, (2 * ROWS, n), 0)
    here = (slot == lane).astype(f32).astype(bf16)
    found = jnp.dot(gback[:, 0, 0 : 2 * ROWS].astype(bf16), here, preferred_element_type=f32)
    dgate = jnp.sum(onehot * found, axis=0, keepdims=True)
    count = jnp.sum(mr[...], axis=0)[2:3, :]
    across = lax.broadcasted_iota(jnp.int32, (E, 128), 0)
    diag = across == lax.broadcasted_iota(jnp.int32, (E, 128), 1)
    column = jnp.sum(jnp.where(diag, jnp.broadcast_to(count, (E, 128)), 0.0), axis=1, keepdims=True)
    pulls = onehot * dgate + 1.0 * E * (column / (E * n))
    gl_ref[...] = probs * (pulls - jnp.sum(probs * pulls, axis=0, keepdims=True))
    norm_ref[...] = jnp.sqrt(jnp.sum(gback[:, 0, 2 * ROWS : 2 * ROWS + 128], axis=0, keepdims=True))


def finish(ids, logits, back, backh, gback, mr):
    n = ids.shape[1]
    return pl.pallas_call(
        finish_kernel,
        in_specs=[VM] * 6,
        out_specs=[VM] * 3,
        out_shape=[
            jax.ShapeDtypeStruct((n, W), bf16),
            jax.ShapeDtypeStruct((E, n), f32),
            jax.ShapeDtypeStruct((1, 128), f32),
        ],
        name="finish",
    )(ids, logits, back, backh, gback, mr)


def local(rows_x, rows_dy, router_logits, expert_of, w_gate, w_up, w_down):
    c = place()[4]
    ids = expert_of.reshape(1, -1)
    logits = router_logits.T
    s1, s2, m = lay_out(ids, logits, rows_x, rows_dy)
    cold, extra, mr = dispatch(s1, s2, m)
    hot = mr[c, 3, 0].astype(jnp.int32).reshape(1)
    dxc, dxh, gp, gg, gu, gd = experts(hot, mr, cold, extra, w_gate[0], w_up[0], w_down[0])
    back, backh, gback = combine(dxc, dxh, gp)
    grad_rows, grad_logits, norm = finish(ids, logits, back, backh, gback, mr)
    return grad_rows, grad_logits.T, gg[None], gu[None], gd[None], norm[0, 0]


def solution(mesh):
    rows = P("expert", None)
    weights = P("expert", "dp", None)
    return jax.shard_map(
        local,
        mesh=mesh,
        in_specs=(rows, rows, rows, rows, weights, weights, weights),
        out_specs=(P("expert", "dp"), rows, weights, weights, weights, P()),
        check_vma=False,
    )
```

```python
import jax
import jax.numpy as jnp
from jax import lax
from jax.experimental import pallas as pl
from jax.experimental.pallas import tpu as pltpu
from jax.sharding import PartitionSpec as P

f32 = jnp.float32
bf16 = jnp.bfloat16
MESH = pl.DeviceIdType.MESH
ANY = pl.BlockSpec(memory_space=pl.ANY)
VM = pl.BlockSpec(memory_space=pltpu.VMEM)
SM = pl.BlockSpec(memory_space=pltpu.SMEM)

E = 16
NDP = 8
SLOT = 32
W = 512
ROWS = E * SLOT
LOCAL = 2 * SLOT
GW = 1280


def place():
    e = lax.axis_index("expert")
    d = lax.axis_index("dp")
    return e, d, e // 4, (e // 2) % 2, e % 2, d // 2, d % 2


def expert_at(x, zh, c):
    return (x * 2 + zh) * 2 + c


def to(e, d):
    return {"expert": e, "dp": d}


def row_facts(ids, experts):
    rows = ids.shape[1]
    onehot = (lax.broadcasted_iota(jnp.int32, (experts, rows), 0) == ids).astype(f32)
    before = lax.broadcasted_iota(jnp.int32, (rows, rows), 0) < lax.broadcasted_iota(
        jnp.int32, (rows, rows), 1
    )
    earlier = jnp.dot(onehot.astype(bf16), before.astype(bf16), preferred_element_type=f32)
    rank = jnp.sum(onehot * earlier, axis=0, keepdims=True).astype(jnp.int32)
    return onehot, rank


def soft(logits):
    top = jnp.max(logits, axis=0, keepdims=True)
    ex = jnp.exp(logits - top)
    return ex / jnp.sum(ex, axis=0, keepdims=True)


def nt(a, b):
    return lax.dot_general(a, b, (((1,), (1,)), ((), ())), preferred_element_type=f32)


def tn(a, b):
    return lax.dot_general(a, b, (((0,), (0,)), ((), ())), preferred_element_type=f32)


def seen_from(ids, x, zh, c):
    return (((x - (ids >> 2)) & 3) * 2 + (zh ^ ((ids >> 1) & 1))) * 2 + c


def slots_kernel(ids_ref, logits_ref, x_ref, dy_ref, s1_ref, s2_ref, m_ref):
    e, d, x, zh, c, y, zl = place()
    ids = ids_ref[...]
    onehot, rank = row_facts(ids, E)
    rows = ids.shape[1]
    none = -1

    def perm(slots, target):
        slot = lax.broadcasted_iota(jnp.int32, (slots, rows), 0)
        return (slot == target).astype(f32).astype(bf16)

    far = (zh ^ ((ids >> 1) & 1)) == 1
    first = rank < SLOT
    chip = ((ids >> 2) * 2 + (ids & 1)) * SLOT + rank
    for g, ours in ((0, jnp.logical_not(far)), (1, far)):
        p = perm(ROWS // 2, jnp.where(first & ours, chip, none))
        at = pl.ds(pl.multiple_of((d if g == 0 else y * 2 + 1 - zl) * W, W), W)
        s1_ref[0, g] = jnp.dot(p, x_ref[:, at], preferred_element_type=f32).astype(bf16)
        s1_ref[1, g] = jnp.dot(p, dy_ref[:, at], preferred_element_type=f32).astype(bf16)
    home = jnp.where(ids == e, rank, jnp.where(ids == e + 1 - 2 * c, SLOT + rank, none))
    p = perm(3 * SLOT, jnp.where(first, home, SLOT + rank))
    for j in range(NDP):
        at = slice(j * W, (j + 1) * W)
        s2_ref[0, j] = jnp.dot(p, x_ref[:, at], preferred_element_type=f32).astype(bf16)
        s2_ref[1, j] = jnp.dot(p, dy_ref[:, at], preferred_element_type=f32).astype(bf16)

    gate = jnp.sum(soft(logits_ref[...]) * onehot, axis=0, keepdims=True).astype(bf16).astype(f32)
    lane = lax.broadcasted_iota(jnp.int32, (128, rows), 0)
    spot = (seen_from(ids, x, zh, c) & 3) * SLOT + rank
    cold = (onehot * gate * first.astype(f32)).astype(bf16)
    cold = nt(cold, (lane == spot).astype(f32).astype(bf16))
    gate8 = jnp.broadcast_to(gate, (8, rows)).astype(bf16)
    spot = jnp.where(first, none, (e & 3) * SLOT + rank - SLOT)
    hot = nt(gate8, (lane == spot).astype(f32).astype(bf16))
    count = nt(jnp.ones((8, rows), bf16), (lane == ids).astype(f32).astype(bf16))
    line = lax.broadcasted_iota(jnp.int32, (8, 128), 0)
    for k in range(E):
        mine = jnp.broadcast_to(cold[k : k + 1, :], (8, 128))
        busy = (jnp.sum(onehot[k : k + 1, :], axis=1, keepdims=True) > SLOT).astype(f32)
        rest = jnp.where(line == 2, count, jnp.broadcast_to(busy, (8, 128)))
        m_ref[k] = jnp.where(line == 0, mine, jnp.where(line == 1, hot, rest))


def lay_out(ids, logits, x, dy):
    return pl.pallas_call(
        slots_kernel,
        in_specs=[VM] * 4,
        out_specs=[VM] * 3,
        out_shape=[
            jax.ShapeDtypeStruct((2, 2, ROWS // 2, W), bf16),
            jax.ShapeDtypeStruct((2, NDP, 3 * SLOT, W), bf16),
            jax.ShapeDtypeStruct((E, 8, 128), f32),
        ],
        name="lay_out",
    )(ids, logits, x, dy)


class Gather:
    names = (
        "0oz", "0or", "0ol", "0lr", "0lz", "0rl", "0rz", "0dz", "0ez",
        "1oz", "1or", "1ol", "1zr", "1zl", "1lr", "1kr", "1rl", "1ql",
    )

    def __init__(self, own, piece, j, z, right, left, pair, ssem, rsem):
        self.own, self.piece, self.ssem, self.rsem = own, piece, ssem, rsem
        self.j, self.z = j, z
        self.jl, self.jr, self.jd = (j + 3) % 4, (j + 1) % 4, (j + 2) % 4
        self.right, self.left, self.pair = right, left, pair
        self.sent = []

    def send(self, name, src, dst, dev):
        i = self.names.index(name)
        copy = pltpu.make_async_remote_copy(
            src, dst, self.ssem.at[i], self.rsem.at[i], device_id=dev, device_id_type=MESH
        )
        copy.start()
        self.sent.append(copy)

    def pass_on(self, name, dev, *where):
        ref = self.piece(*where)
        self.send(name, ref, ref, dev)

    def got(self, name, *where):
        i = self.names.index(name)
        ref = self.piece(*where)
        pltpu.make_async_remote_copy(
            ref, ref, self.ssem.at[i], self.rsem.at[i], device_id=self.pair, device_id_type=MESH
        ).wait_recv()

    def start(self, a):
        for way, dev in (("z", self.pair), ("r", self.right), ("l", self.left)):
            self.send(f"{a}o{way}", self.own(a), self.piece(a, self.j, self.z, None), dev)

    def s2(self):
        self.got("0or", 0, self.jl, self.z, None)
        self.pass_on("0lr", self.right, 0, self.jl, self.z, 0)
        self.pass_on("0lz", self.pair, 0, self.jl, self.z, None)

    def s3(self):
        self.got("0ol", 0, self.jr, self.z, None)
        self.pass_on("0rl", self.left, 0, self.jr, self.z, 1)
        self.pass_on("0rz", self.pair, 0, self.jr, self.z, None)

    def s4(self):
        self.got("1oz", 1, self.j, 1 - self.z, None)
        self.pass_on("1zr", self.right, 1, self.j, 1 - self.z, None)
        self.pass_on("1zl", self.left, 1, self.j, 1 - self.z, None)

    def s5(self):
        self.got("1or", 1, self.jl, self.z, None)
        self.pass_on("1lr", self.right, 1, self.jl, self.z, 0)

    def s6(self):
        self.got("1ol", 1, self.jr, self.z, None)
        self.pass_on("1rl", self.left, 1, self.jr, self.z, 1)

    def s7(self):
        self.got("0lr", 0, self.jd, self.z, 0)
        self.pass_on("0dz", self.pair, 0, self.jd, self.z, 0)

    def s8(self):
        self.got("0rl", 0, self.jd, self.z, 1)
        self.pass_on("0ez", self.pair, 0, self.jd, self.z, 1)

    def s9(self):
        self.got("1zr", 1, self.jl, 1 - self.z, None)
        self.pass_on("1kr", self.right, 1, self.jl, 1 - self.z, 0)

    def s10(self):
        self.got("1zl", 1, self.jr, 1 - self.z, None)
        self.pass_on("1ql", self.left, 1, self.jr, 1 - self.z, 1)

    def end_of_1_d(self):
        self.got("1lr", 1, self.jd, self.z, 0)
        self.got("1rl", 1, self.jd, self.z, 1)

    def end_of_1_e(self):
        self.got("1kr", 1, self.jd, 1 - self.z, 0)
        self.got("1ql", 1, self.jd, 1 - self.z, 1)

    def end_of_0_d(self):
        self.got("0dz", 0, self.jd, 1 - self.z, 0)
        self.got("0ez", 0, self.jd, 1 - self.z, 1)

    def drain(self):
        for copy in self.sent:
            copy.wait_send()


def meet(partners):
    barrier = pltpu.get_barrier_semaphore()
    for dev in partners:
        pl.semaphore_signal(barrier, inc=1, device_id=dev, device_id_type=MESH)
    pl.semaphore_wait(barrier, len(partners))


def others(x, zh):
    for k in range(1, 8):
        dx, dz = k // 2, k % 2
        yield k, ((4 - dx) % 4) * 2 + dz, (x + dx) % 4, (zh + dz) % 2


def sigmoid(v):
    return 1.0 / (1.0 + jnp.exp(-v))


def gate_row(mr, t):
    _, _, x, _, c, _, _ = place()
    parts = []
    for g in range(E // 4):
        at = g * 4 if t == 0 else ((g - x) & 3) * 4
        part = mr[at, t : t + 1, :]
        for i in range(1, 4):
            part = part + mr[at + i, t : t + 1, :]
        parts.append(part if t == 0 else part * mr[c, 3:4, :])
    return jnp.concatenate(parts, axis=1)


def add_into(out, *terms):
    n, rows, _ = out.shape
    step_rows = min(rows, 64)
    for i in range(n):

        def step(k, _):
            r = pl.ds(pl.multiple_of(k * step_rows, step_rows), step_rows)
            total = terms[0][i, r, :].astype(f32)
            for term in terms[1:]:
                total = total + term[i, r, :].astype(f32)
            out[i, r, :] = total.astype(out.dtype)
            return 0

        if rows == step_rows:
            step(0, 0)
        else:
            lax.fori_loop(0, rows // step_rows, step, 0)


class Scatter:
    names = (
        "ar0", "ar1", "al0", "al1", "br0", "br1", "bl0", "bl1", "cr0", "cr1", "cl0", "cl1", "p",
        "zd", "zr", "zl", "z0", "hr", "hl", "ir", "il", "kr", "kl",
    )

    @staticmethod
    def scratch(piece, half):
        V = pltpu.VMEM
        return [
            V((2,) + half, bf16), V((2,) + half, bf16), V((2,) + half, bf16), V((2,) + half, bf16),
            V((2,) + piece, bf16), V((2,) + piece, bf16),
            V(piece, bf16), V(piece, bf16), V(piece, f32),
            V((4,) + piece, bf16), V((4,) + piece, bf16),
            V(half, bf16), V(half, bf16), V(piece, bf16), V(piece, bf16),
            pltpu.SemaphoreType.DMA((23,)), pltpu.SemaphoreType.DMA((23,)),
        ]

    def __init__(self, chunk, cut, j, z, right, left, pair, refs):
        self.chunk, self.cut, self.j, self.z = chunk, cut, j, z
        self.jl, self.jr, self.jd = (j + 3) % 4, (j + 1) % 4, (j + 2) % 4
        self.right, self.left, self.pair = right, left, pair
        (
            self.rl, self.rr, self.tr, self.tl, self.fl, self.fr, self.zs, self.zin, self.own,
            self.hz, self.hw, self.hrl, self.hrr, self.hfl, self.hfr, self.ssem, self.rsem,
        ) = refs
        self.sent = []

    def send(self, name, src, dst, dev):
        i = self.names.index(name)
        copy = pltpu.make_async_remote_copy(
            src, dst, self.ssem.at[i], self.rsem.at[i], device_id=dev, device_id_type=MESH
        )
        copy.start()
        self.sent.append(copy)

    def got(self, name, ref):
        i = self.names.index(name)
        pltpu.make_async_remote_copy(
            ref, ref, self.ssem.at[i], self.rsem.at[i], device_id=self.pair, device_id_type=MESH
        ).wait_recv()

    def start0_far(self):
        for k in (0, 1):
            far = self.chunk(0, self.jd, k)
            self.send(f"ar{k}", self.cut(far, 0), self.rl.at[k], self.right)
            self.send(f"al{k}", self.cut(far, 1), self.rr.at[k], self.left)

    def start0_right(self):
        for k in (0, 1):
            right = self.chunk(0, self.jr, k)
            self.send(f"br{k}", self.cut(right, 1), self.cut(self.fl.at[k], 1), self.right)

    def start0_left(self):
        for k in (0, 1):
            left = self.chunk(0, self.jl, k)
            self.send(f"bl{k}", self.cut(left, 0), self.cut(self.fr.at[k], 0), self.left)

    def start1(self, way):
        j = {"d": self.jd, "r": self.jr, "l": self.jl, "0": self.j}[way]
        self.send("z" + way, self.chunk(1, j, 1 - self.z), self.hz.at[j], self.pair)

    def relay0(self):
        for k in (0, 1):
            self.got(f"ar{k}", self.rl.at[k])
            add_into(self.tr.at[k], self.cut(self.chunk(0, self.jr, k), 0), self.rl.at[k])
            self.send(f"cr{k}", self.tr.at[k], self.cut(self.fl.at[k], 0), self.right)
            self.got(f"al{k}", self.rr.at[k])
            add_into(self.tl.at[k], self.cut(self.chunk(0, self.jl, k), 1), self.rr.at[k])
            self.send(f"cl{k}", self.tl.at[k], self.cut(self.fr.at[k], 1), self.left)

    def pair0(self):
        for k in (0, 1):
            for n, ref, h in (("br", self.fl, 1), ("bl", self.fr, 0), ("cr", self.fl, 0), ("cl", self.fr, 1)):
                self.got(f"{n}{k}", self.cut(ref.at[k], h))
        k = 1 - self.z
        add_into(self.zs, self.chunk(0, self.j, k), self.fl.at[k], self.fr.at[k])
        self.send("p", self.zs, self.zin, self.pair)
        k = self.z
        add_into(self.own, self.chunk(0, self.j, k), self.fl.at[k], self.fr.at[k])

    def end0(self, out):
        self.got("p", self.zin)
        add_into(out, self.own, self.zin)

    def relay1_far(self):
        self.got("zd", self.hz.at[self.jd])
        w = self.hw.at[self.jd]
        add_into(w, self.chunk(1, self.jd, self.z), self.hz.at[self.jd])
        self.send("hr", self.cut(w, 0), self.hrl, self.right)
        self.send("hl", self.cut(w, 1), self.hrr, self.left)

    def relay1_near(self):
        for way, j, h, ref, dev in (
            ("r", self.jr, 1, self.hfl, self.right), ("l", self.jl, 0, self.hfr, self.left)
        ):
            self.got("z" + way, self.hz.at[j])
            w = self.cut(self.hw.at[j], h)
            add_into(w, self.cut(self.chunk(1, j, self.z), h), self.cut(self.hz.at[j], h))
            self.send("i" + way, w, self.cut(ref, h), dev)

    def relay1_last(self):
        for way, j, h, inp, ref, dev in (
            ("r", self.jr, 0, self.hrl, self.hfl, self.right),
            ("l", self.jl, 1, self.hrr, self.hfr, self.left),
        ):
            self.got("h" + way, inp)
            w = self.cut(self.hw.at[j], h)
            add_into(w, self.cut(self.chunk(1, j, self.z), h), self.cut(self.hz.at[j], h), inp)
            self.send("k" + way, w, self.cut(ref, h), dev)

    def end1(self, out):
        self.got("z0", self.hz.at[self.j])
        self.got("ir", self.cut(self.hfl, 1))
        self.got("il", self.cut(self.hfr, 0))
        self.got("kr", self.cut(self.hfl, 0))
        self.got("kl", self.cut(self.hfr, 1))
        add_into(out, self.chunk(1, self.j, self.z), self.hz.at[self.j], self.hfl, self.hfr)

    def drain(self):
        for copy in self.sent:
            copy.wait_send()


HR = ROWS // 2
C_PIECE, C_HALF = (1, HR, W), (1, HR // 2, W)
H_PIECE, H_HALF = (NDP // 2, SLOT, W), (NDP // 4, SLOT, W)


def moe_kernel(
    s1, s2, ms, wg_hbm, wu_hbm, wd_hbm,
    back, backh, gback, mr, gg, gu, gd,
    *refs,
):
    e, d, x, zh, c, y, zl = place()
    c_refs, refs = refs[:17], refs[17:]
    h_refs, refs = refs[:17], refs[17:]
    (
        cold, extra, weights, acc, lhs, rhs, stage, dxc, dxh, gp,
        rc, hs, hin, outh, hp, gall, gsum,
        st_s, st_r, m_s, m_r, sib_s, sib_r, dp_s, dp_r, ex_s, ex_r, xs_s, xs_r, loc, osem,
        g_s, g_r, b_s, b_r, gb_s, gb_r, x_s, x_r, q_s, q_r,
    ) = refs
    wg, wu, wd = weights.at[0], weights.at[1], weights.at[2]
    FFL = weights.shape[1]
    dbar = y * 2 + 1 - zl
    sib = to(expert_at(x, zh, 1 - c), d)
    right, left, pair = to(e, ((y + 1) % 4) * 2 + zl), to(e, ((y + 3) % 4) * 2 + zl), to(e, dbar)
    x_r_dev, x_l_dev = to(expert_at((x + 1) % 4, zh, c), d), to(expert_at((x + 3) % 4, zh, c), d)
    z_p = to(expert_at(x, 1 - zh, c), dbar)
    peers, places, mine = [expert_at(x, zh, 1 - c)], [1 - c], [c]
    row_peers = []
    for rel, seen, x2, zh2 in others(x, zh):
        for c2 in (0, 1):
            peers.append(expert_at(x2, zh2, c2))
            places.append(rel * 2 + c2)
            mine.append(seen * 2 + c)
            d2 = d if rel % 2 == 0 else dbar
            row_peers.append((rel, seen, expert_at(x2, zh2, c2), d2, x2 * 2 + c2))
    dps = [(d + k) % NDP for k in range(1, NDP)]

    own_in = [
        pltpu.make_async_copy(s2.at[:, :, 0:SLOT, :], cold.at[:, :, pl.ds(pl.multiple_of(c * SLOT, SLOT), SLOT), :], loc.at[0]),
        pltpu.make_async_copy(s2.at[:, :, 2 * SLOT :, :], extra.at[:, :, pl.ds(pl.multiple_of(e * SLOT, SLOT), SLOT), :], loc.at[1]),
        pltpu.make_async_copy(ms.at[e], mr.at[c], loc.at[2]),
        pltpu.make_async_copy(wg_hbm, wg, loc.at[3]),
        pltpu.make_async_copy(wu_hbm, wu, loc.at[4]),
        pltpu.make_async_copy(wd_hbm, wd, loc.at[5]),
    ]
    for copy in own_in:
        copy.start()
    meet(
        [to(e2, d) for e2 in peers] + [to(e, d2) for d2 in dps]
        + [to(p[2], dbar) for p in row_peers if p[0] % 2]
    )

    rest = []

    def send(src, dst, ssem, rsem, dev):
        copy = pltpu.make_async_remote_copy(
            src, dst, ssem, rsem, device_id=dev, device_id_type=MESH
        )
        copy.start()
        rest.append(copy)

    def wait(ref, ssem, rsem):
        pltpu.make_async_remote_copy(
            ref, ref, ssem, rsem, device_id=sib, device_id_type=MESH
        ).wait_recv()

    def slots_at(n):
        return pl.ds(pl.multiple_of(n * SLOT, SLOT), SLOT)

    for a in (0, 1):
        for rel, seen, e2, d2, q in row_peers:
            pltpu.make_async_remote_copy(
                s1.at[a, rel % 2, slots_at(q), :], cold.at[a, d2, slots_at(seen * 2 + c), :],
                st_s.at[a], st_r.at[a], device_id=to(e2, d2), device_id_type=MESH,
            ).start()
    meta_peers = row_peers + [(0, 0, expert_at(x, zh, 1 - c), d, 0)]
    for n, (_, seen, e2, d2, _) in enumerate(meta_peers):
        send(ms.at[e2], mr.at[seen * 2 + c], m_s.at[n], m_r.at[seen * 2 + c], to(e2, d2))
    send(s2.at[:, :, SLOT : 2 * SLOT, :], cold.at[:, :, slots_at(c), :], sib_s, sib_r, sib)

    half = (ROWS - LOCAL) // 2

    def dp_piece(a, j, z, h):
        rows = {None: (LOCAL, 2 * half), 0: (LOCAL, half), 1: (LOCAL + half, half)}[h]
        return cold.at[a, j * 2 + z, pl.ds(*rows), :]

    def ex_piece_of(core):
        def piece(a, j, z, h):
            chunks = {None: (0, NDP), 0: (0, NDP // 2), 1: (NDP // 2, NDP // 2)}[h]
            return extra.at[a, pl.ds(*chunks), slots_at(expert_at(j, z, core)), :]
        return piece

    ex_piece, ex_other = ex_piece_of(c), ex_piece_of(1 - c)
    dp = Gather(
        lambda a: dp_piece(a, y, zl, None), dp_piece, y, zl, right, left, pair, dp_s, dp_r
    )
    ex = Gather(
        lambda a: s2.at[a, :, 2 * SLOT :, :], ex_piece, x, zh, x_r_dev, x_l_dev, z_p, ex_s, ex_r
    )
    C = Scatter(
        lambda a, j, z: dxc.at[pl.ds(j * 2 + z, 1), pl.ds(a * HR, HR)],
        lambda ref, h: ref.at[:, pl.ds(h * (HR // 2), HR // 2)],
        y, zl, right, left, pair, c_refs,
    )
    X = Scatter(
        lambda a, j, z: hs.at[j * 2 + z, pl.ds(a * (NDP // 2), NDP // 2)],
        lambda ref, h: ref.at[pl.ds(h * (NDP // 4), NDP // 4)],
        x, zh, x_r_dev, x_l_dev, z_p, h_refs,
    )
    shares = []

    def share(a, j, z, src=None):
        i = len(shares)
        dst = ex_piece(a, j, z, None)
        send(dst if src is None else src, dst, xs_s.at[i], xs_r.at[i], sib)
        shares.append((a, j, z))

    def whole(a):
        ref = cold.at[a, d, pl.ds(LOCAL, ROWS - LOCAL), :]
        return pltpu.make_async_remote_copy(
            ref, ref, st_s.at[a], st_r.at[a], device_id=sib, device_id_type=MESH
        )

    def cols(j):
        return pl.ds(pl.multiple_of(j * W, W), W)

    def forward_x(rows, t, at, n):
        def step(i, _):
            j = at(i)
            xj = rows[0, j]
            acc[t, 0] += nt(wg[:, cols(j)], xj)
            acc[t, 1] += nt(wu[:, cols(j)], xj)
            return 0

        lax.fori_loop(0, n, step, 0)

    def forward_dy(rows, t, at, n):
        def step(i, _):
            j = at(i)
            acc[t, 2] += nt(wd[:, cols(j)], rows[1, j])
            return 0

        lax.fori_loop(0, n, step, 0)

    def between(t):
        gate = gate_row(mr, t)
        pre, up, g = acc[t, 0], acc[t, 1], acc[t, 2]
        s = sigmoid(pre)
        active = pre * s
        hidden = (active * up).astype(bf16).astype(f32)
        gp[0:1, t * ROWS : (t + 1) * ROWS] = jnp.sum(hidden * g, axis=0, keepdims=True)
        gh = g * gate
        d_up = gh * active
        d_pre = gh * up * s * (1.0 + pre * (1.0 - s))
        lhs[t, 0] = d_pre.astype(bf16)
        lhs[t, 1] = d_up.astype(bf16)
        lhs[t, 2] = (hidden * gate).astype(bf16)
        rhs[t, :, 0:FFL] = d_pre.T.astype(bf16)
        rhs[t, :, FFL : 2 * FFL] = d_up.T.astype(bf16)

    def rows_back(t, out, at, n):
        def step(i, _):
            j = at(i)
            r = jnp.dot(rhs[t, :, 0:FFL], wg[:, cols(j)], preferred_element_type=f32)
            r += jnp.dot(rhs[t, :, FFL : 2 * FFL], wu[:, cols(j)], preferred_element_type=f32)
            out[j] = r.astype(bf16)
            return 0

        lax.fori_loop(0, n, step, 0)

    outs = (gg, gu, gd)

    def put(j, slot, i):
        return pltpu.make_async_copy(
            stage.at[slot, i], outs[i].at[:, cols(j)], osem.at[slot, i]
        )

    def weights_back(first, sq, fresh):
        def step(j, sq):
            slot = j % 2
            if not fresh:
                for i in range(3):
                    put(j - 2, slot, i).wait()
            for i in range(3):
                v = jnp.dot(lhs[0, i], cold[i // 2, j], preferred_element_type=f32)
                v += jnp.dot(lhs[1, i], extra[i // 2, j], preferred_element_type=f32)
                stage[slot, i] = v
                sq = sq + jnp.sum((v * v).reshape(-1, 8, W), axis=0)
                put(j, slot, i).start()
            return sq

        return lax.fori_loop(first, first + 2, step, sq)

    acc[...] = jnp.zeros_like(acc)
    for copy in own_in[2:]:
        copy.wait()
    own_in[0].wait()
    wait(cold.at[:, :, slots_at(1 - c), :], sib_s, sib_r)
    whole(0).wait_recv()
    dp.start(0)
    ex.start(0)
    forward_x(cold, 0, lambda i: d, 1)
    whole(1).wait_recv()
    dp.start(1)
    ex.start(1)
    own_in[1].wait()
    share(0, x, zh, s2.at[0, :, 2 * SLOT :, :])
    share(1, x, zh, s2.at[1, :, 2 * SLOT :, :])
    forward_dy(cold, 0, lambda i: d, 1)
    ex.s2()
    ex.s3()
    dp.s2()
    dp.s3()
    ex.s4()
    ex.s5()
    ex.s6()
    for a, j, z in ((0, ex.jl, zh), (0, ex.jr, zh), (1, x, 1 - zh), (1, ex.jl, zh), (1, ex.jr, zh)):
        share(a, j, z)
    forward_x(cold, 0, lambda i: ((y + 1 + 2 * i) % 4) * 2 + zl, 2)
    ex.s7()
    ex.s8()
    share(0, ex.jd, zh)
    dp.s4()
    dp.s5()
    dp.s6()
    forward_dy(cold, 0, lambda i: ((y + 1 + 2 * i) % 4) * 2 + zl, 2)
    forward_dy(cold, 0, lambda i: dbar, 1)
    ex.s9()
    ex.s10()
    share(1, ex.jl, 1 - zh)
    share(1, ex.jr, 1 - zh)
    dp.s7()
    dp.s8()
    dp.got("0oz", 0, y, 1 - zl, None)
    forward_x(cold, 0, lambda i: i * (dp.jd * 2 + zl) + (1 - i) * dbar, 2)
    ex.got("0oz", 0, x, 1 - zh, None)
    share(0, x, 1 - zh)
    ex.got("0lz", 0, ex.jl, 1 - zh, None)
    share(0, ex.jl, 1 - zh)
    ex.got("0rz", 0, ex.jr, 1 - zh, None)
    share(0, ex.jr, 1 - zh)
    ex.end_of_1_d()
    share(1, ex.jd, zh)
    ex.end_of_1_e()
    share(1, ex.jd, 1 - zh)
    ex.end_of_0_d()
    share(0, ex.jd, 1 - zh)
    dp.s9()
    dp.s10()
    forward_dy(cold, 0, lambda i: ((y + 1 + 2 * i) % 4) * 2 + 1 - zl, 2)
    for i in [1 - c] + list(range(2, E)):
        wait(mr.at[i], m_s.at[0], m_r.at[i])
    for i, where in enumerate(shares):
        wait(ex_other(*where, None), xs_s.at[i], xs_r.at[i])
    forward_x(extra, 1, lambda i: i, NDP)
    forward_dy(extra, 1, lambda i: i, NDP)
    between(1)
    rows_back(1, dxh, lambda i: i, NDP)
    far = [X.jd * 2, X.jd * 2 + 1, X.jr * 2, X.jl * 2, X.jr * 2 + 1, X.jl * 2 + 1, x * 2, x * 2 + 1]

    def h_rows(chip, core):
        return slots_at(chip * 2 + core)

    for i, chip in enumerate(far):
        send(dxh.at[:, h_rows(chip, 1 - c)], hin.at[chip], x_s.at[i], x_r.at[i], sib)
    dp.end_of_1_d()
    forward_dy(cold, 0, lambda i: dp.jd * 2 + zl, 1)
    for i, chip in enumerate(far):
        wait(hin.at[chip], x_s.at[i], x_r.at[i])
        add_into(hs.at[chip], dxh.at[:, h_rows(chip, c)], hin.at[chip])
        if i == 1:
            X.start0_far()
        if i == 5:
            X.start0_right()
            X.start0_left()
    for way in ("d", "r", "l", "0"):
        X.start1(way)
    dp.got("0lz", 0, dp.jl, 1 - zl, None)
    dp.got("0rz", 0, dp.jr, 1 - zl, None)
    forward_x(cold, 0, lambda i: ((y + 1 + 2 * i) % 4) * 2 + 1 - zl, 2)
    dp.end_of_1_e()
    forward_dy(cold, 0, lambda i: dp.jd * 2 + 1 - zl, 1)
    dp.end_of_0_d()
    forward_x(cold, 0, lambda i: dp.jd * 2 + 1 - zl, 1)
    between(0)

    rows_back(0, dxc, lambda i: C.jd * 2 + i, 2)
    C.start0_far()
    C.start1("d")
    rows_back(0, dxc, lambda i: C.jr * 2 + i, 2)
    C.start0_right()
    C.start1("r")
    rows_back(0, dxc, lambda i: C.jl * 2 + i, 2)
    C.start0_left()
    C.start1("l")
    rows_back(0, dxc, lambda i: y * 2 + i, 2)
    C.start1("0")
    X.relay0()
    X.relay1_far()
    X.relay1_near()
    sq = weights_back(0, jnp.zeros((8, W), f32), True)
    C.relay0()
    C.relay1_far()
    X.relay1_last()
    X.pair0()
    sq = weights_back(2, sq, False)
    C.relay1_near()
    sq = weights_back(4, sq, False)
    C.relay1_last()
    sq = weights_back(6, sq, False)
    total = jnp.sum(jnp.sum(sq, axis=0, keepdims=True), axis=1, keepdims=True)
    gp[0:1, 2 * ROWS :] = jnp.broadcast_to(total, (1, GW - 2 * ROWS))
    for k, d2 in enumerate(dps):
        send(gp, gall.at[d], g_s.at[k], g_r.at[k], to(e, d2))
    gall[d] = gp[...]
    C.pair0()
    X.end1(outh.at[pl.ds(NDP // 2, NDP // 2)])
    X.end0(outh.at[pl.ds(0, NDP // 2)])
    for k, d2 in enumerate(dps):
        send(outh.at[d2], hp.at[d], q_s.at[k], q_r.at[k], to(e, d2))
    hp[d] = outh[d]

    def give(a):
        for n, e2 in enumerate(peers):
            if (n >= 7) == (a == 1):
                send(
                    rc.at[0, slots_at(places[n]), :],
                    back.at[e], b_s.at[n], b_r.at[mine[n]], to(e2, d),
                )

    C.end1(rc.at[:, pl.ds(HR, HR)])
    give(1)
    for k in range(NDP - 1):
        wait(gall.at[(d + NDP - 1 - k) % NDP], g_s.at[k], g_r.at[k])
    total = gall[0]
    for k in range(1, NDP):
        total = total + gall[k]
    gsum[...] = total
    gback[e] = total
    for n, e2 in enumerate(peers):
        send(gsum, gback.at[e], gb_s.at[n], gb_r.at[mine[n]], to(e2, d))
    C.end0(rc.at[:, pl.ds(0, HR)])
    give(0)
    back[e] = rc[0, slots_at(c), :]
    for k in range(NDP - 1):
        wait(hp.at[(d + NDP - 1 - k) % NDP], q_s.at[k], q_r.at[k])
    total = hp[0].astype(f32)
    for k in range(1, NDP):
        total = total + hp[k].astype(f32)
    backh[...] = total.astype(bf16)

    for i in [1 - c] + list(range(2, E)):
        wait(back.at[0], b_s.at[0], b_r.at[i])
        wait(gback.at[0], gb_s.at[0], gb_r.at[i])
    for j in (NDP - 2, NDP - 1):
        for i in range(3):
            put(j, j % 2, i).wait()
    whole(0).wait_send()
    whole(1).wait_send()
    for copy in rest:
        copy.wait_send()
    dp.drain()
    ex.drain()
    C.drain()
    X.drain()


def moe(s1, s2, m, wg, wu, wd):
    FFL, width = wg.shape
    D = pltpu.SemaphoreType.DMA
    V = pltpu.VMEM
    return pl.pallas_call(
        moe_kernel,
        in_specs=[ANY] * 6,
        out_specs=[VM] * 4 + [ANY] * 3,
        out_shape=[
            jax.ShapeDtypeStruct((E, SLOT, W), bf16),
            jax.ShapeDtypeStruct((SLOT, W), bf16),
            jax.ShapeDtypeStruct((E, 1, GW), f32),
            jax.ShapeDtypeStruct((E, 8, 128), f32),
        ]
        + [jax.ShapeDtypeStruct((FFL, width), f32)] * 3,
        scratch_shapes=Scatter.scratch(C_PIECE, C_HALF)
        + Scatter.scratch(H_PIECE, H_HALF)
        + [
            V((2, NDP, ROWS, W), bf16), V((2, NDP, ROWS, W), bf16),
            V((3, FFL, width), bf16),
            V((2, 3, FFL, ROWS), f32), V((2, 3, FFL, ROWS), bf16), V((2, ROWS, 2 * FFL), bf16),
            V((2, 3, FFL, W), f32),
            V((NDP, ROWS, W), bf16), V((NDP, ROWS, W), bf16), V((1, GW), f32),
            V((1, ROWS, W), bf16),
            V((NDP, NDP, SLOT, W), bf16), V((NDP, NDP, SLOT, W), bf16),
            V((NDP, SLOT, W), bf16), V((NDP, SLOT, W), bf16),
            V((NDP, 1, GW), f32), V((1, GW), f32),
            D((2,)), D((2,)), D((15,)), D((16,)), D, D,
            D((18,)), D((18,)), D((18,)), D((18,)), D((16,)), D((16,)), D((6,)), D((2, 3)),
            D((7,)), D((7,)), D((15,)), D((16,)), D((15,)), D((16,)),
            D((8,)), D((8,)), D((7,)), D((7,)),
        ],
        compiler_params=pltpu.CompilerParams(
            collective_id=1, has_side_effects=True, vmem_limit_bytes=62 * 1024 * 1024
        ),
        name="moe",
    )(s1, s2, m, wg, wu, wd)


def finish_kernel(ids_ref, logits_ref, back, backh, gback, mr, rows_ref, gl_ref, norm_ref):
    e, _, x, zh, c, _, _ = place()
    ids = ids_ref[...]
    onehot, rank = row_facts(ids, E)
    probs = soft(logits_ref[...])
    n = ids.shape[1]
    first = rank < SLOT
    slot = lax.broadcasted_iota(jnp.int32, (ROWS, n), 0)
    pick = (slot == jnp.where(first, ids * SLOT + rank, -1)).astype(f32).astype(bf16)
    slot = lax.broadcasted_iota(jnp.int32, (SLOT, n), 0)
    pickh = (slot == rank - SLOT).astype(f32).astype(bf16)
    got = tn(pick, back[...].reshape(ROWS, W)) + tn(pickh, backh[...])
    rows_ref[...] = got.astype(bf16)
    rel = seen_from(ids, x, zh, c)
    lane = jnp.where(first, rel * SLOT + rank, ROWS + e * SLOT + rank - SLOT)
    slot = lax.broadcasted_iota(jnp.int32, (2 * ROWS, n), 0)
    here = (slot == lane).astype(f32).astype(bf16)
    found = jnp.dot(gback[:, 0, 0 : 2 * ROWS].astype(bf16), here, preferred_element_type=f32)
    dgate = jnp.sum(onehot * found, axis=0, keepdims=True)
    count = jnp.sum(mr[...], axis=0)[2:3, :]
    across = lax.broadcasted_iota(jnp.int32, (E, 128), 0)
    diag = across == lax.broadcasted_iota(jnp.int32, (E, 128), 1)
    column = jnp.sum(jnp.where(diag, jnp.broadcast_to(count, (E, 128)), 0.0), axis=1, keepdims=True)
    pulls = onehot * dgate + 1.0 * E * (column / (E * n))
    gl_ref[...] = probs * (pulls - jnp.sum(probs * pulls, axis=0, keepdims=True))
    norm_ref[...] = jnp.sqrt(jnp.sum(gback[:, 0, 2 * ROWS : 2 * ROWS + 128], axis=0, keepdims=True))


def finish(ids, logits, back, backh, gback, mr):
    n = ids.shape[1]
    return pl.pallas_call(
        finish_kernel,
        in_specs=[VM] * 6,
        out_specs=[VM] * 3,
        out_shape=[
            jax.ShapeDtypeStruct((n, W), bf16),
            jax.ShapeDtypeStruct((E, n), f32),
            jax.ShapeDtypeStruct((1, 128), f32),
        ],
        name="finish",
    )(ids, logits, back, backh, gback, mr)


def local(rows_x, rows_dy, router_logits, expert_of, w_gate, w_up, w_down):
    ids = expert_of.reshape(1, -1)
    logits = router_logits.T
    s1, s2, m = lay_out(ids, logits, rows_x, rows_dy)
    back, backh, gback, mr, gg, gu, gd = moe(s1, s2, m, w_gate[0], w_up[0], w_down[0])
    grad_rows, grad_logits, norm = finish(ids, logits, back, backh, gback, mr)
    return grad_rows, grad_logits.T, gg[None], gu[None], gd[None], norm[0, 0]


def solution(mesh):
    rows = P("expert", None)
    weights = P("expert", "dp", None)
    return jax.shard_map(
        local,
        mesh=mesh,
        in_specs=(rows, rows, rows, rows, weights, weights, weights),
        out_specs=(P("expert", "dp"), rows, weights, weights, weights, P()),
        check_vma=False,
    )
```

```python
import jax
import jax.numpy as jnp
from jax import lax
from jax.experimental import pallas as pl
from jax.experimental.pallas import tpu as pltpu
from jax.sharding import PartitionSpec as P

f32 = jnp.float32
bf16 = jnp.bfloat16
MESH = pl.DeviceIdType.MESH
ANY = pl.BlockSpec(memory_space=pl.ANY)
VM = pl.BlockSpec(memory_space=pltpu.VMEM)
SM = pl.BlockSpec(memory_space=pltpu.SMEM)

E = 16
NDP = 8
SLOT = 32
W = 512
ROWS = E * SLOT
LOCAL = 2 * SLOT
GW = 1280


def place():
    e = lax.axis_index("expert")
    d = lax.axis_index("dp")
    return e, d, e // 4, (e // 2) % 2, e % 2, d // 2, d % 2


def expert_at(x, zh, c):
    return (x * 2 + zh) * 2 + c


def to(e, d):
    return {"expert": e, "dp": d}


def row_facts(ids, experts):
    rows = ids.shape[1]
    onehot = (lax.broadcasted_iota(jnp.int32, (experts, rows), 0) == ids).astype(f32)
    before = lax.broadcasted_iota(jnp.int32, (rows, rows), 0) < lax.broadcasted_iota(
        jnp.int32, (rows, rows), 1
    )
    earlier = jnp.dot(onehot.astype(bf16), before.astype(bf16), preferred_element_type=f32)
    rank = jnp.sum(onehot * earlier, axis=0, keepdims=True).astype(jnp.int32)
    return onehot, rank


def soft(logits):
    top = jnp.max(logits, axis=0, keepdims=True)
    ex = jnp.exp(logits - top)
    return ex / jnp.sum(ex, axis=0, keepdims=True)


def nt(a, b):
    return lax.dot_general(a, b, (((1,), (1,)), ((), ())), preferred_element_type=f32)


def tn(a, b):
    return lax.dot_general(a, b, (((0,), (0,)), ((), ())), preferred_element_type=f32)


def seen_from(ids, x, zh, c):
    dx = (x - (ids >> 2)) & 3
    return ((dx ^ (dx >> 1)) + 4 * (zh ^ ((ids >> 1) & 1))) * 2 + c


def slots_kernel(ids_ref, logits_ref, x_ref, dy_ref, s1_ref, s2_ref, s3_ref, m_ref):
    e, d, x, zh, c, y, zl = place()
    ids = ids_ref[...]
    onehot, rank = row_facts(ids, E)
    rows = ids.shape[1]
    none = -1

    def perm(slots, target):
        slot = lax.broadcasted_iota(jnp.int32, (slots, rows), 0)
        return (slot == target).astype(f32).astype(bf16)

    far = (zh ^ ((ids >> 1) & 1)) == 1
    first = rank < SLOT
    chip = ((ids >> 2) * 2 + (ids & 1)) * SLOT + rank
    for g, ours in ((0, jnp.logical_not(far)), (1, far)):
        p = perm(ROWS // 2, jnp.where(first & ours, chip, none))
        at = pl.ds(pl.multiple_of((d if g == 0 else y * 2 + 1 - zl) * W, W), W)
        s1_ref[0, g] = jnp.dot(p, x_ref[:, at], preferred_element_type=f32).astype(bf16)
        s1_ref[1, g] = jnp.dot(p, dy_ref[:, at], preferred_element_type=f32).astype(bf16)
    home = jnp.where(ids == e, rank, jnp.where(ids == e + 1 - 2 * c, SLOT + rank, none))
    dx = ((ids >> 2) - x) & 3
    side = (3 + (dx & 2) + (ids & 1)) * SLOT + rank
    home = jnp.where(((dx & 1) == 1) & jnp.logical_not(far), side, home)
    p = perm(7 * SLOT, jnp.where(first, home, SLOT + rank))
    for j in range(NDP):
        at = slice(j * W, (j + 1) * W)
        got = jnp.dot(p, x_ref[:, at], preferred_element_type=f32).astype(bf16)
        s2_ref[0, j] = got[: 3 * SLOT]
        s3_ref[j] = got[3 * SLOT :]
        s2_ref[1, j] = jnp.dot(p[: 3 * SLOT], dy_ref[:, at], preferred_element_type=f32).astype(bf16)

    gate = jnp.sum(soft(logits_ref[...]) * onehot, axis=0, keepdims=True).astype(bf16).astype(f32)
    lane = lax.broadcasted_iota(jnp.int32, (128, rows), 0)
    spot = (seen_from(ids, x, zh, c) & 3) * SLOT + rank
    cold = (onehot * gate * first.astype(f32)).astype(bf16)
    cold = nt(cold, (lane == spot).astype(f32).astype(bf16))
    gate8 = jnp.broadcast_to(gate, (8, rows)).astype(bf16)
    spot = jnp.where(first, none, (e & 3) * SLOT + rank - SLOT)
    hot = nt(gate8, (lane == spot).astype(f32).astype(bf16))
    count = nt(jnp.ones((8, rows), bf16), (lane == ids).astype(f32).astype(bf16))
    line = lax.broadcasted_iota(jnp.int32, (8, 128), 0)
    for k in range(E):
        mine = jnp.broadcast_to(cold[k : k + 1, :], (8, 128))
        busy = (jnp.sum(onehot[k : k + 1, :], axis=1, keepdims=True) > SLOT).astype(f32)
        rest = jnp.where(line == 2, count, jnp.broadcast_to(busy, (8, 128)))
        m_ref[k] = jnp.where(line == 0, mine, jnp.where(line == 1, hot, rest))


def lay_out(ids, logits, x, dy):
    return pl.pallas_call(
        slots_kernel,
        in_specs=[VM] * 4,
        out_specs=[VM] * 4,
        out_shape=[
            jax.ShapeDtypeStruct((2, 2, ROWS // 2, W), bf16),
            jax.ShapeDtypeStruct((2, NDP, 3 * SLOT, W), bf16),
            jax.ShapeDtypeStruct((NDP, 4 * SLOT, W), bf16),
            jax.ShapeDtypeStruct((E, 8, 128), f32),
        ],
        name="lay_out",
    )(ids, logits, x, dy)


class Gather:
    names = (
        "0oz", "0or", "0ol", "0lr", "0lz", "0rl", "0rz", "0dz", "0ez",
        "1oz", "1or", "1ol", "1zr", "1zl", "1lr", "1kr", "1rl", "1ql",
    )

    def __init__(self, own, piece, j, z, right, left, pair, ssem, rsem):
        self.own, self.piece, self.ssem, self.rsem = own, piece, ssem, rsem
        self.j, self.z = j, z
        self.jl, self.jr, self.jd = (j + 3) % 4, (j + 1) % 4, (j + 2) % 4
        self.right, self.left, self.pair = right, left, pair
        self.sent = []

    def send(self, name, src, dst, dev):
        i = self.names.index(name)
        copy = pltpu.make_async_remote_copy(
            src, dst, self.ssem.at[i], self.rsem.at[i], device_id=dev, device_id_type=MESH
        )
        copy.start()
        self.sent.append(copy)

    def pass_on(self, name, dev, *where):
        ref = self.piece(*where)
        self.send(name, ref, ref, dev)

    def got(self, name, *where):
        i = self.names.index(name)
        ref = self.piece(*where)
        pltpu.make_async_remote_copy(
            ref, ref, self.ssem.at[i], self.rsem.at[i], device_id=self.pair, device_id_type=MESH
        ).wait_recv()

    def start(self, a):
        for way, dev in (("z", self.pair), ("r", self.right), ("l", self.left)):
            self.send(f"{a}o{way}", self.own(a), self.piece(a, self.j, self.z, None), dev)

    def s2(self):
        self.got("0or", 0, self.jl, self.z, None)
        self.pass_on("0lr", self.right, 0, self.jl, self.z, 0)
        self.pass_on("0lz", self.pair, 0, self.jl, self.z, None)

    def s3(self):
        self.got("0ol", 0, self.jr, self.z, None)
        self.pass_on("0rl", self.left, 0, self.jr, self.z, 1)
        self.pass_on("0rz", self.pair, 0, self.jr, self.z, None)

    def s4(self):
        self.got("1oz", 1, self.j, 1 - self.z, None)
        self.pass_on("1zr", self.right, 1, self.j, 1 - self.z, None)
        self.pass_on("1zl", self.left, 1, self.j, 1 - self.z, None)

    def s5(self):
        self.got("1or", 1, self.jl, self.z, None)
        self.pass_on("1lr", self.right, 1, self.jl, self.z, 0)

    def s6(self):
        self.got("1ol", 1, self.jr, self.z, None)
        self.pass_on("1rl", self.left, 1, self.jr, self.z, 1)

    def s7(self):
        self.got("0lr", 0, self.jd, self.z, 0)
        self.pass_on("0dz", self.pair, 0, self.jd, self.z, 0)

    def s8(self):
        self.got("0rl", 0, self.jd, self.z, 1)
        self.pass_on("0ez", self.pair, 0, self.jd, self.z, 1)

    def s9(self):
        self.got("1zr", 1, self.jl, 1 - self.z, None)
        self.pass_on("1kr", self.right, 1, self.jl, 1 - self.z, 0)

    def s10(self):
        self.got("1zl", 1, self.jr, 1 - self.z, None)
        self.pass_on("1ql", self.left, 1, self.jr, 1 - self.z, 1)

    def end_of_1_d(self):
        self.got("1lr", 1, self.jd, self.z, 0)
        self.got("1rl", 1, self.jd, self.z, 1)

    def end_of_1_e(self):
        self.got("1kr", 1, self.jd, 1 - self.z, 0)
        self.got("1ql", 1, self.jd, 1 - self.z, 1)

    def end_of_0_d(self):
        self.got("0dz", 0, self.jd, 1 - self.z, 0)
        self.got("0ez", 0, self.jd, 1 - self.z, 1)

    def drain(self):
        for copy in self.sent:
            copy.wait_send()


def meet(partners):
    barrier = pltpu.get_barrier_semaphore()
    for dev in partners:
        pl.semaphore_signal(barrier, inc=1, device_id=dev, device_id_type=MESH)
    pl.semaphore_wait(barrier, len(partners))


def others(x, zh):
    order = (0, 1, 3, 2)
    for k in range(1, 8):
        dx, dz = k // 2, k % 2
        yield order[dx] + 4 * dz, order[(4 - dx) % 4] + 4 * dz, (x + dx) % 4, (zh + dz) % 2


def sigmoid(v):
    return 1.0 / (1.0 + jnp.exp(-v))


def gate_row(mr, t):
    _, _, x, _, c, _, _ = place()
    parts = []
    for g in range(E // 4):
        dx = (g + 4 - x) % 4
        at = g * 4 if t == 0 else (dx + dx // 2 - 2 * (dx // 3)) * 2
        part = mr[at, t : t + 1, :]
        for i in (1, 2, 3) if t == 0 else (1, 8, 9):
            part = part + mr[at + i, t : t + 1, :]
        parts.append(part if t == 0 else part * mr[c, 3:4, :])
    return jnp.concatenate(parts, axis=1)


def add_into(out, *terms):
    n, rows, _ = out.shape
    step_rows = min(rows, 64)
    for i in range(n):

        def step(k, _):
            r = pl.ds(pl.multiple_of(k * step_rows, step_rows), step_rows)
            total = terms[0][i, r, :].astype(f32)
            for term in terms[1:]:
                total = total + term[i, r, :].astype(f32)
            out[i, r, :] = total.astype(out.dtype)
            return 0

        if rows == step_rows:
            step(0, 0)
        else:
            lax.fori_loop(0, rows // step_rows, step, 0)


class Scatter:
    names = (
        "ar0", "ar1", "al0", "al1", "br0", "br1", "bl0", "bl1", "cr0", "cr1", "cl0", "cl1", "p",
        "zd", "zr", "zl", "z0", "hr", "hl", "ir", "il", "kr", "kl",
    )

    @staticmethod
    def scratch(piece, half):
        V = pltpu.VMEM
        return [
            V((2,) + half, bf16), V((2,) + half, bf16), V((2,) + half, bf16), V((2,) + half, bf16),
            V((2,) + piece, bf16), V((2,) + piece, bf16),
            V(piece, bf16), V(piece, bf16), V(piece, f32),
            V((4,) + piece, bf16), V((4,) + piece, bf16),
            V(half, bf16), V(half, bf16), V(piece, bf16), V(piece, bf16),
            pltpu.SemaphoreType.DMA((23,)), pltpu.SemaphoreType.DMA((23,)),
        ]

    def __init__(self, chunk, cut, j, z, right, left, pair, refs):
        self.chunk, self.cut, self.j, self.z = chunk, cut, j, z
        self.jl, self.jr, self.jd = (j + 3) % 4, (j + 1) % 4, (j + 2) % 4
        self.right, self.left, self.pair = right, left, pair
        (
            self.rl, self.rr, self.tr, self.tl, self.fl, self.fr, self.zs, self.zin, self.own,
            self.hz, self.hw, self.hrl, self.hrr, self.hfl, self.hfr, self.ssem, self.rsem,
        ) = refs
        self.sent = []

    def send(self, name, src, dst, dev):
        i = self.names.index(name)
        copy = pltpu.make_async_remote_copy(
            src, dst, self.ssem.at[i], self.rsem.at[i], device_id=dev, device_id_type=MESH
        )
        copy.start()
        self.sent.append(copy)

    def got(self, name, ref):
        i = self.names.index(name)
        pltpu.make_async_remote_copy(
            ref, ref, self.ssem.at[i], self.rsem.at[i], device_id=self.pair, device_id_type=MESH
        ).wait_recv()

    def start0_far(self):
        for k in (0, 1):
            far = self.chunk(0, self.jd, k)
            self.send(f"ar{k}", self.cut(far, 0), self.rl.at[k], self.right)
            self.send(f"al{k}", self.cut(far, 1), self.rr.at[k], self.left)

    def start0_right(self):
        for k in (0, 1):
            right = self.chunk(0, self.jr, k)
            self.send(f"br{k}", self.cut(right, 1), self.cut(self.fl.at[k], 1), self.right)

    def start0_left(self):
        for k in (0, 1):
            left = self.chunk(0, self.jl, k)
            self.send(f"bl{k}", self.cut(left, 0), self.cut(self.fr.at[k], 0), self.left)

    def start1(self, way):
        j = {"d": self.jd, "r": self.jr, "l": self.jl, "0": self.j}[way]
        self.send("z" + way, self.chunk(1, j, 1 - self.z), self.hz.at[j], self.pair)

    def relay0(self):
        for k in (0, 1):
            self.got(f"ar{k}", self.rl.at[k])
            add_into(self.tr.at[k], self.cut(self.chunk(0, self.jr, k), 0), self.rl.at[k])
            self.send(f"cr{k}", self.tr.at[k], self.cut(self.fl.at[k], 0), self.right)
            self.got(f"al{k}", self.rr.at[k])
            add_into(self.tl.at[k], self.cut(self.chunk(0, self.jl, k), 1), self.rr.at[k])
            self.send(f"cl{k}", self.tl.at[k], self.cut(self.fr.at[k], 1), self.left)

    def pair0(self):
        for k in (0, 1):
            for n, ref, h in (("br", self.fl, 1), ("bl", self.fr, 0), ("cr", self.fl, 0), ("cl", self.fr, 1)):
                self.got(f"{n}{k}", self.cut(ref.at[k], h))
        k = 1 - self.z
        add_into(self.zs, self.chunk(0, self.j, k), self.fl.at[k], self.fr.at[k])
        self.send("p", self.zs, self.zin, self.pair)
        k = self.z
        add_into(self.own, self.chunk(0, self.j, k), self.fl.at[k], self.fr.at[k])

    def end0(self, out):
        self.got("p", self.zin)
        add_into(out, self.own, self.zin)

    def relay1_far(self):
        self.got("zd", self.hz.at[self.jd])
        w = self.hw.at[self.jd]
        add_into(w, self.chunk(1, self.jd, self.z), self.hz.at[self.jd])
        self.send("hr", self.cut(w, 0), self.hrl, self.right)
        self.send("hl", self.cut(w, 1), self.hrr, self.left)

    def relay1_near(self):
        for way, j, h, ref, dev in (
            ("r", self.jr, 1, self.hfl, self.right), ("l", self.jl, 0, self.hfr, self.left)
        ):
            self.got("z" + way, self.hz.at[j])
            w = self.cut(self.hw.at[j], h)
            add_into(w, self.cut(self.chunk(1, j, self.z), h), self.cut(self.hz.at[j], h))
            self.send("i" + way, w, self.cut(ref, h), dev)

    def relay1_last(self):
        for way, j, h, inp, ref, dev in (
            ("r", self.jr, 0, self.hrl, self.hfl, self.right),
            ("l", self.jl, 1, self.hrr, self.hfr, self.left),
        ):
            self.got("h" + way, inp)
            w = self.cut(self.hw.at[j], h)
            add_into(w, self.cut(self.chunk(1, j, self.z), h), self.cut(self.hz.at[j], h), inp)
            self.send("k" + way, w, self.cut(ref, h), dev)

    def end1(self, out):
        self.got("z0", self.hz.at[self.j])
        self.got("ir", self.cut(self.hfl, 1))
        self.got("il", self.cut(self.hfr, 0))
        self.got("kr", self.cut(self.hfl, 0))
        self.got("kl", self.cut(self.hfr, 1))
        add_into(out, self.chunk(1, self.j, self.z), self.hz.at[self.j], self.hfl, self.hfr)

    def drain(self):
        for copy in self.sent:
            copy.wait_send()


HR = ROWS // 2
C_PIECE, C_HALF = (1, HR, W), (1, HR // 2, W)
H_PIECE, H_HALF = (NDP // 2, SLOT, W), (NDP // 4, SLOT, W)


def moe_kernel(
    s1, s2, s3, ms, wg_hbm, wu_hbm, wd_hbm,
    back, backh, gback, mr, gg, gu, gd,
    *refs,
):
    e, d, x, zh, c, y, zl = place()
    c_refs, refs = refs[:17], refs[17:]
    h_refs, refs = refs[:17], refs[17:]
    (
        cold, extra, weights, acc, lhs, rhs, stage, dxc, dxh, gp,
        rc, hs, hin, outh, hp, gall, gsum,
        st_s, st_r, sd_s, sd_r, m_s, m_r, sib_s, sib_r, dp_s, dp_r, ex_s, ex_r, xs_s, xs_r, loc, osem,
        g_s, g_r, b_s, b_r, gb_s, gb_r, x_s, x_r, q_s, q_r,
    ) = refs
    wg, wu, wd = weights.at[0], weights.at[1], weights.at[2]
    FFL = weights.shape[1]
    dbar = y * 2 + 1 - zl
    sib = to(expert_at(x, zh, 1 - c), d)
    right, left, pair = to(e, ((y + 1) % 4) * 2 + zl), to(e, ((y + 3) % 4) * 2 + zl), to(e, dbar)
    x_r_dev, x_l_dev = to(expert_at((x + 1) % 4, zh, c), d), to(expert_at((x + 3) % 4, zh, c), d)
    z_p = to(expert_at(x, 1 - zh, c), dbar)
    peers, places, mine, parts = [expert_at(x, zh, 1 - c)], [1 - c], [c], [0]
    row_peers = []
    for here, seen, x2, zh2 in others(x, zh):
        for c2 in (0, 1):
            peers.append(expert_at(x2, zh2, c2))
            places.append(here * 2 + c2)
            mine.append(seen * 2 + c)
            parts.append(here // 4)
            d2 = d if here < 4 else dbar
            row_peers.append((here, seen, expert_at(x2, zh2, c2), d2, x2 * 2 + c2))
    dps = [(d + k) % NDP for k in range(1, NDP)]

    own_in = [
        pltpu.make_async_copy(s2.at[:, :, 0:SLOT, :], cold.at[:, :, pl.ds(pl.multiple_of(c * SLOT, SLOT), SLOT), :], loc.at[0]),
        pltpu.make_async_copy(s2.at[:, :, 2 * SLOT :, :], extra.at[:, :, pl.ds(pl.multiple_of(e * SLOT, SLOT), SLOT), :], loc.at[1]),
        pltpu.make_async_copy(ms.at[e], mr.at[c], loc.at[2]),
        pltpu.make_async_copy(wg_hbm, wg, loc.at[3]),
        pltpu.make_async_copy(wu_hbm, wu, loc.at[4]),
        pltpu.make_async_copy(wd_hbm, wd, loc.at[5]),
    ]
    for copy in own_in:
        copy.start()
    meet(
        [to(e2, d) for e2 in peers] + [to(e, d2) for d2 in dps]
        + [to(p[2], dbar) for p in row_peers if p[0] >= 4]
    )

    rest = []

    def send(src, dst, ssem, rsem, dev):
        copy = pltpu.make_async_remote_copy(
            src, dst, ssem, rsem, device_id=dev, device_id_type=MESH
        )
        copy.start()
        rest.append(copy)

    def wait(ref, ssem, rsem):
        pltpu.make_async_remote_copy(
            ref, ref, ssem, rsem, device_id=sib, device_id_type=MESH
        ).wait_recv()

    def slots_at(n):
        return pl.ds(pl.multiple_of(n * SLOT, SLOT), SLOT)

    for a in (0, 1):
        for here, seen, e2, d2, q in row_peers:
            if a == 0 and here in (1, 2):
                continue
            pltpu.make_async_remote_copy(
                s1.at[a, here // 4, slots_at(q), :], cold.at[a, d2, slots_at(seen * 2 + c), :],
                st_s.at[a], st_r.at[a], device_id=to(e2, d2), device_id_type=MESH,
            ).start()
    meta_peers = row_peers + [(0, 0, expert_at(x, zh, 1 - c), d, 0)]
    for n, (_, seen, e2, d2, _) in enumerate(meta_peers):
        send(ms.at[e2], mr.at[seen * 2 + c], m_s.at[n], m_r.at[seen * 2 + c], to(e2, d2))
    send(s2.at[:, :, SLOT : 2 * SLOT, :], cold.at[:, :, slots_at(c), :], sib_s, sib_r, sib)

    def dp_piece(a, j, z, h):
        start = (3 if a == 0 else 1) * 2 * SLOT
        half = (ROWS - start) // 2
        rows = {None: (start, 2 * half), 0: (start, half), 1: (start + half, half)}[h]
        return cold.at[a, j * 2 + z, pl.ds(*rows), :]

    def ex_piece_of(core):
        def piece(a, j, z, h):
            chunks = {None: (0, NDP), 0: (0, NDP // 2), 1: (NDP // 2, NDP // 2)}[h]
            return extra.at[a, pl.ds(*chunks), slots_at(expert_at(j, z, core)), :]
        return piece

    ex_piece, ex_other = ex_piece_of(c), ex_piece_of(1 - c)
    dp = Gather(
        lambda a: dp_piece(a, y, zl, None), dp_piece, y, zl, right, left, pair, dp_s, dp_r
    )
    ex = Gather(
        lambda a: s2.at[a, :, 2 * SLOT :, :], ex_piece, x, zh, x_r_dev, x_l_dev, z_p, ex_s, ex_r
    )
    C = Scatter(
        lambda a, j, z: dxc.at[pl.ds(j * 2 + z, 1), pl.ds(a * HR, HR)],
        lambda ref, h: ref.at[:, pl.ds(h * (HR // 2), HR // 2)],
        y, zl, right, left, pair, c_refs,
    )
    X = Scatter(
        lambda a, j, z: hs.at[j * 2 + z, pl.ds(a * (NDP // 2), NDP // 2)],
        lambda ref, h: ref.at[pl.ds(h * (NDP // 4), NDP // 4)],
        x, zh, x_r_dev, x_l_dev, z_p, h_refs,
    )
    shares = []

    def share(a, j, z, src=None):
        i = len(shares)
        dst = ex_piece(a, j, z, None)
        send(dst if src is None else src, dst, xs_s.at[i], xs_r.at[i], sib)
        shares.append((a, j, z))

    def whole(a):
        ref = dp_piece(a, y, zl, None)
        return pltpu.make_async_remote_copy(
            ref, ref, st_s.at[a], st_r.at[a], device_id=sib, device_id_type=MESH
        )

    def cols(j):
        return pl.ds(pl.multiple_of(j * W, W), W)

    def forward_x(rows, t, at, n):
        def step(i, _):
            j = at(i)
            xj = rows[0, j]
            acc[t, 0] += nt(wg[:, cols(j)], xj)
            acc[t, 1] += nt(wu[:, cols(j)], xj)
            return 0

        lax.fori_loop(0, n, step, 0)

    def forward_dy(rows, t, at, n):
        def step(i, _):
            j = at(i)
            acc[t, 2] += nt(wd[:, cols(j)], rows[1, j])
            return 0

        lax.fori_loop(0, n, step, 0)

    def between(t):
        gate = gate_row(mr, t)
        pre, up, g = acc[t, 0], acc[t, 1], acc[t, 2]
        s = sigmoid(pre)
        active = pre * s
        hidden = (active * up).astype(bf16).astype(f32)
        gp[0:1, t * ROWS : (t + 1) * ROWS] = jnp.sum(hidden * g, axis=0, keepdims=True)
        gh = g * gate
        d_up = gh * active
        d_pre = gh * up * s * (1.0 + pre * (1.0 - s))
        lhs[t, 0] = d_pre.astype(bf16)
        lhs[t, 1] = d_up.astype(bf16)
        lhs[t, 2] = (hidden * gate).astype(bf16)
        rhs[t, :, 0:FFL] = d_pre.T.astype(bf16)
        rhs[t, :, FFL : 2 * FFL] = d_up.T.astype(bf16)

    def rows_back(t, out, at, n):
        def step(i, _):
            j = at(i)
            r = jnp.dot(rhs[t, :, 0:FFL], wg[:, cols(j)], preferred_element_type=f32)
            r += jnp.dot(rhs[t, :, FFL : 2 * FFL], wu[:, cols(j)], preferred_element_type=f32)
            out[j] = r.astype(bf16)
            return 0

        lax.fori_loop(0, n, step, 0)

    outs = (gg, gu, gd)

    def put(j, slot, i):
        return pltpu.make_async_copy(
            stage.at[slot, i], outs[i].at[:, cols(j)], osem.at[slot, i]
        )

    def weights_back(first, sq, fresh):
        def step(j, sq):
            slot = j % 2
            if not fresh:
                for i in range(3):
                    put(j - 2, slot, i).wait()
            for i in range(3):
                v = jnp.dot(lhs[0, i], cold[i // 2, j], preferred_element_type=f32)
                v += jnp.dot(lhs[1, i], extra[i // 2, j], preferred_element_type=f32)
                stage[slot, i] = v
                sq = sq + jnp.sum((v * v).reshape(-1, 8, W), axis=0)
                put(j, slot, i).start()
            return sq

        return lax.fori_loop(first, first + 2, step, sq)

    ex.start(1)
    ex.start(0)
    for i, (x2, seen) in enumerate((((x + 1) % 4, 2), ((x + 3) % 4, 1))):
        for c2 in (0, 1):
            send(
                s3.at[:, pl.ds((i * 2 + c2) * SLOT, SLOT), :],
                cold.at[0, :, slots_at(seen * 2 + c), :],
                sd_s.at[i * 2 + c2], sd_r.at[(seen - 1) * 2 + c], to(expert_at(x2, zh, c2), d),
            )
    share(0, x, zh, s2.at[0, :, 2 * SLOT :, :])
    share(1, x, zh, s2.at[1, :, 2 * SLOT :, :])
    acc[...] = jnp.zeros_like(acc)
    whole(0).wait_recv()
    dp.start(0)
    whole(1).wait_recv()
    dp.start(1)
    for copy in own_in:
        copy.wait()
    wait(cold.at[:, :, slots_at(1 - c), :], sib_s, sib_r)
    forward_dy(cold, 0, lambda i: d, 1)
    ex.s2()
    ex.s3()
    dp.s2()
    dp.s3()
    ex.s4()
    ex.s5()
    ex.s6()
    for a, j, z in ((0, ex.jl, zh), (0, ex.jr, zh), (1, x, 1 - zh), (1, ex.jl, zh), (1, ex.jr, zh)):
        share(a, j, z)
    dp.s4()
    dp.s5()
    dp.s6()
    for i in range(4):
        wait(cold.at[0, :, pl.ds((2 + i) * SLOT, SLOT), :], sd_s.at[0], sd_r.at[i])
    ex.s7()
    ex.s8()
    share(0, ex.jd, zh)
    dp.s7()
    dp.s8()
    forward_x(cold, 0, lambda i: d, 1)
    forward_x(cold, 0, lambda i: ((y + 1 + 2 * i) % 4) * 2 + zl, 2)
    ex.s9()
    ex.s10()
    share(1, ex.jl, 1 - zh)
    share(1, ex.jr, 1 - zh)
    dp.s9()
    dp.s10()
    forward_dy(cold, 0, lambda i: ((y + 1 + 2 * i) % 4) * 2 + zl, 2)
    forward_dy(cold, 0, lambda i: dbar, 1)
    dp.got("0oz", 0, y, 1 - zl, None)
    forward_x(cold, 0, lambda i: i * (dp.jd * 2 + zl) + (1 - i) * dbar, 2)
    ex.got("0oz", 0, x, 1 - zh, None)
    share(0, x, 1 - zh)
    ex.got("0lz", 0, ex.jl, 1 - zh, None)
    share(0, ex.jl, 1 - zh)
    ex.got("0rz", 0, ex.jr, 1 - zh, None)
    share(0, ex.jr, 1 - zh)
    ex.end_of_1_d()
    share(1, ex.jd, zh)
    ex.end_of_1_e()
    share(1, ex.jd, 1 - zh)
    ex.end_of_0_d()
    share(0, ex.jd, 1 - zh)
    forward_dy(cold, 0, lambda i: ((y + 1 + 2 * i) % 4) * 2 + 1 - zl, 2)
    for i in [1 - c] + list(range(2, E)):
        wait(mr.at[i], m_s.at[0], m_r.at[i])
    dp.end_of_1_d()
    forward_dy(cold, 0, lambda i: dp.jd * 2 + zl, 1)
    dp.got("0lz", 0, dp.jl, 1 - zl, None)
    dp.got("0rz", 0, dp.jr, 1 - zl, None)
    forward_x(cold, 0, lambda i: ((y + 1 + 2 * i) % 4) * 2 + 1 - zl, 2)
    dp.end_of_1_e()
    forward_dy(cold, 0, lambda i: dp.jd * 2 + 1 - zl, 1)
    dp.end_of_0_d()
    forward_x(cold, 0, lambda i: dp.jd * 2 + 1 - zl, 1)
    between(0)

    rows_back(0, dxc, lambda i: C.jd * 2 + i, 2)
    C.start0_far()
    C.start1("d")
    rows_back(0, dxc, lambda i: C.jr * 2 + i, 2)
    C.start0_right()
    C.start1("r")
    rows_back(0, dxc, lambda i: C.jl * 2 + i, 2)
    C.start0_left()
    C.start1("l")
    rows_back(0, dxc, lambda i: y * 2 + i, 2)
    C.start1("0")
    for i, where in enumerate(shares):
        wait(ex_other(*where, None), xs_s.at[i], xs_r.at[i])
    forward_x(extra, 1, lambda i: i, NDP)
    forward_dy(extra, 1, lambda i: i, NDP)
    C.relay0()
    C.relay1_far()
    between(1)
    far = [X.jd * 2, X.jd * 2 + 1, X.jr * 2, X.jl * 2, X.jr * 2 + 1, X.jl * 2 + 1, x * 2, x * 2 + 1]
    rows_back(1, dxh, lambda i: i, NDP)

    def h_rows(chip, core):
        return slots_at(chip * 2 + core)

    for i, chip in enumerate(far):
        send(dxh.at[:, h_rows(chip, 1 - c)], hin.at[chip], x_s.at[i], x_r.at[i], sib)
    C.relay1_near()
    for i, chip in enumerate(far):
        wait(hin.at[chip], x_s.at[i], x_r.at[i])
        add_into(hs.at[chip], dxh.at[:, h_rows(chip, c)], hin.at[chip])
        if i == 1:
            X.start0_far()
        if i == 5:
            X.start0_right()
            X.start0_left()
    for way in ("d", "r", "l", "0"):
        X.start1(way)
    C.relay1_last()
    sq = weights_back(0, jnp.zeros((8, W), f32), True)
    X.relay0()
    X.relay1_far()
    X.relay1_near()
    C.pair0()
    sq = weights_back(2, sq, False)
    X.relay1_last()
    X.pair0()
    sq = weights_back(4, sq, False)

    def give(a):
        for n, e2 in enumerate(peers):
            if parts[n] == a:
                send(
                    rc.at[0, slots_at(places[n]), :],
                    back.at[e], b_s.at[n], b_r.at[mine[n]], to(e2, d),
                )

    C.end1(rc.at[:, pl.ds(HR, HR)])
    give(1)
    sq = weights_back(6, sq, False)
    total = jnp.sum(jnp.sum(sq, axis=0, keepdims=True), axis=1, keepdims=True)
    gp[0:1, 2 * ROWS :] = jnp.broadcast_to(total, (1, GW - 2 * ROWS))
    for k, d2 in enumerate(dps):
        send(gp, gall.at[d], g_s.at[k], g_r.at[k], to(e, d2))
    gall[d] = gp[...]
    C.end0(rc.at[:, pl.ds(0, HR)])
    give(0)
    back[e] = rc[0, slots_at(c), :]
    X.end1(outh.at[pl.ds(NDP // 2, NDP // 2)])
    X.end0(outh.at[pl.ds(0, NDP // 2)])
    for k, d2 in enumerate(dps):
        send(outh.at[d2], hp.at[d], q_s.at[k], q_r.at[k], to(e, d2))
    hp[d] = outh[d]
    for k in range(NDP - 1):
        wait(gall.at[(d + NDP - 1 - k) % NDP], g_s.at[k], g_r.at[k])
    total = gall[0]
    for k in range(1, NDP):
        total = total + gall[k]
    gsum[...] = total
    gback[e] = total
    for n, e2 in enumerate(peers):
        send(gsum, gback.at[e], gb_s.at[n], gb_r.at[mine[n]], to(e2, d))
    for k in range(NDP - 1):
        wait(hp.at[(d + NDP - 1 - k) % NDP], q_s.at[k], q_r.at[k])
    total = hp[0].astype(f32)
    for k in range(1, NDP):
        total = total + hp[k].astype(f32)
    backh[...] = total.astype(bf16)

    for i in [1 - c] + list(range(2, E)):
        wait(back.at[0], b_s.at[0], b_r.at[i])
        wait(gback.at[0], gb_s.at[0], gb_r.at[i])
    for j in (NDP - 2, NDP - 1):
        for i in range(3):
            put(j, j % 2, i).wait()
    whole(0).wait_send()
    whole(1).wait_send()
    for copy in rest:
        copy.wait_send()
    dp.drain()
    ex.drain()
    C.drain()
    X.drain()


def moe(s1, s2, s3, m, wg, wu, wd):
    FFL, width = wg.shape
    D = pltpu.SemaphoreType.DMA
    V = pltpu.VMEM
    return pl.pallas_call(
        moe_kernel,
        in_specs=[ANY] * 7,
        out_specs=[VM] * 4 + [ANY] * 3,
        out_shape=[
            jax.ShapeDtypeStruct((E, SLOT, W), bf16),
            jax.ShapeDtypeStruct((SLOT, W), bf16),
            jax.ShapeDtypeStruct((E, 1, GW), f32),
            jax.ShapeDtypeStruct((E, 8, 128), f32),
        ]
        + [jax.ShapeDtypeStruct((FFL, width), f32)] * 3,
        scratch_shapes=Scatter.scratch(C_PIECE, C_HALF)
        + Scatter.scratch(H_PIECE, H_HALF)
        + [
            V((2, NDP, ROWS, W), bf16), V((2, NDP, ROWS, W), bf16),
            V((3, FFL, width), bf16),
            V((2, 3, FFL, ROWS), f32), V((2, 3, FFL, ROWS), bf16), V((2, ROWS, 2 * FFL), bf16),
            V((2, 3, FFL, W), f32),
            V((NDP, ROWS, W), bf16), V((NDP, ROWS, W), bf16), V((1, GW), f32),
            V((1, ROWS, W), bf16),
            V((NDP, NDP, SLOT, W), bf16), V((NDP, NDP, SLOT, W), bf16),
            V((NDP, SLOT, W), bf16), V((NDP, SLOT, W), bf16),
            V((NDP, 1, GW), f32), V((1, GW), f32),
            D((2,)), D((2,)), D((4,)), D((4,)), D((15,)), D((16,)), D, D,
            D((18,)), D((18,)), D((18,)), D((18,)), D((16,)), D((16,)), D((6,)), D((2, 3)),
            D((7,)), D((7,)), D((15,)), D((16,)), D((15,)), D((16,)),
            D((8,)), D((8,)), D((7,)), D((7,)),
        ],
        compiler_params=pltpu.CompilerParams(
            collective_id=1, has_side_effects=True, vmem_limit_bytes=62 * 1024 * 1024
        ),
        name="moe",
    )(s1, s2, s3, m, wg, wu, wd)


GRAD_CUTS = 4


def finish_kernel(
    ids_ref, logits_ref, back, backh, gback, mr, g1, g2, g3,
    rows_ref, gl_ref, norm_ref, o1, o2, o3, held, isem, osem,
):
    cuts = [(i, k) for i in range(3) for k in range(GRAD_CUTS)]
    n = g1.shape[0] // GRAD_CUTS

    def load(i, k):
        r = pl.ds(k * n, n)
        return pltpu.make_async_copy((g1, g2, g3)[i].at[r], held.at[i, r], isem.at[i, k])

    def store(i, k):
        r = pl.ds(k * n, n)
        return pltpu.make_async_copy(held.at[i, r], (o1, o2, o3)[i].at[r], osem.at[i, k])

    for cut in cuts:
        load(*cut).start()
    for cut in cuts:
        load(*cut).wait()
        store(*cut).start()
    finish_rows(ids_ref, logits_ref, back, backh, gback, mr, rows_ref, gl_ref, norm_ref)
    for cut in cuts:
        store(*cut).wait()


def finish_rows(ids_ref, logits_ref, back, backh, gback, mr, rows_ref, gl_ref, norm_ref):
    e, _, x, zh, c, _, _ = place()
    ids = ids_ref[...]
    onehot, rank = row_facts(ids, E)
    probs = soft(logits_ref[...])
    n = ids.shape[1]
    first = rank < SLOT
    slot = lax.broadcasted_iota(jnp.int32, (ROWS, n), 0)
    pick = (slot == jnp.where(first, ids * SLOT + rank, -1)).astype(f32).astype(bf16)
    slot = lax.broadcasted_iota(jnp.int32, (SLOT, n), 0)
    pickh = (slot == rank - SLOT).astype(f32).astype(bf16)
    got = tn(pick, back[...].reshape(ROWS, W)) + tn(pickh, backh[...])
    rows_ref[...] = got.astype(bf16)
    rel = seen_from(ids, x, zh, c)
    lane = jnp.where(first, rel * SLOT + rank, ROWS + e * SLOT + rank - SLOT)
    slot = lax.broadcasted_iota(jnp.int32, (2 * ROWS, n), 0)
    here = (slot == lane).astype(f32).astype(bf16)
    found = jnp.dot(gback[:, 0, 0 : 2 * ROWS].astype(bf16), here, preferred_element_type=f32)
    dgate = jnp.sum(onehot * found, axis=0, keepdims=True)
    count = jnp.sum(mr[...], axis=0)[2:3, :]
    across = lax.broadcasted_iota(jnp.int32, (E, 128), 0)
    diag = across == lax.broadcasted_iota(jnp.int32, (E, 128), 1)
    column = jnp.sum(jnp.where(diag, jnp.broadcast_to(count, (E, 128)), 0.0), axis=1, keepdims=True)
    pulls = onehot * dgate + 1.0 * E * (column / (E * n))
    gl_ref[...] = probs * (pulls - jnp.sum(probs * pulls, axis=0, keepdims=True))
    norm_ref[...] = jnp.sqrt(jnp.sum(gback[:, 0, 2 * ROWS : 2 * ROWS + 128], axis=0, keepdims=True))


def finish(ids, logits, back, backh, gback, mr, *grads):
    n = ids.shape[1]
    return pl.pallas_call(
        finish_kernel,
        in_specs=[VM] * 6 + [ANY] * 3,
        out_specs=[VM] * 3 + [ANY] * 3,
        out_shape=[
            jax.ShapeDtypeStruct((n, W), bf16),
            jax.ShapeDtypeStruct((E, n), f32),
            jax.ShapeDtypeStruct((1, 128), f32),
        ]
        + [jax.ShapeDtypeStruct(g.shape, f32) for g in grads],
        scratch_shapes=[
            pltpu.VMEM((3,) + grads[0].shape, f32),
            pltpu.SemaphoreType.DMA((3, GRAD_CUTS)),
            pltpu.SemaphoreType.DMA((3, GRAD_CUTS)),
        ],
        name="finish",
    )(ids, logits, back, backh, gback, mr, *grads)


def local(rows_x, rows_dy, router_logits, expert_of, w_gate, w_up, w_down):
    ids = expert_of.reshape(1, -1)
    logits = router_logits.T
    s1, s2, s3, m = lay_out(ids, logits, rows_x, rows_dy)
    back, backh, gback, mr, gg, gu, gd = moe(
        s1, s2, s3, m, w_gate[0], w_up[0], w_down[0]
    )
    grad_rows, grad_logits, norm, gg, gu, gd = finish(
        ids, logits, back, backh, gback, mr, gg, gu, gd
    )
    return grad_rows, grad_logits.T, gg[None], gu[None], gd[None], norm[0, 0]


def solution(mesh):
    rows = P("expert", None)
    weights = P("expert", "dp", None)
    return jax.shard_map(
        local,
        mesh=mesh,
        in_specs=(rows, rows, rows, rows, weights, weights, weights),
        out_specs=(P("expert", "dp"), rows, weights, weights, weights, P()),
        check_vma=False,
    )
```

```python
import jax
import jax.numpy as jnp
from jax import lax
from jax.experimental import pallas as pl
from jax.experimental.pallas import tpu as pltpu
from jax.sharding import PartitionSpec as P

f32 = jnp.float32
bf16 = jnp.bfloat16
MESH = pl.DeviceIdType.MESH
ANY = pl.BlockSpec(memory_space=pl.ANY)
VM = pl.BlockSpec(memory_space=pltpu.VMEM)
SM = pl.BlockSpec(memory_space=pltpu.SMEM)

E = 16
NDP = 8
SLOT = 32
W = 512
ROWS = E * SLOT
LOCAL = 2 * SLOT
GW = 1280


def place():
    e = lax.axis_index("expert")
    d = lax.axis_index("dp")
    return e, d, e // 4, (e // 2) % 2, e % 2, d // 2, d % 2


def expert_at(x, zh, c):
    return (x * 2 + zh) * 2 + c


def to(e, d):
    return {"expert": e, "dp": d}


def row_facts(ids, experts):
    rows = ids.shape[1]
    onehot = (lax.broadcasted_iota(jnp.int32, (experts, rows), 0) == ids).astype(f32)
    before = lax.broadcasted_iota(jnp.int32, (rows, rows), 0) < lax.broadcasted_iota(
        jnp.int32, (rows, rows), 1
    )
    earlier = jnp.dot(onehot.astype(bf16), before.astype(bf16), preferred_element_type=f32)
    rank = jnp.sum(onehot * earlier, axis=0, keepdims=True).astype(jnp.int32)
    return onehot, rank


def soft(logits):
    top = jnp.max(logits, axis=0, keepdims=True)
    ex = jnp.exp(logits - top)
    return ex / jnp.sum(ex, axis=0, keepdims=True)


def nt(a, b):
    return lax.dot_general(a, b, (((1,), (1,)), ((), ())), preferred_element_type=f32)


def tn(a, b):
    return lax.dot_general(a, b, (((0,), (0,)), ((), ())), preferred_element_type=f32)


def seen_from(ids, x, zh, c):
    dx = (x - (ids >> 2)) & 3
    return ((dx ^ (dx >> 1)) + 4 * (zh ^ ((ids >> 1) & 1))) * 2 + c


def slots_kernel(ids_ref, logits_ref, x_ref, dy_ref, s1_ref, s2_ref, s3_ref, m_ref):
    e, d, x, zh, c, y, zl = place()
    ids = ids_ref[...]
    onehot, rank = row_facts(ids, E)
    rows = ids.shape[1]
    none = -1

    def perm(slots, target):
        slot = lax.broadcasted_iota(jnp.int32, (slots, rows), 0)
        return (slot == target).astype(f32).astype(bf16)

    far = (zh ^ ((ids >> 1) & 1)) == 1
    first = rank < SLOT
    chip = ((ids >> 2) * 2 + (ids & 1)) * SLOT + rank
    for g, ours in ((0, jnp.logical_not(far)), (1, far)):
        p = perm(ROWS // 2, jnp.where(first & ours, chip, none))
        at = pl.ds(pl.multiple_of((d if g == 0 else y * 2 + 1 - zl) * W, W), W)
        s1_ref[0, g] = jnp.dot(p, x_ref[:, at], preferred_element_type=f32).astype(bf16)
        s1_ref[1, g] = jnp.dot(p, dy_ref[:, at], preferred_element_type=f32).astype(bf16)
    home = jnp.where(ids == e, rank, jnp.where(ids == e + 1 - 2 * c, SLOT + rank, none))
    dx = ((ids >> 2) - x) & 3
    side = (3 + (dx & 2) + (ids & 1)) * SLOT + rank
    home = jnp.where(((dx & 1) == 1) & jnp.logical_not(far), side, home)
    p = perm(7 * SLOT, jnp.where(first, home, SLOT + rank))
    for j in range(NDP):
        at = slice(j * W, (j + 1) * W)
        got = jnp.dot(p, x_ref[:, at], preferred_element_type=f32).astype(bf16)
        s2_ref[0, j] = got[: 3 * SLOT]
        s3_ref[j] = got[3 * SLOT :]
        s2_ref[1, j] = jnp.dot(p[: 3 * SLOT], dy_ref[:, at], preferred_element_type=f32).astype(bf16)

    gate = jnp.sum(soft(logits_ref[...]) * onehot, axis=0, keepdims=True).astype(bf16).astype(f32)
    lane = lax.broadcasted_iota(jnp.int32, (128, rows), 0)
    spot = (seen_from(ids, x, zh, c) & 3) * SLOT + rank
    cold = (onehot * gate * first.astype(f32)).astype(bf16)
    cold = nt(cold, (lane == spot).astype(f32).astype(bf16))
    gate8 = jnp.broadcast_to(gate, (8, rows)).astype(bf16)
    spot = jnp.where(first, none, (e & 3) * SLOT + rank - SLOT)
    hot = nt(gate8, (lane == spot).astype(f32).astype(bf16))
    count = nt(jnp.ones((8, rows), bf16), (lane == ids).astype(f32).astype(bf16))
    line = lax.broadcasted_iota(jnp.int32, (8, 128), 0)
    for k in range(E):
        mine = jnp.broadcast_to(cold[k : k + 1, :], (8, 128))
        busy = (jnp.sum(onehot[k : k + 1, :], axis=1, keepdims=True) > SLOT).astype(f32)
        rest = jnp.where(line == 2, count, jnp.broadcast_to(busy, (8, 128)))
        m_ref[k] = jnp.where(line == 0, mine, jnp.where(line == 1, hot, rest))


def lay_out(ids, logits, x, dy):
    return pl.pallas_call(
        slots_kernel,
        in_specs=[VM] * 4,
        out_specs=[VM] * 4,
        out_shape=[
            jax.ShapeDtypeStruct((2, 2, ROWS // 2, W), bf16),
            jax.ShapeDtypeStruct((2, NDP, 3 * SLOT, W), bf16),
            jax.ShapeDtypeStruct((NDP, 4 * SLOT, W), bf16),
            jax.ShapeDtypeStruct((E, 8, 128), f32),
        ],
        name="lay_out",
    )(ids, logits, x, dy)


class Gather:
    names = (
        "0oz", "0or", "0ol", "0lr", "0lz", "0rl", "0rz", "0dz", "0ez",
        "1oz", "1or", "1ol", "1zr", "1zl", "1lr", "1kr", "1rl", "1ql",
    )

    def __init__(self, own, piece, j, z, right, left, pair, ssem, rsem):
        self.own, self.piece, self.ssem, self.rsem = own, piece, ssem, rsem
        self.j, self.z = j, z
        self.jl, self.jr, self.jd = (j + 3) % 4, (j + 1) % 4, (j + 2) % 4
        self.right, self.left, self.pair = right, left, pair
        self.sent = []

    def send(self, name, src, dst, dev):
        i = self.names.index(name)
        copy = pltpu.make_async_remote_copy(
            src, dst, self.ssem.at[i], self.rsem.at[i], device_id=dev, device_id_type=MESH
        )
        copy.start()
        self.sent.append(copy)

    def pass_on(self, name, dev, *where):
        ref = self.piece(*where)
        self.send(name, ref, ref, dev)

    def got(self, name, *where):
        i = self.names.index(name)
        ref = self.piece(*where)
        pltpu.make_async_remote_copy(
            ref, ref, self.ssem.at[i], self.rsem.at[i], device_id=self.pair, device_id_type=MESH
        ).wait_recv()

    def start(self, a):
        for way, dev in (("z", self.pair), ("r", self.right), ("l", self.left)):
            self.send(f"{a}o{way}", self.own(a), self.piece(a, self.j, self.z, None), dev)

    def s2(self):
        self.got("0or", 0, self.jl, self.z, None)
        self.pass_on("0lr", self.right, 0, self.jl, self.z, 0)
        self.pass_on("0lz", self.pair, 0, self.jl, self.z, None)

    def s3(self):
        self.got("0ol", 0, self.jr, self.z, None)
        self.pass_on("0rl", self.left, 0, self.jr, self.z, 1)
        self.pass_on("0rz", self.pair, 0, self.jr, self.z, None)

    def s4(self):
        self.got("1oz", 1, self.j, 1 - self.z, None)
        self.pass_on("1zr", self.right, 1, self.j, 1 - self.z, None)
        self.pass_on("1zl", self.left, 1, self.j, 1 - self.z, None)

    def s5(self):
        self.got("1or", 1, self.jl, self.z, None)
        self.pass_on("1lr", self.right, 1, self.jl, self.z, 0)

    def s6(self):
        self.got("1ol", 1, self.jr, self.z, None)
        self.pass_on("1rl", self.left, 1, self.jr, self.z, 1)

    def s7(self):
        self.got("0lr", 0, self.jd, self.z, 0)
        self.pass_on("0dz", self.pair, 0, self.jd, self.z, 0)

    def s8(self):
        self.got("0rl", 0, self.jd, self.z, 1)
        self.pass_on("0ez", self.pair, 0, self.jd, self.z, 1)

    def s9(self):
        self.got("1zr", 1, self.jl, 1 - self.z, None)
        self.pass_on("1kr", self.right, 1, self.jl, 1 - self.z, 0)

    def s10(self):
        self.got("1zl", 1, self.jr, 1 - self.z, None)
        self.pass_on("1ql", self.left, 1, self.jr, 1 - self.z, 1)

    def end_of_1_d(self):
        self.got("1lr", 1, self.jd, self.z, 0)
        self.got("1rl", 1, self.jd, self.z, 1)

    def end_of_1_e(self):
        self.got("1kr", 1, self.jd, 1 - self.z, 0)
        self.got("1ql", 1, self.jd, 1 - self.z, 1)

    def end_of_0_d(self):
        self.got("0dz", 0, self.jd, 1 - self.z, 0)
        self.got("0ez", 0, self.jd, 1 - self.z, 1)

    def drain(self):
        for copy in self.sent:
            copy.wait_send()


def meet(partners):
    barrier = pltpu.get_barrier_semaphore()
    for dev in partners:
        pl.semaphore_signal(barrier, inc=1, device_id=dev, device_id_type=MESH)
    pl.semaphore_wait(barrier, len(partners))


def others(x, zh):
    order = (0, 1, 3, 2)
    for k in range(1, 8):
        dx, dz = k // 2, k % 2
        yield order[dx] + 4 * dz, order[(4 - dx) % 4] + 4 * dz, (x + dx) % 4, (zh + dz) % 2


def sigmoid(v):
    return 1.0 / (1.0 + jnp.exp(-v))


def gate_row(mr, t):
    _, _, x, _, c, _, _ = place()
    parts = []
    for g in range(E // 4):
        dx = (g + 4 - x) % 4
        at = g * 4 if t == 0 else (dx + dx // 2 - 2 * (dx // 3)) * 2
        part = mr[at, t : t + 1, :]
        for i in (1, 2, 3) if t == 0 else (1, 8, 9):
            part = part + mr[at + i, t : t + 1, :]
        parts.append(part if t == 0 else part * mr[c, 3:4, :])
    return jnp.concatenate(parts, axis=1)


def add_into(out, *terms):
    n, rows, _ = out.shape
    step_rows = min(rows, 64)
    for i in range(n):

        def step(k, _):
            r = pl.ds(pl.multiple_of(k * step_rows, step_rows), step_rows)
            total = terms[0][i, r, :].astype(f32)
            for term in terms[1:]:
                total = total + term[i, r, :].astype(f32)
            out[i, r, :] = total.astype(out.dtype)
            return 0

        if rows == step_rows:
            step(0, 0)
        else:
            lax.fori_loop(0, rows // step_rows, step, 0)


class Scatter:
    names = (
        "ar0", "ar1", "al0", "al1", "br0", "br1", "bl0", "bl1", "cr0", "cr1", "cl0", "cl1", "p",
        "zd", "zr", "zl", "z0", "hr", "hl", "ir", "il", "kr", "kl",
    )

    @staticmethod
    def scratch(piece, half):
        V = pltpu.VMEM
        return [
            V((2,) + half, bf16), V((2,) + half, bf16), V((2,) + half, bf16), V((2,) + half, bf16),
            V((2,) + piece, bf16), V((2,) + piece, bf16),
            V(piece, bf16), V(piece, bf16), V(piece, f32),
            V((4,) + piece, bf16), V((4,) + piece, bf16),
            V(half, bf16), V(half, bf16), V(piece, bf16), V(piece, bf16),
            pltpu.SemaphoreType.DMA((23,)), pltpu.SemaphoreType.DMA((23,)),
        ]

    def __init__(self, chunk, cut, j, z, right, left, pair, refs):
        self.chunk, self.cut, self.j, self.z = chunk, cut, j, z
        self.jl, self.jr, self.jd = (j + 3) % 4, (j + 1) % 4, (j + 2) % 4
        self.right, self.left, self.pair = right, left, pair
        (
            self.rl, self.rr, self.tr, self.tl, self.fl, self.fr, self.zs, self.zin, self.own,
            self.hz, self.hw, self.hrl, self.hrr, self.hfl, self.hfr, self.ssem, self.rsem,
        ) = refs
        self.sent = []

    def send(self, name, src, dst, dev):
        i = self.names.index(name)
        copy = pltpu.make_async_remote_copy(
            src, dst, self.ssem.at[i], self.rsem.at[i], device_id=dev, device_id_type=MESH
        )
        copy.start()
        self.sent.append(copy)

    def got(self, name, ref):
        i = self.names.index(name)
        pltpu.make_async_remote_copy(
            ref, ref, self.ssem.at[i], self.rsem.at[i], device_id=self.pair, device_id_type=MESH
        ).wait_recv()

    def start0_far(self):
        for k in (0, 1):
            far = self.chunk(0, self.jd, k)
            self.send(f"ar{k}", self.cut(far, 0), self.rl.at[k], self.right)
            self.send(f"al{k}", self.cut(far, 1), self.rr.at[k], self.left)

    def start0_right(self):
        for k in (0, 1):
            right = self.chunk(0, self.jr, k)
            self.send(f"br{k}", self.cut(right, 1), self.cut(self.fl.at[k], 1), self.right)

    def start0_left(self):
        for k in (0, 1):
            left = self.chunk(0, self.jl, k)
            self.send(f"bl{k}", self.cut(left, 0), self.cut(self.fr.at[k], 0), self.left)

    def start1(self, way):
        j = {"d": self.jd, "r": self.jr, "l": self.jl, "0": self.j}[way]
        self.send("z" + way, self.chunk(1, j, 1 - self.z), self.hz.at[j], self.pair)

    def relay0(self):
        for k in (0, 1):
            self.got(f"ar{k}", self.rl.at[k])
            add_into(self.tr.at[k], self.cut(self.chunk(0, self.jr, k), 0), self.rl.at[k])
            self.send(f"cr{k}", self.tr.at[k], self.cut(self.fl.at[k], 0), self.right)
            self.got(f"al{k}", self.rr.at[k])
            add_into(self.tl.at[k], self.cut(self.chunk(0, self.jl, k), 1), self.rr.at[k])
            self.send(f"cl{k}", self.tl.at[k], self.cut(self.fr.at[k], 1), self.left)

    def pair0(self):
        for k in (0, 1):
            for n, ref, h in (("br", self.fl, 1), ("bl", self.fr, 0), ("cr", self.fl, 0), ("cl", self.fr, 1)):
                self.got(f"{n}{k}", self.cut(ref.at[k], h))
        k = 1 - self.z
        add_into(self.zs, self.chunk(0, self.j, k), self.fl.at[k], self.fr.at[k])
        self.send("p", self.zs, self.zin, self.pair)
        k = self.z
        add_into(self.own, self.chunk(0, self.j, k), self.fl.at[k], self.fr.at[k])

    def end0(self, out):
        self.got("p", self.zin)
        add_into(out, self.own, self.zin)

    def relay1_far(self):
        self.got("zd", self.hz.at[self.jd])
        w = self.hw.at[self.jd]
        add_into(w, self.chunk(1, self.jd, self.z), self.hz.at[self.jd])
        self.send("hr", self.cut(w, 0), self.hrl, self.right)
        self.send("hl", self.cut(w, 1), self.hrr, self.left)

    def relay1_near(self):
        for way, j, h, ref, dev in (
            ("r", self.jr, 1, self.hfl, self.right), ("l", self.jl, 0, self.hfr, self.left)
        ):
            self.got("z" + way, self.hz.at[j])
            w = self.cut(self.hw.at[j], h)
            add_into(w, self.cut(self.chunk(1, j, self.z), h), self.cut(self.hz.at[j], h))
            self.send("i" + way, w, self.cut(ref, h), dev)

    def relay1_last(self):
        for way, j, h, inp, ref, dev in (
            ("r", self.jr, 0, self.hrl, self.hfl, self.right),
            ("l", self.jl, 1, self.hrr, self.hfr, self.left),
        ):
            self.got("h" + way, inp)
            w = self.cut(self.hw.at[j], h)
            add_into(w, self.cut(self.chunk(1, j, self.z), h), self.cut(self.hz.at[j], h), inp)
            self.send("k" + way, w, self.cut(ref, h), dev)

    def end1(self, out):
        self.got("z0", self.hz.at[self.j])
        self.got("ir", self.cut(self.hfl, 1))
        self.got("il", self.cut(self.hfr, 0))
        self.got("kr", self.cut(self.hfl, 0))
        self.got("kl", self.cut(self.hfr, 1))
        add_into(out, self.chunk(1, self.j, self.z), self.hz.at[self.j], self.hfl, self.hfr)

    def drain(self):
        for copy in self.sent:
            copy.wait_send()


HR = ROWS // 2
C_PIECE, C_HALF = (1, HR, W), (1, HR // 2, W)
H_PIECE, H_HALF = (NDP // 2, SLOT, W), (NDP // 4, SLOT, W)


def moe_kernel(
    s1, s2, s3, ms, wg_hbm, wu_hbm, wd_hbm,
    back, backh, gback, mr, gg, gu, gd,
    *refs,
):
    e, d, x, zh, c, y, zl = place()
    c_refs, refs = refs[:17], refs[17:]
    h_refs, refs = refs[:17], refs[17:]
    (
        cold, extra, weights, acc, lhs, rhs, dxc, dxh, gp,
        rc, hs, hin, outh, hp, gall, gsum,
        st_s, st_r, sd_s, sd_r, m_s, m_r, sib_s, sib_r, dp_s, dp_r, ex_s, ex_r, xs_s, xs_r, loc,
        g_s, g_r, b_s, b_r, gb_s, gb_r, x_s, x_r, q_s, q_r,
    ) = refs
    wg, wu, wd = weights.at[0], weights.at[1], weights.at[2]
    FFL = weights.shape[1]
    dbar = y * 2 + 1 - zl
    sib = to(expert_at(x, zh, 1 - c), d)
    right, left, pair = to(e, ((y + 1) % 4) * 2 + zl), to(e, ((y + 3) % 4) * 2 + zl), to(e, dbar)
    x_r_dev, x_l_dev = to(expert_at((x + 1) % 4, zh, c), d), to(expert_at((x + 3) % 4, zh, c), d)
    z_p = to(expert_at(x, 1 - zh, c), dbar)
    peers, places, mine, parts = [expert_at(x, zh, 1 - c)], [1 - c], [c], [0]
    row_peers = []
    for here, seen, x2, zh2 in others(x, zh):
        for c2 in (0, 1):
            peers.append(expert_at(x2, zh2, c2))
            places.append(here * 2 + c2)
            mine.append(seen * 2 + c)
            parts.append(here // 4)
            d2 = d if here < 4 else dbar
            row_peers.append((here, seen, expert_at(x2, zh2, c2), d2, x2 * 2 + c2))
    dps = [(d + k) % NDP for k in range(1, NDP)]

    own_in = [
        pltpu.make_async_copy(s2.at[:, :, 0:SLOT, :], cold.at[:, :, pl.ds(pl.multiple_of(c * SLOT, SLOT), SLOT), :], loc.at[0]),
        pltpu.make_async_copy(s2.at[:, :, 2 * SLOT :, :], extra.at[:, :, pl.ds(pl.multiple_of(e * SLOT, SLOT), SLOT), :], loc.at[1]),
        pltpu.make_async_copy(ms.at[e], mr.at[c], loc.at[2]),
        pltpu.make_async_copy(wg_hbm, wg, loc.at[3]),
        pltpu.make_async_copy(wu_hbm, wu, loc.at[4]),
        pltpu.make_async_copy(wd_hbm, wd, loc.at[5]),
    ]
    for copy in own_in:
        copy.start()
    meet(
        [to(e2, d) for e2 in peers] + [to(e, d2) for d2 in dps]
        + [to(p[2], dbar) for p in row_peers if p[0] >= 4]
    )

    rest = []

    def send(src, dst, ssem, rsem, dev):
        copy = pltpu.make_async_remote_copy(
            src, dst, ssem, rsem, device_id=dev, device_id_type=MESH
        )
        copy.start()
        rest.append(copy)

    def wait(ref, ssem, rsem):
        pltpu.make_async_remote_copy(
            ref, ref, ssem, rsem, device_id=sib, device_id_type=MESH
        ).wait_recv()

    def slots_at(n):
        return pl.ds(pl.multiple_of(n * SLOT, SLOT), SLOT)

    for a in (0, 1):
        for here, seen, e2, d2, q in row_peers:
            if a == 0 and here in (1, 2):
                continue
            pltpu.make_async_remote_copy(
                s1.at[a, here // 4, slots_at(q), :], cold.at[a, d2, slots_at(seen * 2 + c), :],
                st_s.at[a], st_r.at[a], device_id=to(e2, d2), device_id_type=MESH,
            ).start()
    meta_peers = row_peers + [(0, 0, expert_at(x, zh, 1 - c), d, 0)]
    for n, (_, seen, e2, d2, _) in enumerate(meta_peers):
        send(ms.at[e2], mr.at[seen * 2 + c], m_s.at[n], m_r.at[seen * 2 + c], to(e2, d2))
    send(s2.at[:, :, SLOT : 2 * SLOT, :], cold.at[:, :, slots_at(c), :], sib_s, sib_r, sib)

    def dp_piece(a, j, z, h):
        start = (3 if a == 0 else 1) * 2 * SLOT
        half = (ROWS - start) // 2
        rows = {None: (start, 2 * half), 0: (start, half), 1: (start + half, half)}[h]
        return cold.at[a, j * 2 + z, pl.ds(*rows), :]

    def ex_piece_of(core):
        def piece(a, j, z, h):
            chunks = {None: (0, NDP), 0: (0, NDP // 2), 1: (NDP // 2, NDP // 2)}[h]
            return extra.at[a, pl.ds(*chunks), slots_at(expert_at(j, z, core)), :]
        return piece

    ex_piece, ex_other = ex_piece_of(c), ex_piece_of(1 - c)
    dp = Gather(
        lambda a: dp_piece(a, y, zl, None), dp_piece, y, zl, right, left, pair, dp_s, dp_r
    )
    ex = Gather(
        lambda a: s2.at[a, :, 2 * SLOT :, :], ex_piece, x, zh, x_r_dev, x_l_dev, z_p, ex_s, ex_r
    )
    C = Scatter(
        lambda a, j, z: dxc.at[pl.ds(j * 2 + z, 1), pl.ds(a * HR, HR)],
        lambda ref, h: ref.at[:, pl.ds(h * (HR // 2), HR // 2)],
        y, zl, right, left, pair, c_refs,
    )
    X = Scatter(
        lambda a, j, z: hs.at[j * 2 + z, pl.ds(a * (NDP // 2), NDP // 2)],
        lambda ref, h: ref.at[pl.ds(h * (NDP // 4), NDP // 4)],
        x, zh, x_r_dev, x_l_dev, z_p, h_refs,
    )
    shares = []

    def share(a, j, z, src=None):
        i = len(shares)
        dst = ex_piece(a, j, z, None)
        send(dst if src is None else src, dst, xs_s.at[i], xs_r.at[i], sib)
        shares.append((a, j, z))

    def whole(a):
        ref = dp_piece(a, y, zl, None)
        return pltpu.make_async_remote_copy(
            ref, ref, st_s.at[a], st_r.at[a], device_id=sib, device_id_type=MESH
        )

    def cols(j):
        return pl.ds(pl.multiple_of(j * W, W), W)

    def forward_x(rows, t, at, n):
        def step(i, _):
            j = at(i)
            xj = rows[0, j]
            acc[t, 0] += nt(wg[:, cols(j)], xj)
            acc[t, 1] += nt(wu[:, cols(j)], xj)
            return 0

        lax.fori_loop(0, n, step, 0)

    def forward_dy(rows, t, at, n):
        def step(i, _):
            j = at(i)
            acc[t, 2] += nt(wd[:, cols(j)], rows[1, j])
            return 0

        lax.fori_loop(0, n, step, 0)

    def between(t):
        gate = gate_row(mr, t)
        pre, up, g = acc[t, 0], acc[t, 1], acc[t, 2]
        s = sigmoid(pre)
        active = pre * s
        hidden = (active * up).astype(bf16).astype(f32)
        gp[0:1, t * ROWS : (t + 1) * ROWS] = jnp.sum(hidden * g, axis=0, keepdims=True)
        gh = g * gate
        d_up = gh * active
        d_pre = gh * up * s * (1.0 + pre * (1.0 - s))
        lhs[t, 0] = d_pre.astype(bf16)
        lhs[t, 1] = d_up.astype(bf16)
        lhs[t, 2] = (hidden * gate).astype(bf16)
        rhs[t, :, 0:FFL] = d_pre.T.astype(bf16)
        rhs[t, :, FFL : 2 * FFL] = d_up.T.astype(bf16)

    def rows_back(t, out, at, n):
        def step(i, _):
            j = at(i)
            r = jnp.dot(rhs[t, :, 0:FFL], wg[:, cols(j)], preferred_element_type=f32)
            r += jnp.dot(rhs[t, :, FFL : 2 * FFL], wu[:, cols(j)], preferred_element_type=f32)
            out[j] = r.astype(bf16)
            return 0

        lax.fori_loop(0, n, step, 0)

    outs = (gg, gu, gd)

    def weights_back(first, sq):
        def step(j, sq):
            for i in range(3):
                v = jnp.dot(lhs[0, i], cold[i // 2, j], preferred_element_type=f32)
                v += jnp.dot(lhs[1, i], extra[i // 2, j], preferred_element_type=f32)
                outs[i][:, cols(j)] = v
                sq = sq + jnp.sum((v * v).reshape(-1, 8, W), axis=0)
            return sq

        return lax.fori_loop(first, first + 2, step, sq)

    ex.start(1)
    ex.start(0)
    for i, (x2, seen) in enumerate((((x + 1) % 4, 2), ((x + 3) % 4, 1))):
        for c2 in (0, 1):
            send(
                s3.at[:, pl.ds((i * 2 + c2) * SLOT, SLOT), :],
                cold.at[0, :, slots_at(seen * 2 + c), :],
                sd_s.at[i * 2 + c2], sd_r.at[(seen - 1) * 2 + c], to(expert_at(x2, zh, c2), d),
            )
    share(0, x, zh, s2.at[0, :, 2 * SLOT :, :])
    share(1, x, zh, s2.at[1, :, 2 * SLOT :, :])
    acc[...] = jnp.zeros_like(acc)
    whole(0).wait_recv()
    dp.start(0)
    whole(1).wait_recv()
    dp.start(1)
    for copy in own_in:
        copy.wait()
    wait(cold.at[:, :, slots_at(1 - c), :], sib_s, sib_r)
    forward_dy(cold, 0, lambda i: d, 1)
    ex.s2()
    ex.s3()
    dp.s2()
    dp.s3()
    ex.s4()
    ex.s5()
    ex.s6()
    for a, j, z in ((0, ex.jl, zh), (0, ex.jr, zh), (1, x, 1 - zh), (1, ex.jl, zh), (1, ex.jr, zh)):
        share(a, j, z)
    dp.s4()
    dp.s5()
    dp.s6()
    for i in range(4):
        wait(cold.at[0, :, pl.ds((2 + i) * SLOT, SLOT), :], sd_s.at[0], sd_r.at[i])
    ex.s7()
    ex.s8()
    share(0, ex.jd, zh)
    dp.s7()
    dp.s8()
    forward_x(cold, 0, lambda i: d, 1)
    forward_x(cold, 0, lambda i: ((y + 1 + 2 * i) % 4) * 2 + zl, 2)
    ex.s9()
    ex.s10()
    share(1, ex.jl, 1 - zh)
    share(1, ex.jr, 1 - zh)
    dp.s9()
    dp.s10()
    forward_dy(cold, 0, lambda i: ((y + 1 + 2 * i) % 4) * 2 + zl, 2)
    forward_dy(cold, 0, lambda i: dbar, 1)
    dp.got("0oz", 0, y, 1 - zl, None)
    forward_x(cold, 0, lambda i: i * (dp.jd * 2 + zl) + (1 - i) * dbar, 2)
    ex.got("0oz", 0, x, 1 - zh, None)
    share(0, x, 1 - zh)
    ex.got("0lz", 0, ex.jl, 1 - zh, None)
    share(0, ex.jl, 1 - zh)
    ex.got("0rz", 0, ex.jr, 1 - zh, None)
    share(0, ex.jr, 1 - zh)
    ex.end_of_1_d()
    share(1, ex.jd, zh)
    ex.end_of_1_e()
    share(1, ex.jd, 1 - zh)
    ex.end_of_0_d()
    share(0, ex.jd, 1 - zh)
    forward_dy(cold, 0, lambda i: ((y + 1 + 2 * i) % 4) * 2 + 1 - zl, 2)
    for i in [1 - c] + list(range(2, E)):
        wait(mr.at[i], m_s.at[0], m_r.at[i])
    dp.end_of_1_d()
    forward_dy(cold, 0, lambda i: dp.jd * 2 + zl, 1)
    dp.got("0lz", 0, dp.jl, 1 - zl, None)
    dp.got("0rz", 0, dp.jr, 1 - zl, None)
    forward_x(cold, 0, lambda i: ((y + 1 + 2 * i) % 4) * 2 + 1 - zl, 2)
    dp.end_of_1_e()
    forward_dy(cold, 0, lambda i: dp.jd * 2 + 1 - zl, 1)
    dp.end_of_0_d()
    forward_x(cold, 0, lambda i: dp.jd * 2 + 1 - zl, 1)
    between(0)

    rows_back(0, dxc, lambda i: C.jd * 2 + i, 2)
    C.start0_far()
    C.start1("d")
    rows_back(0, dxc, lambda i: C.jr * 2 + i, 2)
    C.start0_right()
    C.start1("r")
    rows_back(0, dxc, lambda i: C.jl * 2 + i, 2)
    C.start0_left()
    C.start1("l")
    rows_back(0, dxc, lambda i: y * 2 + i, 2)
    C.start1("0")
    for i, where in enumerate(shares):
        wait(ex_other(*where, None), xs_s.at[i], xs_r.at[i])
    forward_x(extra, 1, lambda i: i, NDP)
    forward_dy(extra, 1, lambda i: i, NDP)
    C.relay0()
    C.relay1_far()
    between(1)
    far = [X.jd * 2, X.jd * 2 + 1, X.jr * 2, X.jl * 2, X.jr * 2 + 1, X.jl * 2 + 1, x * 2, x * 2 + 1]
    rows_back(1, dxh, lambda i: i, NDP)

    def h_rows(chip, core):
        return slots_at(chip * 2 + core)

    for i, chip in enumerate(far):
        send(dxh.at[:, h_rows(chip, 1 - c)], hin.at[chip], x_s.at[i], x_r.at[i], sib)
    C.relay1_near()
    for i, chip in enumerate(far):
        wait(hin.at[chip], x_s.at[i], x_r.at[i])
        add_into(hs.at[chip], dxh.at[:, h_rows(chip, c)], hin.at[chip])
        if i == 1:
            X.start0_far()
        if i == 5:
            X.start0_right()
            X.start0_left()
    for way in ("d", "r", "l", "0"):
        X.start1(way)
    C.pair0()
    C.relay1_last()
    sq = weights_back(0, jnp.zeros((8, W), f32))
    X.relay0()
    X.relay1_far()
    X.relay1_near()
    sq = weights_back(2, sq)
    X.relay1_last()
    X.pair0()
    sq = weights_back(4, sq)

    def give(a):
        for n, e2 in enumerate(peers):
            if parts[n] == a:
                send(
                    rc.at[0, slots_at(places[n]), :],
                    back.at[e], b_s.at[n], b_r.at[mine[n]], to(e2, d),
                )

    sq = weights_back(6, sq)
    total = jnp.sum(jnp.sum(sq, axis=0, keepdims=True), axis=1, keepdims=True)
    gp[0:1, 2 * ROWS :] = jnp.broadcast_to(total, (1, GW - 2 * ROWS))
    for k, d2 in enumerate(dps):
        send(gp, gall.at[d], g_s.at[k], g_r.at[k], to(e, d2))
    gall[d] = gp[...]
    C.end1(rc.at[:, pl.ds(HR, HR)])
    give(1)
    C.end0(rc.at[:, pl.ds(0, HR)])
    give(0)
    back[e] = rc[0, slots_at(c), :]
    X.end1(outh.at[pl.ds(NDP // 2, NDP // 2)])
    X.end0(outh.at[pl.ds(0, NDP // 2)])
    for k, d2 in enumerate(dps):
        send(outh.at[d2], hp.at[d], q_s.at[k], q_r.at[k], to(e, d2))
    hp[d] = outh[d]
    for k in range(NDP - 1):
        wait(gall.at[(d + NDP - 1 - k) % NDP], g_s.at[k], g_r.at[k])
    total = gall[0]
    for k in range(1, NDP):
        total = total + gall[k]
    gsum[...] = total
    gback[e] = total
    for n, e2 in enumerate(peers):
        send(gsum, gback.at[e], gb_s.at[n], gb_r.at[mine[n]], to(e2, d))
    for k in range(NDP - 1):
        wait(hp.at[(d + NDP - 1 - k) % NDP], q_s.at[k], q_r.at[k])
    total = hp[0].astype(f32)
    for k in range(1, NDP):
        total = total + hp[k].astype(f32)
    backh[...] = total.astype(bf16)

    for i in [1 - c] + list(range(2, E)):
        wait(back.at[0], b_s.at[0], b_r.at[i])
        wait(gback.at[0], gb_s.at[0], gb_r.at[i])
    whole(0).wait_send()
    whole(1).wait_send()
    for copy in rest:
        copy.wait_send()
    dp.drain()
    ex.drain()
    C.drain()
    X.drain()


def moe(s1, s2, s3, m, wg, wu, wd):
    FFL, width = wg.shape
    D = pltpu.SemaphoreType.DMA
    V = pltpu.VMEM
    return pl.pallas_call(
        moe_kernel,
        in_specs=[ANY] * 7,
        out_specs=[VM] * 7,
        out_shape=[
            pltpu.VMEM((E, SLOT, W), bf16),
            pltpu.VMEM((SLOT, W), bf16),
            pltpu.VMEM((E, 1, GW), f32),
            pltpu.VMEM((E, 8, 128), f32),
        ]
        + [pltpu.VMEM((FFL, width), f32)] * 3,
        scratch_shapes=Scatter.scratch(C_PIECE, C_HALF)
        + Scatter.scratch(H_PIECE, H_HALF)
        + [
            V((2, NDP, ROWS, W), bf16), V((2, NDP, ROWS, W), bf16),
            V((3, FFL, width), bf16),
            V((2, 3, FFL, ROWS), f32), V((2, 3, FFL, ROWS), bf16), V((2, ROWS, 2 * FFL), bf16),
            V((NDP, ROWS, W), bf16), V((NDP, ROWS, W), bf16), V((1, GW), f32),
            V((1, ROWS, W), bf16),
            V((NDP, NDP, SLOT, W), bf16), V((NDP, NDP, SLOT, W), bf16),
            V((NDP, SLOT, W), bf16), V((NDP, SLOT, W), bf16),
            V((NDP, 1, GW), f32), V((1, GW), f32),
            D((2,)), D((2,)), D((4,)), D((4,)), D((15,)), D((16,)), D, D,
            D((18,)), D((18,)), D((18,)), D((18,)), D((16,)), D((16,)), D((6,)),
            D((7,)), D((7,)), D((15,)), D((16,)), D((15,)), D((16,)),
            D((8,)), D((8,)), D((7,)), D((7,)),
        ],
        compiler_params=pltpu.CompilerParams(
            collective_id=1, has_side_effects=True, vmem_limit_bytes=54 * 1024 * 1024
        ),
        name="moe",
    )(s1, s2, s3, m, wg, wu, wd)


def finish_kernel(
    ids_ref, logits_ref, back, backh, gback, mr, g1, g2, g3,
    rows_ref, gl_ref, norm_ref, o1, o2, o3, osem,
):
    stores = [
        pltpu.make_async_copy(g, o, osem.at[i])
        for i, (g, o) in enumerate(((g1, o1), (g2, o2), (g3, o3)))
    ]
    for copy in stores:
        copy.start()
    finish_rows(ids_ref, logits_ref, back, backh, gback, mr, rows_ref, gl_ref, norm_ref)
    for copy in stores:
        copy.wait()


def finish_rows(ids_ref, logits_ref, back, backh, gback, mr, rows_ref, gl_ref, norm_ref):
    e, _, x, zh, c, _, _ = place()
    ids = ids_ref[...]
    onehot, rank = row_facts(ids, E)
    probs = soft(logits_ref[...])
    n = ids.shape[1]
    first = rank < SLOT
    slot = lax.broadcasted_iota(jnp.int32, (ROWS, n), 0)
    pick = (slot == jnp.where(first, ids * SLOT + rank, -1)).astype(f32).astype(bf16)
    slot = lax.broadcasted_iota(jnp.int32, (SLOT, n), 0)
    pickh = (slot == rank - SLOT).astype(f32).astype(bf16)
    got = tn(pick, back[...].reshape(ROWS, W)) + tn(pickh, backh[...])
    rows_ref[...] = got.astype(bf16)
    rel = seen_from(ids, x, zh, c)
    lane = jnp.where(first, rel * SLOT + rank, ROWS + e * SLOT + rank - SLOT)
    slot = lax.broadcasted_iota(jnp.int32, (2 * ROWS, n), 0)
    here = (slot == lane).astype(f32).astype(bf16)
    found = jnp.dot(gback[:, 0, 0 : 2 * ROWS].astype(bf16), here, preferred_element_type=f32)
    dgate = jnp.sum(onehot * found, axis=0, keepdims=True)
    count = jnp.sum(mr[...], axis=0)[2:3, :]
    across = lax.broadcasted_iota(jnp.int32, (E, 128), 0)
    diag = across == lax.broadcasted_iota(jnp.int32, (E, 128), 1)
    column = jnp.sum(jnp.where(diag, jnp.broadcast_to(count, (E, 128)), 0.0), axis=1, keepdims=True)
    pulls = onehot * dgate + 1.0 * E * (column / (E * n))
    gl_ref[...] = probs * (pulls - jnp.sum(probs * pulls, axis=0, keepdims=True))
    norm_ref[...] = jnp.sqrt(jnp.sum(gback[:, 0, 2 * ROWS : 2 * ROWS + 128], axis=0, keepdims=True))


def finish(ids, logits, back, backh, gback, mr, *grads):
    n = ids.shape[1]
    return pl.pallas_call(
        finish_kernel,
        in_specs=[VM] * 9,
        out_specs=[VM] * 3 + [ANY] * 3,
        out_shape=[
            jax.ShapeDtypeStruct((n, W), bf16),
            jax.ShapeDtypeStruct((E, n), f32),
            jax.ShapeDtypeStruct((1, 128), f32),
        ]
        + [jax.ShapeDtypeStruct(g.shape, f32) for g in grads],
        scratch_shapes=[
            pltpu.SemaphoreType.DMA((3,)),
        ],
        compiler_params=pltpu.CompilerParams(vmem_limit_bytes=20 * 1024 * 1024),
        name="finish",
    )(ids, logits, back, backh, gback, mr, *grads)


def local(rows_x, rows_dy, router_logits, expert_of, w_gate, w_up, w_down):
    ids = expert_of.reshape(1, -1)
    logits = router_logits.T
    s1, s2, s3, m = lay_out(ids, logits, rows_x, rows_dy)
    back, backh, gback, mr, gg, gu, gd = moe(
        s1, s2, s3, m, w_gate[0], w_up[0], w_down[0]
    )
    held = (back, backh, gback, mr, gg, gu, gd)
    held = [pltpu.with_memory_space_constraint(v, pltpu.VMEM) for v in held]
    grad_rows, grad_logits, norm, gg, gu, gd = finish(ids, logits, *held)
    return grad_rows, grad_logits.T, gg[None], gu[None], gd[None], norm[0, 0]


def solution(mesh):
    rows = P("expert", None)
    weights = P("expert", "dp", None)
    return jax.shard_map(
        local,
        mesh=mesh,
        in_specs=(rows, rows, rows, rows, weights, weights, weights),
        out_specs=(P("expert", "dp"), rows, weights, weights, weights, P()),
        check_vma=False,
    )
```

```python
import jax
import jax.numpy as jnp
from jax import lax
from jax.experimental import pallas as pl
from jax.experimental.pallas import tpu as pltpu
from jax.sharding import PartitionSpec as P

f32 = jnp.float32
bf16 = jnp.bfloat16
MESH = pl.DeviceIdType.MESH
ANY = pl.BlockSpec(memory_space=pl.ANY)
VM = pl.BlockSpec(memory_space=pltpu.VMEM)
SM = pl.BlockSpec(memory_space=pltpu.SMEM)

E = 16
NDP = 8
SLOT = 32
W = 512
ROWS = E * SLOT
LOCAL = 2 * SLOT
GW = 1280


def place():
    e = lax.axis_index("expert")
    d = lax.axis_index("dp")
    return e, d, e // 4, (e // 2) % 2, e % 2, d // 2, d % 2


def expert_at(x, zh, c):
    return (x * 2 + zh) * 2 + c


def to(e, d):
    return {"expert": e, "dp": d}


def row_facts(ids, experts):
    rows = ids.shape[1]
    onehot = (lax.broadcasted_iota(jnp.int32, (experts, rows), 0) == ids).astype(f32)
    before = lax.broadcasted_iota(jnp.int32, (rows, rows), 0) < lax.broadcasted_iota(
        jnp.int32, (rows, rows), 1
    )
    earlier = jnp.dot(onehot.astype(bf16), before.astype(bf16), preferred_element_type=f32)
    rank = jnp.sum(onehot * earlier, axis=0, keepdims=True).astype(jnp.int32)
    return onehot, rank


def soft(logits):
    top = jnp.max(logits, axis=0, keepdims=True)
    ex = jnp.exp(logits - top)
    return ex / jnp.sum(ex, axis=0, keepdims=True)


def nt(a, b):
    return lax.dot_general(a, b, (((1,), (1,)), ((), ())), preferred_element_type=f32)


def tn(a, b):
    return lax.dot_general(a, b, (((0,), (0,)), ((), ())), preferred_element_type=f32)


def seen_from(ids, x, zh, c):
    dx = (x - (ids >> 2)) & 3
    return ((dx ^ (dx >> 1)) + 4 * (zh ^ ((ids >> 1) & 1))) * 2 + c


def permute(slots, target):
    slot = lax.broadcasted_iota(jnp.int32, (slots, target.shape[1]), 0)
    return (slot == target).astype(f32).astype(bf16)


def slot_maps(ids, rank):
    e, _, x, zh, c, _, _ = place()
    far = (zh ^ ((ids >> 1) & 1)) == 1
    near = jnp.logical_not(far)
    first = rank < SLOT
    chip = ((ids >> 2) * 2 + (ids & 1)) * SLOT + rank
    maps = [permute(ROWS // 2, jnp.where(first & ours, chip, -1)) for ours in (near, far)]
    home = jnp.where(ids == e, rank, jnp.where(ids == e + 1 - 2 * c, SLOT + rank, -1))
    dx = ((ids >> 2) - x) & 3
    side = (3 + (dx & 2) + (ids & 1)) * SLOT + rank
    home = jnp.where(((dx & 1) == 1) & near, side, home)
    return maps + [permute(7 * SLOT, jnp.where(first, home, SLOT + rank))]


def fill_meta(m_ref, ids, logits, onehot, rank):
    e, _, x, zh, c, _, _ = place()
    rows = ids.shape[1]
    first = rank < SLOT
    gate = jnp.sum(soft(logits) * onehot, axis=0, keepdims=True).astype(bf16).astype(f32)
    lane = lax.broadcasted_iota(jnp.int32, (128, rows), 0)
    spot = (seen_from(ids, x, zh, c) & 3) * SLOT + rank
    cold = (onehot * gate * first.astype(f32)).astype(bf16)
    cold = nt(cold, (lane == spot).astype(f32).astype(bf16))
    gate8 = jnp.broadcast_to(gate, (8, rows)).astype(bf16)
    spot = jnp.where(first, -1, (e & 3) * SLOT + rank - SLOT)
    hot = nt(gate8, (lane == spot).astype(f32).astype(bf16))
    count = nt(jnp.ones((8, rows), bf16), (lane == ids).astype(f32).astype(bf16))
    line = lax.broadcasted_iota(jnp.int32, (8, 128), 0)
    for k in range(E):
        mine = jnp.broadcast_to(cold[k : k + 1, :], (8, 128))
        busy = (jnp.sum(onehot[k : k + 1, :], axis=1, keepdims=True) > SLOT).astype(f32)
        rest = jnp.where(line == 2, count, jnp.broadcast_to(busy, (8, 128)))
        m_ref[k] = jnp.where(line == 0, mine, jnp.where(line == 1, hot, rest))


class Gather:
    names = (
        "0oz", "0or", "0ol", "0lr", "0lz", "0rl", "0rz", "0dz", "0ez",
        "1oz", "1or", "1ol", "1zr", "1zl", "1lr", "1kr", "1rl", "1ql",
    )

    def __init__(self, own, piece, j, z, right, left, pair, ssem, rsem):
        self.own, self.piece, self.ssem, self.rsem = own, piece, ssem, rsem
        self.j, self.z = j, z
        self.jl, self.jr, self.jd = (j + 3) % 4, (j + 1) % 4, (j + 2) % 4
        self.right, self.left, self.pair = right, left, pair
        self.sent = []

    def send(self, name, src, dst, dev):
        i = self.names.index(name)
        copy = pltpu.make_async_remote_copy(
            src, dst, self.ssem.at[i], self.rsem.at[i], device_id=dev, device_id_type=MESH
        )
        copy.start()
        self.sent.append(copy)

    def pass_on(self, name, dev, *where):
        ref = self.piece(*where)
        self.send(name, ref, ref, dev)

    def got(self, name, *where):
        i = self.names.index(name)
        ref = self.piece(*where)
        pltpu.make_async_remote_copy(
            ref, ref, self.ssem.at[i], self.rsem.at[i], device_id=self.pair, device_id_type=MESH
        ).wait_recv()

    def start(self, a):
        for way, dev in (("z", self.pair), ("r", self.right), ("l", self.left)):
            self.send(f"{a}o{way}", self.own(a), self.piece(a, self.j, self.z, None), dev)

    def s2(self):
        self.got("0or", 0, self.jl, self.z, None)
        self.pass_on("0lr", self.right, 0, self.jl, self.z, 0)
        self.pass_on("0lz", self.pair, 0, self.jl, self.z, None)

    def s3(self):
        self.got("0ol", 0, self.jr, self.z, None)
        self.pass_on("0rl", self.left, 0, self.jr, self.z, 1)
        self.pass_on("0rz", self.pair, 0, self.jr, self.z, None)

    def s4(self):
        self.got("1oz", 1, self.j, 1 - self.z, None)
        self.pass_on("1zr", self.right, 1, self.j, 1 - self.z, None)
        self.pass_on("1zl", self.left, 1, self.j, 1 - self.z, None)

    def s5(self):
        self.got("1or", 1, self.jl, self.z, None)
        self.pass_on("1lr", self.right, 1, self.jl, self.z, 0)

    def s6(self):
        self.got("1ol", 1, self.jr, self.z, None)
        self.pass_on("1rl", self.left, 1, self.jr, self.z, 1)

    def s7(self):
        self.got("0lr", 0, self.jd, self.z, 0)
        self.pass_on("0dz", self.pair, 0, self.jd, self.z, 0)

    def s8(self):
        self.got("0rl", 0, self.jd, self.z, 1)
        self.pass_on("0ez", self.pair, 0, self.jd, self.z, 1)

    def s9(self):
        self.got("1zr", 1, self.jl, 1 - self.z, None)
        self.pass_on("1kr", self.right, 1, self.jl, 1 - self.z, 0)

    def s10(self):
        self.got("1zl", 1, self.jr, 1 - self.z, None)
        self.pass_on("1ql", self.left, 1, self.jr, 1 - self.z, 1)

    def end_of_1_d(self):
        self.got("1lr", 1, self.jd, self.z, 0)
        self.got("1rl", 1, self.jd, self.z, 1)

    def end_of_1_e(self):
        self.got("1kr", 1, self.jd, 1 - self.z, 0)
        self.got("1ql", 1, self.jd, 1 - self.z, 1)

    def end_of_0_d(self):
        self.got("0dz", 0, self.jd, 1 - self.z, 0)
        self.got("0ez", 0, self.jd, 1 - self.z, 1)

    def drain(self):
        for copy in self.sent:
            copy.wait_send()


def others(x, zh):
    order = (0, 1, 3, 2)
    for k in range(1, 8):
        dx, dz = k // 2, k % 2
        yield order[dx] + 4 * dz, order[(4 - dx) % 4] + 4 * dz, (x + dx) % 4, (zh + dz) % 2


def sigmoid(v):
    return 1.0 / (1.0 + jnp.exp(-v))


def gate_row(mr, t):
    _, _, x, _, c, _, _ = place()
    parts = []
    for g in range(E // 4):
        dx = (g + 4 - x) % 4
        at = g * 4 if t == 0 else (dx + dx // 2 - 2 * (dx // 3)) * 2
        part = mr[at, t : t + 1, :]
        for i in (1, 2, 3) if t == 0 else (1, 8, 9):
            part = part + mr[at + i, t : t + 1, :]
        parts.append(part if t == 0 else part * mr[c, 3:4, :])
    return jnp.concatenate(parts, axis=1)


def add_into(out, *terms):
    n, rows, _ = out.shape
    step_rows = min(rows, 64)
    for i in range(n):

        def step(k, _):
            r = pl.ds(pl.multiple_of(k * step_rows, step_rows), step_rows)
            total = terms[0][i, r, :].astype(f32)
            for term in terms[1:]:
                total = total + term[i, r, :].astype(f32)
            out[i, r, :] = total.astype(out.dtype)
            return 0

        if rows == step_rows:
            step(0, 0)
        else:
            lax.fori_loop(0, rows // step_rows, step, 0)


class Scatter:
    names = (
        "ar0", "ar1", "al0", "al1", "br0", "br1", "bl0", "bl1", "cr0", "cr1", "cl0", "cl1", "p",
        "zd", "zr", "zl", "z0", "hr", "hl", "ir", "il", "kr", "kl",
    )

    @staticmethod
    def scratch(piece, half):
        V = pltpu.VMEM
        return [
            V((2,) + half, bf16), V((2,) + half, bf16), V((2,) + half, bf16), V((2,) + half, bf16),
            V((2,) + piece, bf16), V((2,) + piece, bf16),
            V(piece, bf16), V(piece, bf16), V(piece, f32),
            V((4,) + piece, bf16), V((4,) + piece, bf16),
            V(half, bf16), V(half, bf16), V(piece, bf16), V(piece, bf16),
            pltpu.SemaphoreType.DMA((23,)), pltpu.SemaphoreType.DMA((23,)),
        ]

    def __init__(self, chunk, cut, j, z, right, left, pair, refs):
        self.chunk, self.cut, self.j, self.z = chunk, cut, j, z
        self.jl, self.jr, self.jd = (j + 3) % 4, (j + 1) % 4, (j + 2) % 4
        self.right, self.left, self.pair = right, left, pair
        (
            self.rl, self.rr, self.tr, self.tl, self.fl, self.fr, self.zs, self.zin, self.own,
            self.hz, self.hw, self.hrl, self.hrr, self.hfl, self.hfr, self.ssem, self.rsem,
        ) = refs
        self.sent = []

    def send(self, name, src, dst, dev):
        i = self.names.index(name)
        copy = pltpu.make_async_remote_copy(
            src, dst, self.ssem.at[i], self.rsem.at[i], device_id=dev, device_id_type=MESH
        )
        copy.start()
        self.sent.append(copy)

    def got(self, name, ref):
        i = self.names.index(name)
        pltpu.make_async_remote_copy(
            ref, ref, self.ssem.at[i], self.rsem.at[i], device_id=self.pair, device_id_type=MESH
        ).wait_recv()

    def start0_far(self):
        for k in (0, 1):
            far = self.chunk(0, self.jd, k)
            self.send(f"ar{k}", self.cut(far, 0), self.rl.at[k], self.right)
            self.send(f"al{k}", self.cut(far, 1), self.rr.at[k], self.left)

    def start0_right(self):
        for k in (0, 1):
            right = self.chunk(0, self.jr, k)
            self.send(f"br{k}", self.cut(right, 1), self.cut(self.fl.at[k], 1), self.right)

    def start0_left(self):
        for k in (0, 1):
            left = self.chunk(0, self.jl, k)
            self.send(f"bl{k}", self.cut(left, 0), self.cut(self.fr.at[k], 0), self.left)

    def start1(self, way):
        j = {"d": self.jd, "r": self.jr, "l": self.jl, "0": self.j}[way]
        self.send("z" + way, self.chunk(1, j, 1 - self.z), self.hz.at[j], self.pair)

    def relay0(self):
        for k in (0, 1):
            self.got(f"ar{k}", self.rl.at[k])
            add_into(self.tr.at[k], self.cut(self.chunk(0, self.jr, k), 0), self.rl.at[k])
            self.send(f"cr{k}", self.tr.at[k], self.cut(self.fl.at[k], 0), self.right)
            self.got(f"al{k}", self.rr.at[k])
            add_into(self.tl.at[k], self.cut(self.chunk(0, self.jl, k), 1), self.rr.at[k])
            self.send(f"cl{k}", self.tl.at[k], self.cut(self.fr.at[k], 1), self.left)

    def pair0(self):
        for k in (0, 1):
            for n, ref, h in (("br", self.fl, 1), ("bl", self.fr, 0), ("cr", self.fl, 0), ("cl", self.fr, 1)):
                self.got(f"{n}{k}", self.cut(ref.at[k], h))
        k = 1 - self.z
        add_into(self.zs, self.chunk(0, self.j, k), self.fl.at[k], self.fr.at[k])
        self.send("p", self.zs, self.zin, self.pair)
        k = self.z
        add_into(self.own, self.chunk(0, self.j, k), self.fl.at[k], self.fr.at[k])

    def end0(self, out):
        self.got("p", self.zin)
        add_into(out, self.own, self.zin)

    def relay1_far(self):
        self.got("zd", self.hz.at[self.jd])
        w = self.hw.at[self.jd]
        add_into(w, self.chunk(1, self.jd, self.z), self.hz.at[self.jd])
        self.send("hr", self.cut(w, 0), self.hrl, self.right)
        self.send("hl", self.cut(w, 1), self.hrr, self.left)

    def relay1_near(self):
        for way, j, h, ref, dev in (
            ("r", self.jr, 1, self.hfl, self.right), ("l", self.jl, 0, self.hfr, self.left)
        ):
            self.got("z" + way, self.hz.at[j])
            w = self.cut(self.hw.at[j], h)
            add_into(w, self.cut(self.chunk(1, j, self.z), h), self.cut(self.hz.at[j], h))
            self.send("i" + way, w, self.cut(ref, h), dev)

    def relay1_last(self):
        for way, j, h, inp, ref, dev in (
            ("r", self.jr, 0, self.hrl, self.hfl, self.right),
            ("l", self.jl, 1, self.hrr, self.hfr, self.left),
        ):
            self.got("h" + way, inp)
            w = self.cut(self.hw.at[j], h)
            add_into(w, self.cut(self.chunk(1, j, self.z), h), self.cut(self.hz.at[j], h), inp)
            self.send("k" + way, w, self.cut(ref, h), dev)

    def end1(self, out):
        self.got("z0", self.hz.at[self.j])
        self.got("ir", self.cut(self.hfl, 1))
        self.got("il", self.cut(self.hfr, 0))
        self.got("kr", self.cut(self.hfl, 0))
        self.got("kl", self.cut(self.hfr, 1))
        add_into(out, self.chunk(1, self.j, self.z), self.hz.at[self.j], self.hfl, self.hfr)

    def drain(self):
        for copy in self.sent:
            copy.wait_send()


HR = ROWS // 2
C_PIECE, C_HALF = (1, HR, W), (1, HR // 2, W)
H_PIECE, H_HALF = (NDP // 2, SLOT, W), (NDP // 4, SLOT, W)


def moe_kernel(
    ids_ref, logits_ref, x_hbm, dy_hbm, wg_hbm, wu_hbm, wd_hbm,
    back, backh, gback, mr, gg, gu, gd,
    *refs,
):
    e, d, x, zh, c, y, zl = place()
    c_refs, refs = refs[:17], refs[17:]
    h_refs, refs = refs[:17], refs[17:]
    (
        s1, s2, s3, ms, in_s, cold, extra, weights, acc, lhs, rhs, dxc, dxh, gp,
        rc, hs, hin, outh, hp, gall, gsum,
        st_s, st_r, sd_s, sd_r, m_s, m_r, sib_s, sib_r, dp_s, dp_r, ex_s, ex_r, xs_s, xs_r, loc,
        g_s, g_r, b_s, b_r, gb_s, gb_r, x_s, x_r, q_s, q_r,
    ) = refs
    wg, wu, wd = weights.at[0], weights.at[1], weights.at[2]
    FFL = weights.shape[1]
    dbar = y * 2 + 1 - zl
    sib = to(expert_at(x, zh, 1 - c), d)
    right, left, pair = to(e, ((y + 1) % 4) * 2 + zl), to(e, ((y + 3) % 4) * 2 + zl), to(e, dbar)
    x_r_dev, x_l_dev = to(expert_at((x + 1) % 4, zh, c), d), to(expert_at((x + 3) % 4, zh, c), d)
    z_p = to(expert_at(x, 1 - zh, c), dbar)
    peers, places, mine, parts = [expert_at(x, zh, 1 - c)], [1 - c], [c], [0]
    row_peers = []
    for here, seen, x2, zh2 in others(x, zh):
        for c2 in (0, 1):
            peers.append(expert_at(x2, zh2, c2))
            places.append(here * 2 + c2)
            mine.append(seen * 2 + c)
            parts.append(here // 4)
            d2 = d if here < 4 else dbar
            row_peers.append((here, seen, expert_at(x2, zh2, c2), d2, x2 * 2 + c2))
    dps = [(d + k) % NDP for k in range(1, NDP)]

    partners = (
        [to(e2, d) for e2 in peers] + [to(e, d2) for d2 in dps]
        + [to(p[2], dbar) for p in row_peers if p[0] >= 4]
    )
    barrier = pltpu.get_barrier_semaphore()
    for dev in partners:
        pl.semaphore_signal(barrier, inc=1, device_id=dev, device_id_type=MESH)

    R = ids_ref.shape[1]
    loads = [
        pltpu.make_async_copy(
            ref.at[:, j * W : (j + 1) * W], dxc.at[j, a * R : (a + 1) * R], in_s.at[a, j]
        )
        for a, ref in ((0, x_hbm), (1, dy_hbm))
        for j in range(NDP)
    ]
    loads += [
        pltpu.make_async_copy(ref, weights.at[i], loc.at[3 + i])
        for i, ref in enumerate((wg_hbm, wu_hbm, wd_hbm))
    ]
    for copy in loads:
        copy.start()
    ids = ids_ref[...]
    onehot, rank = row_facts(ids, E)
    maps = slot_maps(ids, rank)
    for copy in loads[: 2 * NDP]:
        copy.wait()
    for a in (0, 1):
        for g, chunk in ((0, d), (1, dbar)):
            block = dxc[chunk, a * R : (a + 1) * R, :]
            s1[a, g] = jnp.dot(maps[g], block, preferred_element_type=f32).astype(bf16)
    pl.semaphore_wait(barrier, len(partners))

    rest = []

    def send(src, dst, ssem, rsem, dev):
        copy = pltpu.make_async_remote_copy(
            src, dst, ssem, rsem, device_id=dev, device_id_type=MESH
        )
        copy.start()
        rest.append(copy)

    def wait(ref, ssem, rsem):
        pltpu.make_async_remote_copy(
            ref, ref, ssem, rsem, device_id=sib, device_id_type=MESH
        ).wait_recv()

    def slots_at(n):
        return pl.ds(pl.multiple_of(n * SLOT, SLOT), SLOT)

    for a in (0, 1):
        for here, seen, e2, d2, q in row_peers:
            if a == 0 and here in (1, 2):
                continue
            pltpu.make_async_remote_copy(
                s1.at[a, here // 4, slots_at(q), :], cold.at[a, d2, slots_at(seen * 2 + c), :],
                st_s.at[a], st_r.at[a], device_id=to(e2, d2), device_id_type=MESH,
            ).start()
    def lay(j, _):
        got = jnp.dot(maps[2], dxc[j, 0:R, :], preferred_element_type=f32).astype(bf16)
        s2[0, j] = got[: 3 * SLOT]
        s3[j] = got[3 * SLOT :]
        got = jnp.dot(maps[2][: 3 * SLOT], dxc[j, R : 2 * R, :], preferred_element_type=f32)
        s2[1, j] = got.astype(bf16)
        return 0

    lax.fori_loop(0, NDP, lay, 0)
    send(s2.at[:, :, SLOT : 2 * SLOT, :], cold.at[:, :, slots_at(c), :], sib_s, sib_r, sib)

    def dp_piece(a, j, z, h):
        start = (3 if a == 0 else 1) * 2 * SLOT
        half = (ROWS - start) // 2
        rows = {None: (start, 2 * half), 0: (start, half), 1: (start + half, half)}[h]
        return cold.at[a, j * 2 + z, pl.ds(*rows), :]

    def ex_piece_of(core):
        def piece(a, j, z, h):
            chunks = {None: (0, NDP), 0: (0, NDP // 2), 1: (NDP // 2, NDP // 2)}[h]
            return extra.at[a, pl.ds(*chunks), slots_at(expert_at(j, z, core)), :]
        return piece

    ex_piece, ex_other = ex_piece_of(c), ex_piece_of(1 - c)
    dp = Gather(
        lambda a: dp_piece(a, y, zl, None), dp_piece, y, zl, right, left, pair, dp_s, dp_r
    )
    ex = Gather(
        lambda a: s2.at[a, :, 2 * SLOT :, :], ex_piece, x, zh, x_r_dev, x_l_dev, z_p, ex_s, ex_r
    )
    C = Scatter(
        lambda a, j, z: dxc.at[pl.ds(j * 2 + z, 1), pl.ds(a * HR, HR)],
        lambda ref, h: ref.at[:, pl.ds(h * (HR // 2), HR // 2)],
        y, zl, right, left, pair, c_refs,
    )
    X = Scatter(
        lambda a, j, z: hs.at[j * 2 + z, pl.ds(a * (NDP // 2), NDP // 2)],
        lambda ref, h: ref.at[pl.ds(h * (NDP // 4), NDP // 4)],
        x, zh, x_r_dev, x_l_dev, z_p, h_refs,
    )
    shares = []

    def share(a, j, z, src=None):
        i = len(shares)
        dst = ex_piece(a, j, z, None)
        send(dst if src is None else src, dst, xs_s.at[i], xs_r.at[i], sib)
        shares.append((a, j, z))

    def whole(a):
        ref = dp_piece(a, y, zl, None)
        return pltpu.make_async_remote_copy(
            ref, ref, st_s.at[a], st_r.at[a], device_id=sib, device_id_type=MESH
        )

    def cols(j):
        return pl.ds(pl.multiple_of(j * W, W), W)

    def forward_x(rows, t, at, n):
        def step(i, _):
            j = at(i)
            xj = rows[0, j]
            acc[t, 0] += nt(wg[:, cols(j)], xj)
            acc[t, 1] += nt(wu[:, cols(j)], xj)
            return 0

        lax.fori_loop(0, n, step, 0)

    def forward_dy(rows, t, at, n):
        def step(i, _):
            j = at(i)
            acc[t, 2] += nt(wd[:, cols(j)], rows[1, j])
            return 0

        lax.fori_loop(0, n, step, 0)

    def between(t):
        gate = gate_row(mr, t)
        pre, up, g = acc[t, 0], acc[t, 1], acc[t, 2]
        s = sigmoid(pre)
        active = pre * s
        hidden = (active * up).astype(bf16).astype(f32)
        gp[0:1, t * ROWS : (t + 1) * ROWS] = jnp.sum(hidden * g, axis=0, keepdims=True)
        gh = g * gate
        d_up = gh * active
        d_pre = gh * up * s * (1.0 + pre * (1.0 - s))
        lhs[t, 0] = d_pre.astype(bf16)
        lhs[t, 1] = d_up.astype(bf16)
        lhs[t, 2] = (hidden * gate).astype(bf16)
        rhs[t, :, 0:FFL] = d_pre.T.astype(bf16)
        rhs[t, :, FFL : 2 * FFL] = d_up.T.astype(bf16)

    def rows_back(t, out, at, n):
        def step(i, _):
            j = at(i)
            r = jnp.dot(rhs[t, :, 0:FFL], wg[:, cols(j)], preferred_element_type=f32)
            r += jnp.dot(rhs[t, :, FFL : 2 * FFL], wu[:, cols(j)], preferred_element_type=f32)
            out[j] = r.astype(bf16)
            return 0

        lax.fori_loop(0, n, step, 0)

    outs = (gg, gu, gd)

    def weights_back(first, sq):
        def step(j, sq):
            for i in range(3):
                v = jnp.dot(lhs[0, i], cold[i // 2, j], preferred_element_type=f32)
                v += jnp.dot(lhs[1, i], extra[i // 2, j], preferred_element_type=f32)
                outs[i][:, cols(j)] = v
                sq = sq + jnp.sum((v * v).reshape(-1, 8, W), axis=0)
            return sq

        return lax.fori_loop(first, first + 2, step, sq)

    ex.start(1)
    ex.start(0)
    for i, (x2, seen) in enumerate((((x + 1) % 4, 2), ((x + 3) % 4, 1))):
        for c2 in (0, 1):
            send(
                s3.at[:, pl.ds((i * 2 + c2) * SLOT, SLOT), :],
                cold.at[0, :, slots_at(seen * 2 + c), :],
                sd_s.at[i * 2 + c2], sd_r.at[(seen - 1) * 2 + c], to(expert_at(x2, zh, c2), d),
            )
    share(0, x, zh, s2.at[0, :, 2 * SLOT :, :])
    share(1, x, zh, s2.at[1, :, 2 * SLOT :, :])
    fill_meta(ms, ids, logits_ref[...], onehot, rank)
    meta_peers = row_peers + [(0, 0, expert_at(x, zh, 1 - c), d, 0)]
    for n, (_, seen, e2, d2, _) in enumerate(meta_peers):
        send(ms.at[e2], mr.at[seen * 2 + c], m_s.at[n], m_r.at[seen * 2 + c], to(e2, d2))
    own_in = [
        pltpu.make_async_copy(s2.at[:, :, 0:SLOT, :], cold.at[:, :, slots_at(c), :], loc.at[0]),
        pltpu.make_async_copy(s2.at[:, :, 2 * SLOT :, :], extra.at[:, :, slots_at(e), :], loc.at[1]),
        pltpu.make_async_copy(ms.at[e], mr.at[c], loc.at[2]),
    ]
    for copy in own_in:
        copy.start()
    acc[...] = jnp.zeros_like(acc)
    whole(0).wait_recv()
    dp.start(0)
    whole(1).wait_recv()
    dp.start(1)
    for copy in own_in + loads[2 * NDP :]:
        copy.wait()
    wait(cold.at[:, :, slots_at(1 - c), :], sib_s, sib_r)
    forward_dy(cold, 0, lambda i: d, 1)
    ex.s2()
    ex.s3()
    dp.s2()
    dp.s3()
    ex.s4()
    ex.s5()
    ex.s6()
    for a, j, z in ((0, ex.jl, zh), (0, ex.jr, zh), (1, x, 1 - zh), (1, ex.jl, zh), (1, ex.jr, zh)):
        share(a, j, z)
    dp.s4()
    dp.s5()
    dp.s6()
    for i in range(4):
        wait(cold.at[0, :, pl.ds((2 + i) * SLOT, SLOT), :], sd_s.at[0], sd_r.at[i])
    ex.s7()
    ex.s8()
    share(0, ex.jd, zh)
    dp.s7()
    dp.s8()
    forward_x(cold, 0, lambda i: d, 1)
    forward_x(cold, 0, lambda i: ((y + 1 + 2 * i) % 4) * 2 + zl, 2)
    ex.s9()
    ex.s10()
    share(1, ex.jl, 1 - zh)
    share(1, ex.jr, 1 - zh)
    dp.s9()
    dp.s10()
    forward_dy(cold, 0, lambda i: ((y + 1 + 2 * i) % 4) * 2 + zl, 2)
    forward_dy(cold, 0, lambda i: dbar, 1)
    dp.got("0oz", 0, y, 1 - zl, None)
    forward_x(cold, 0, lambda i: i * (dp.jd * 2 + zl) + (1 - i) * dbar, 2)
    ex.got("0oz", 0, x, 1 - zh, None)
    share(0, x, 1 - zh)
    ex.got("0lz", 0, ex.jl, 1 - zh, None)
    share(0, ex.jl, 1 - zh)
    ex.got("0rz", 0, ex.jr, 1 - zh, None)
    share(0, ex.jr, 1 - zh)
    ex.end_of_1_d()
    share(1, ex.jd, zh)
    ex.end_of_1_e()
    share(1, ex.jd, 1 - zh)
    ex.end_of_0_d()
    share(0, ex.jd, 1 - zh)
    forward_dy(cold, 0, lambda i: ((y + 1 + 2 * i) % 4) * 2 + 1 - zl, 2)
    for i in [1 - c] + list(range(2, E)):
        wait(mr.at[i], m_s.at[0], m_r.at[i])
    dp.end_of_1_d()
    forward_dy(cold, 0, lambda i: dp.jd * 2 + zl, 1)
    dp.got("0lz", 0, dp.jl, 1 - zl, None)
    dp.got("0rz", 0, dp.jr, 1 - zl, None)
    forward_x(cold, 0, lambda i: ((y + 1 + 2 * i) % 4) * 2 + 1 - zl, 2)
    dp.end_of_1_e()
    forward_dy(cold, 0, lambda i: dp.jd * 2 + 1 - zl, 1)
    dp.end_of_0_d()
    forward_x(cold, 0, lambda i: dp.jd * 2 + 1 - zl, 1)
    between(0)

    rows_back(0, dxc, lambda i: C.jd * 2 + i, 2)
    C.start0_far()
    C.start1("d")
    rows_back(0, dxc, lambda i: C.jr * 2 + i, 2)
    C.start0_right()
    C.start1("r")
    rows_back(0, dxc, lambda i: C.jl * 2 + i, 2)
    C.start0_left()
    C.start1("l")
    rows_back(0, dxc, lambda i: y * 2 + i, 2)
    C.start1("0")
    for i, where in enumerate(shares):
        wait(ex_other(*where, None), xs_s.at[i], xs_r.at[i])
    forward_x(extra, 1, lambda i: i, NDP)
    forward_dy(extra, 1, lambda i: i, NDP)
    C.relay0()
    C.relay1_far()
    between(1)
    far = [X.jd * 2, X.jd * 2 + 1, X.jr * 2, X.jl * 2, X.jr * 2 + 1, X.jl * 2 + 1, x * 2, x * 2 + 1]
    rows_back(1, dxh, lambda i: i, NDP)

    def h_rows(chip, core):
        return slots_at(chip * 2 + core)

    for i, chip in enumerate(far):
        send(dxh.at[:, h_rows(chip, 1 - c)], hin.at[chip], x_s.at[i], x_r.at[i], sib)
    C.relay1_near()
    for i, chip in enumerate(far):
        wait(hin.at[chip], x_s.at[i], x_r.at[i])
        add_into(hs.at[chip], dxh.at[:, h_rows(chip, c)], hin.at[chip])
        if i == 1:
            X.start0_far()
        if i == 5:
            X.start0_right()
            X.start0_left()
    for way in ("d", "r", "l", "0"):
        X.start1(way)
    C.pair0()
    C.relay1_last()
    sq = weights_back(0, jnp.zeros((8, W), f32))
    X.relay0()
    X.relay1_far()
    X.relay1_near()
    sq = weights_back(2, sq)
    X.relay1_last()
    X.pair0()
    sq = weights_back(4, sq)

    def give(a):
        for n, e2 in enumerate(peers):
            if parts[n] == a:
                send(
                    rc.at[0, slots_at(places[n]), :],
                    back.at[e], b_s.at[n], b_r.at[mine[n]], to(e2, d),
                )

    sq = weights_back(6, sq)
    total = jnp.sum(jnp.sum(sq, axis=0, keepdims=True), axis=1, keepdims=True)
    gp[0:1, 2 * ROWS :] = jnp.broadcast_to(total, (1, GW - 2 * ROWS))
    for k, d2 in enumerate(dps):
        send(gp, gall.at[d], g_s.at[k], g_r.at[k], to(e, d2))
    gall[d] = gp[...]
    C.end1(rc.at[:, pl.ds(HR, HR)])
    give(1)
    C.end0(rc.at[:, pl.ds(0, HR)])
    give(0)
    back[e] = rc[0, slots_at(c), :]
    X.end1(outh.at[pl.ds(NDP // 2, NDP // 2)])
    X.end0(outh.at[pl.ds(0, NDP // 2)])
    for k, d2 in enumerate(dps):
        send(outh.at[d2], hp.at[d], q_s.at[k], q_r.at[k], to(e, d2))
    hp[d] = outh[d]
    for k in range(NDP - 1):
        wait(gall.at[(d + NDP - 1 - k) % NDP], g_s.at[k], g_r.at[k])
    total = gall[0]
    for k in range(1, NDP):
        total = total + gall[k]
    gsum[...] = total
    gback[e] = total
    for n, e2 in enumerate(peers):
        send(gsum, gback.at[e], gb_s.at[n], gb_r.at[mine[n]], to(e2, d))
    for k in range(NDP - 1):
        wait(hp.at[(d + NDP - 1 - k) % NDP], q_s.at[k], q_r.at[k])
    total = hp[0].astype(f32)
    for k in range(1, NDP):
        total = total + hp[k].astype(f32)
    backh[...] = total.astype(bf16)

    for i in [1 - c] + list(range(2, E)):
        wait(back.at[0], b_s.at[0], b_r.at[i])
        wait(gback.at[0], gb_s.at[0], gb_r.at[i])
    whole(0).wait_send()
    whole(1).wait_send()
    for copy in rest:
        copy.wait_send()
    dp.drain()
    ex.drain()
    C.drain()
    X.drain()


def moe(ids, logits, x, dy, wg, wu, wd):
    FFL, width = wg.shape
    D = pltpu.SemaphoreType.DMA
    V = pltpu.VMEM
    return pl.pallas_call(
        moe_kernel,
        in_specs=[VM, VM] + [ANY] * 5,
        out_specs=[VM] * 7,
        out_shape=[
            pltpu.VMEM((E, SLOT, W), bf16),
            pltpu.VMEM((SLOT, W), bf16),
            pltpu.VMEM((E, 1, GW), f32),
            pltpu.VMEM((E, 8, 128), f32),
        ]
        + [pltpu.VMEM((FFL, width), f32)] * 3,
        scratch_shapes=Scatter.scratch(C_PIECE, C_HALF)
        + Scatter.scratch(H_PIECE, H_HALF)
        + [
            V((2, 2, ROWS // 2, W), bf16), V((2, NDP, 3 * SLOT, W), bf16),
            V((NDP, 4 * SLOT, W), bf16), V((E, 8, 128), f32), D((2, NDP)),
            V((2, NDP, ROWS, W), bf16), V((2, NDP, ROWS, W), bf16),
            V((3, FFL, width), bf16),
            V((2, 3, FFL, ROWS), f32), V((2, 3, FFL, ROWS), bf16), V((2, ROWS, 2 * FFL), bf16),
            V((NDP, ROWS, W), bf16), V((NDP, ROWS, W), bf16), V((1, GW), f32),
            V((1, ROWS, W), bf16),
            V((NDP, NDP, SLOT, W), bf16), V((NDP, NDP, SLOT, W), bf16),
            V((NDP, SLOT, W), bf16), V((NDP, SLOT, W), bf16),
            V((NDP, 1, GW), f32), V((1, GW), f32),
            D((2,)), D((2,)), D((4,)), D((4,)), D((15,)), D((16,)), D, D,
            D((18,)), D((18,)), D((18,)), D((18,)), D((16,)), D((16,)), D((6,)),
            D((7,)), D((7,)), D((15,)), D((16,)), D((15,)), D((16,)),
            D((8,)), D((8,)), D((7,)), D((7,)),
        ],
        compiler_params=pltpu.CompilerParams(
            collective_id=1, has_side_effects=True, vmem_limit_bytes=54 * 1024 * 1024
        ),
        name="moe",
    )(ids, logits, x, dy, wg, wu, wd)


def finish_kernel(
    ids_ref, logits_ref, back, backh, gback, mr, g1, g2, g3,
    rows_ref, gl_ref, norm_ref, o1, o2, o3, osem,
):
    stores = [
        pltpu.make_async_copy(g, o, osem.at[i])
        for i, (g, o) in enumerate(((g1, o1), (g2, o2), (g3, o3)))
    ]
    for copy in stores:
        copy.start()
    finish_rows(ids_ref, logits_ref, back, backh, gback, mr, rows_ref, gl_ref, norm_ref)
    for copy in stores:
        copy.wait()


def finish_rows(ids_ref, logits_ref, back, backh, gback, mr, rows_ref, gl_ref, norm_ref):
    e, _, x, zh, c, _, _ = place()
    ids = ids_ref[...]
    onehot, rank = row_facts(ids, E)
    probs = soft(logits_ref[...])
    n = ids.shape[1]
    first = rank < SLOT
    slot = lax.broadcasted_iota(jnp.int32, (ROWS, n), 0)
    pick = (slot == jnp.where(first, ids * SLOT + rank, -1)).astype(f32).astype(bf16)
    slot = lax.broadcasted_iota(jnp.int32, (SLOT, n), 0)
    pickh = (slot == rank - SLOT).astype(f32).astype(bf16)
    got = tn(pick, back[...].reshape(ROWS, W)) + tn(pickh, backh[...])
    rows_ref[...] = got.astype(bf16)
    rel = seen_from(ids, x, zh, c)
    lane = jnp.where(first, rel * SLOT + rank, ROWS + e * SLOT + rank - SLOT)
    slot = lax.broadcasted_iota(jnp.int32, (2 * ROWS, n), 0)
    here = (slot == lane).astype(f32).astype(bf16)
    found = jnp.dot(gback[:, 0, 0 : 2 * ROWS].astype(bf16), here, preferred_element_type=f32)
    dgate = jnp.sum(onehot * found, axis=0, keepdims=True)
    count = jnp.sum(mr[...], axis=0)[2:3, :]
    across = lax.broadcasted_iota(jnp.int32, (E, 128), 0)
    diag = across == lax.broadcasted_iota(jnp.int32, (E, 128), 1)
    column = jnp.sum(jnp.where(diag, jnp.broadcast_to(count, (E, 128)), 0.0), axis=1, keepdims=True)
    pulls = onehot * dgate + 1.0 * E * (column / (E * n))
    gl_ref[...] = probs * (pulls - jnp.sum(probs * pulls, axis=0, keepdims=True))
    norm_ref[...] = jnp.sqrt(jnp.sum(gback[:, 0, 2 * ROWS : 2 * ROWS + 128], axis=0, keepdims=True))


def finish(ids, logits, back, backh, gback, mr, *grads):
    n = ids.shape[1]
    return pl.pallas_call(
        finish_kernel,
        in_specs=[VM] * 9,
        out_specs=[VM] * 3 + [ANY] * 3,
        out_shape=[
            jax.ShapeDtypeStruct((n, W), bf16),
            jax.ShapeDtypeStruct((E, n), f32),
            jax.ShapeDtypeStruct((1, 128), f32),
        ]
        + [jax.ShapeDtypeStruct(g.shape, f32) for g in grads],
        scratch_shapes=[
            pltpu.SemaphoreType.DMA((3,)),
        ],
        compiler_params=pltpu.CompilerParams(vmem_limit_bytes=20 * 1024 * 1024),
        name="finish",
    )(ids, logits, back, backh, gback, mr, *grads)


def local(rows_x, rows_dy, router_logits, expert_of, w_gate, w_up, w_down):
    ids = expert_of.reshape(1, -1)
    logits = router_logits.T
    back, backh, gback, mr, gg, gu, gd = moe(
        ids, logits, rows_x, rows_dy, w_gate[0], w_up[0], w_down[0]
    )
    held = (back, backh, gback, mr, gg, gu, gd)
    held = [pltpu.with_memory_space_constraint(v, pltpu.VMEM) for v in held]
    grad_rows, grad_logits, norm, gg, gu, gd = finish(ids, logits, *held)
    return grad_rows, grad_logits.T, gg[None], gu[None], gd[None], norm[0, 0]


def solution(mesh):
    rows = P("expert", None)
    weights = P("expert", "dp", None)
    return jax.shard_map(
        local,
        mesh=mesh,
        in_specs=(rows, rows, rows, rows, weights, weights, weights),
        out_specs=(P("expert", "dp"), rows, weights, weights, weights, P()),
        check_vma=False,
    )
```

```python
import jax
import jax.numpy as jnp
from jax import lax
from jax.experimental import pallas as pl
from jax.experimental.pallas import tpu as pltpu
from jax.sharding import PartitionSpec as P

f32 = jnp.float32
bf16 = jnp.bfloat16
MESH = pl.DeviceIdType.MESH
ANY = pl.BlockSpec(memory_space=pl.ANY)
VM = pl.BlockSpec(memory_space=pltpu.VMEM)
SM = pl.BlockSpec(memory_space=pltpu.SMEM)

E = 16
NDP = 8
SLOT = 32
W = 512
ROWS = E * SLOT
LOCAL = 2 * SLOT
GW = 1280


def place():
    e = lax.axis_index("expert")
    d = lax.axis_index("dp")
    return e, d, e // 4, (e // 2) % 2, e % 2, d // 2, d % 2


def expert_at(x, zh, c):
    return (x * 2 + zh) * 2 + c


def to(e, d):
    return {"expert": e, "dp": d}


def row_facts(ids, experts):
    rows = ids.shape[1]
    onehot = (lax.broadcasted_iota(jnp.int32, (experts, rows), 0) == ids).astype(f32)
    before = lax.broadcasted_iota(jnp.int32, (rows, rows), 0) < lax.broadcasted_iota(
        jnp.int32, (rows, rows), 1
    )
    earlier = jnp.dot(onehot.astype(bf16), before.astype(bf16), preferred_element_type=f32)
    rank = jnp.sum(onehot * earlier, axis=0, keepdims=True).astype(jnp.int32)
    return onehot, rank


def soft(logits):
    top = jnp.max(logits, axis=0, keepdims=True)
    ex = jnp.exp(logits - top)
    return ex / jnp.sum(ex, axis=0, keepdims=True)


def nt(a, b):
    return lax.dot_general(a, b, (((1,), (1,)), ((), ())), preferred_element_type=f32)


def tn(a, b):
    return lax.dot_general(a, b, (((0,), (0,)), ((), ())), preferred_element_type=f32)


def seen_from(ids, x, zh, c):
    dx = (x - (ids >> 2)) & 3
    return ((dx ^ (dx >> 1)) + 4 * (zh ^ ((ids >> 1) & 1))) * 2 + c


def permute(slots, target):
    slot = lax.broadcasted_iota(jnp.int32, (slots, target.shape[1]), 0)
    return (slot == target).astype(f32).astype(bf16)


def slot_maps(ids, rank):
    e, _, x, zh, c, _, _ = place()
    far = (zh ^ ((ids >> 1) & 1)) == 1
    near = jnp.logical_not(far)
    first = rank < SLOT
    chip = ((ids >> 2) * 2 + (ids & 1)) * SLOT + rank
    maps = [permute(ROWS // 2, jnp.where(first & ours, chip, -1)) for ours in (near, far)]
    home = jnp.where(ids == e, rank, jnp.where(ids == e + 1 - 2 * c, SLOT + rank, -1))
    dx = ((ids >> 2) - x) & 3
    side = (3 + (dx & 2) + (ids & 1)) * SLOT + rank
    home = jnp.where(((dx & 1) == 1) & near, side, home)
    return maps + [permute(7 * SLOT, jnp.where(first, home, SLOT + rank))]


def fill_meta(m_ref, ids, logits, onehot, rank):
    e, _, x, zh, c, _, _ = place()
    rows = ids.shape[1]
    first = rank < SLOT
    gate = jnp.sum(soft(logits) * onehot, axis=0, keepdims=True).astype(bf16).astype(f32)
    lane = lax.broadcasted_iota(jnp.int32, (128, rows), 0)
    spot = (seen_from(ids, x, zh, c) & 3) * SLOT + rank
    cold = (onehot * gate * first.astype(f32)).astype(bf16)
    cold = nt(cold, (lane == spot).astype(f32).astype(bf16))
    gate8 = jnp.broadcast_to(gate, (8, rows)).astype(bf16)
    spot = jnp.where(first, -1, (e & 3) * SLOT + rank - SLOT)
    hot = nt(gate8, (lane == spot).astype(f32).astype(bf16))
    count = nt(jnp.ones((8, rows), bf16), (lane == ids).astype(f32).astype(bf16))
    line = lax.broadcasted_iota(jnp.int32, (8, 128), 0)
    for k in range(E):
        mine = jnp.broadcast_to(cold[k : k + 1, :], (8, 128))
        busy = (jnp.sum(onehot[k : k + 1, :], axis=1, keepdims=True) > SLOT).astype(f32)
        rest = jnp.where(line == 2, count, jnp.broadcast_to(busy, (8, 128)))
        m_ref[k] = jnp.where(line == 0, mine, jnp.where(line == 1, hot, rest))


class Gather:
    names = (
        "0oz", "0or", "0ol", "0lr", "0lz", "0rl", "0rz", "0dz", "0ez",
        "1oz", "1or", "1ol", "1zr", "1zl", "1lr", "1kr", "1rl", "1ql",
    )

    def __init__(self, own, piece, j, z, right, left, pair, ssem, rsem):
        self.own, self.piece, self.ssem, self.rsem = own, piece, ssem, rsem
        self.j, self.z = j, z
        self.jl, self.jr, self.jd = (j + 3) % 4, (j + 1) % 4, (j + 2) % 4
        self.right, self.left, self.pair = right, left, pair
        self.sent = []

    def send(self, name, src, dst, dev):
        i = self.names.index(name)
        copy = pltpu.make_async_remote_copy(
            src, dst, self.ssem.at[i], self.rsem.at[i], device_id=dev, device_id_type=MESH
        )
        copy.start()
        self.sent.append(copy)

    def pass_on(self, name, dev, *where):
        ref = self.piece(*where)
        self.send(name, ref, ref, dev)

    def got(self, name, *where):
        i = self.names.index(name)
        ref = self.piece(*where)
        pltpu.make_async_remote_copy(
            ref, ref, self.ssem.at[i], self.rsem.at[i], device_id=self.pair, device_id_type=MESH
        ).wait_recv()

    def start(self, a):
        for way, dev in (("z", self.pair), ("r", self.right), ("l", self.left)):
            self.send(f"{a}o{way}", self.own(a), self.piece(a, self.j, self.z, None), dev)

    def s2(self):
        self.got("0or", 0, self.jl, self.z, None)
        self.pass_on("0lr", self.right, 0, self.jl, self.z, 0)
        self.pass_on("0lz", self.pair, 0, self.jl, self.z, None)

    def s3(self):
        self.got("0ol", 0, self.jr, self.z, None)
        self.pass_on("0rl", self.left, 0, self.jr, self.z, 1)
        self.pass_on("0rz", self.pair, 0, self.jr, self.z, None)

    def s4(self):
        self.got("1oz", 1, self.j, 1 - self.z, None)
        self.pass_on("1zr", self.right, 1, self.j, 1 - self.z, None)
        self.pass_on("1zl", self.left, 1, self.j, 1 - self.z, None)

    def s5(self):
        self.got("1or", 1, self.jl, self.z, None)
        self.pass_on("1lr", self.right, 1, self.jl, self.z, 0)

    def s6(self):
        self.got("1ol", 1, self.jr, self.z, None)
        self.pass_on("1rl", self.left, 1, self.jr, self.z, 1)

    def s7(self):
        self.got("0lr", 0, self.jd, self.z, 0)
        self.pass_on("0dz", self.pair, 0, self.jd, self.z, 0)

    def s8(self):
        self.got("0rl", 0, self.jd, self.z, 1)
        self.pass_on("0ez", self.pair, 0, self.jd, self.z, 1)

    def s9(self):
        self.got("1zr", 1, self.jl, 1 - self.z, None)
        self.pass_on("1kr", self.right, 1, self.jl, 1 - self.z, 0)

    def s10(self):
        self.got("1zl", 1, self.jr, 1 - self.z, None)
        self.pass_on("1ql", self.left, 1, self.jr, 1 - self.z, 1)

    def end_of_1_d(self):
        self.got("1lr", 1, self.jd, self.z, 0)
        self.got("1rl", 1, self.jd, self.z, 1)

    def end_of_1_e(self):
        self.got("1kr", 1, self.jd, 1 - self.z, 0)
        self.got("1ql", 1, self.jd, 1 - self.z, 1)

    def end_of_0_d(self):
        self.got("0dz", 0, self.jd, 1 - self.z, 0)
        self.got("0ez", 0, self.jd, 1 - self.z, 1)

    def drain(self):
        for copy in self.sent:
            copy.wait_send()


def others(x, zh):
    order = (0, 1, 3, 2)
    for k in range(1, 8):
        dx, dz = k // 2, k % 2
        yield order[dx] + 4 * dz, order[(4 - dx) % 4] + 4 * dz, (x + dx) % 4, (zh + dz) % 2


def sigmoid(v):
    return 1.0 / (1.0 + jnp.exp(-v))


def gate_row(mr, t):
    _, _, x, _, c, _, _ = place()
    parts = []
    for g in range(E // 4):
        dx = (g + 4 - x) % 4
        at = g * 4 if t == 0 else (dx + dx // 2 - 2 * (dx // 3)) * 2
        part = mr[at, t : t + 1, :]
        for i in (1, 2, 3) if t == 0 else (1, 8, 9):
            part = part + mr[at + i, t : t + 1, :]
        parts.append(part if t == 0 else part * mr[c, 3:4, :])
    return jnp.concatenate(parts, axis=1)


def add_into(out, *terms):
    n, rows, _ = out.shape
    step_rows = min(rows, 64)
    for i in range(n):

        def step(k, _):
            r = pl.ds(pl.multiple_of(k * step_rows, step_rows), step_rows)
            total = terms[0][i, r, :].astype(f32)
            for term in terms[1:]:
                total = total + term[i, r, :].astype(f32)
            out[i, r, :] = total.astype(out.dtype)
            return 0

        if rows == step_rows:
            step(0, 0)
        else:
            lax.fori_loop(0, rows // step_rows, step, 0)


class Scatter:
    names = (
        "ar0", "ar1", "al0", "al1", "br0", "br1", "bl0", "bl1", "cr0", "cr1", "cl0", "cl1", "p",
        "zd", "zr", "zl", "z0", "hr", "hl", "ir", "il", "kr", "kl",
    )

    @staticmethod
    def scratch(piece, half):
        V = pltpu.VMEM
        return [
            V((2,) + half, bf16), V((2,) + half, bf16), V((2,) + half, bf16), V((2,) + half, bf16),
            V((2,) + piece, bf16), V((2,) + piece, bf16),
            V(piece, bf16), V(piece, bf16), V(piece, f32),
            V((4,) + piece, bf16), V((4,) + piece, bf16),
            V(half, bf16), V(half, bf16), V(piece, bf16), V(piece, bf16),
            pltpu.SemaphoreType.DMA((23,)), pltpu.SemaphoreType.DMA((23,)),
        ]

    def __init__(self, chunk, cut, j, z, right, left, pair, refs):
        self.chunk, self.cut, self.j, self.z = chunk, cut, j, z
        self.jl, self.jr, self.jd = (j + 3) % 4, (j + 1) % 4, (j + 2) % 4
        self.right, self.left, self.pair = right, left, pair
        (
            self.rl, self.rr, self.tr, self.tl, self.fl, self.fr, self.zs, self.zin, self.own,
            self.hz, self.hw, self.hrl, self.hrr, self.hfl, self.hfr, self.ssem, self.rsem,
        ) = refs
        self.sent = []

    def send(self, name, src, dst, dev):
        i = self.names.index(name)
        copy = pltpu.make_async_remote_copy(
            src, dst, self.ssem.at[i], self.rsem.at[i], device_id=dev, device_id_type=MESH
        )
        copy.start()
        self.sent.append(copy)

    def got(self, name, ref):
        i = self.names.index(name)
        pltpu.make_async_remote_copy(
            ref, ref, self.ssem.at[i], self.rsem.at[i], device_id=self.pair, device_id_type=MESH
        ).wait_recv()

    def start0_far(self):
        for k in (0, 1):
            far = self.chunk(0, self.jd, k)
            self.send(f"ar{k}", self.cut(far, 0), self.rl.at[k], self.right)
            self.send(f"al{k}", self.cut(far, 1), self.rr.at[k], self.left)

    def start0_right(self):
        for k in (0, 1):
            right = self.chunk(0, self.jr, k)
            self.send(f"br{k}", self.cut(right, 1), self.cut(self.fl.at[k], 1), self.right)

    def start0_left(self):
        for k in (0, 1):
            left = self.chunk(0, self.jl, k)
            self.send(f"bl{k}", self.cut(left, 0), self.cut(self.fr.at[k], 0), self.left)

    def start1(self, way):
        j = {"d": self.jd, "r": self.jr, "l": self.jl, "0": self.j}[way]
        self.send("z" + way, self.chunk(1, j, 1 - self.z), self.hz.at[j], self.pair)

    def relay0(self):
        for k in (0, 1):
            self.got(f"ar{k}", self.rl.at[k])
            add_into(self.tr.at[k], self.cut(self.chunk(0, self.jr, k), 0), self.rl.at[k])
            self.send(f"cr{k}", self.tr.at[k], self.cut(self.fl.at[k], 0), self.right)
            self.got(f"al{k}", self.rr.at[k])
            add_into(self.tl.at[k], self.cut(self.chunk(0, self.jl, k), 1), self.rr.at[k])
            self.send(f"cl{k}", self.tl.at[k], self.cut(self.fr.at[k], 1), self.left)

    def pair0(self):
        for k in (0, 1):
            for n, ref, h in (("br", self.fl, 1), ("bl", self.fr, 0), ("cr", self.fl, 0), ("cl", self.fr, 1)):
                self.got(f"{n}{k}", self.cut(ref.at[k], h))
        k = 1 - self.z
        add_into(self.zs, self.chunk(0, self.j, k), self.fl.at[k], self.fr.at[k])
        self.send("p", self.zs, self.zin, self.pair)
        k = self.z
        add_into(self.own, self.chunk(0, self.j, k), self.fl.at[k], self.fr.at[k])

    def end0(self, out):
        self.got("p", self.zin)
        add_into(out, self.own, self.zin)

    def relay1_far(self):
        self.got("zd", self.hz.at[self.jd])
        w = self.hw.at[self.jd]
        add_into(w, self.chunk(1, self.jd, self.z), self.hz.at[self.jd])
        self.send("hr", self.cut(w, 0), self.hrl, self.right)
        self.send("hl", self.cut(w, 1), self.hrr, self.left)

    def relay1_near(self):
        for way, j, h, ref, dev in (
            ("r", self.jr, 1, self.hfl, self.right), ("l", self.jl, 0, self.hfr, self.left)
        ):
            self.got("z" + way, self.hz.at[j])
            w = self.cut(self.hw.at[j], h)
            add_into(w, self.cut(self.chunk(1, j, self.z), h), self.cut(self.hz.at[j], h))
            self.send("i" + way, w, self.cut(ref, h), dev)

    def relay1_last(self):
        for way, j, h, inp, ref, dev in (
            ("r", self.jr, 0, self.hrl, self.hfl, self.right),
            ("l", self.jl, 1, self.hrr, self.hfr, self.left),
        ):
            self.got("h" + way, inp)
            w = self.cut(self.hw.at[j], h)
            add_into(w, self.cut(self.chunk(1, j, self.z), h), self.cut(self.hz.at[j], h), inp)
            self.send("k" + way, w, self.cut(ref, h), dev)

    def end1(self, out):
        self.got("z0", self.hz.at[self.j])
        self.got("ir", self.cut(self.hfl, 1))
        self.got("il", self.cut(self.hfr, 0))
        self.got("kr", self.cut(self.hfl, 0))
        self.got("kl", self.cut(self.hfr, 1))
        add_into(out, self.chunk(1, self.j, self.z), self.hz.at[self.j], self.hfl, self.hfr)

    def drain(self):
        for copy in self.sent:
            copy.wait_send()


HR = ROWS // 2
C_PIECE, C_HALF = (1, HR, W), (1, HR // 2, W)
H_PIECE, H_HALF = (NDP // 2, SLOT, W), (NDP // 4, SLOT, W)


def moe_kernel(
    ids_ref, logits_ref, x_hbm, dy_hbm, wg_hbm, wu_hbm, wd_hbm,
    back, backh, gback, mr, gg, gu, gd,
    *refs,
):
    e, d, x, zh, c, y, zl = place()
    c_refs, refs = refs[:17], refs[17:]
    h_refs, refs = refs[:17], refs[17:]
    (
        s1, s2, s3, ms, in_s, cold, extra, weights, acc, lhs, rhs, dxc, dxh, gp,
        rc, hs, hin, outh, hp, gall, gsum,
        st_s, st_r, sd_s, sd_r, m_s, m_r, sib_s, sib_r, dp_s, dp_r, ex_s, ex_r, xs_s, xs_r, loc,
        g_s, g_r, b_s, b_r, gb_s, gb_r, x_s, x_r, q_s, q_r,
    ) = refs
    wg, wu, wd = weights.at[0], weights.at[1], weights.at[2]
    FFL = weights.shape[1]
    dbar = y * 2 + 1 - zl
    sib = to(expert_at(x, zh, 1 - c), d)
    right, left, pair = to(e, ((y + 1) % 4) * 2 + zl), to(e, ((y + 3) % 4) * 2 + zl), to(e, dbar)
    x_r_dev, x_l_dev = to(expert_at((x + 1) % 4, zh, c), d), to(expert_at((x + 3) % 4, zh, c), d)
    z_p = to(expert_at(x, 1 - zh, c), dbar)
    peers, places, mine, parts = [expert_at(x, zh, 1 - c)], [1 - c], [c], [0]
    row_peers = []
    for here, seen, x2, zh2 in others(x, zh):
        for c2 in (0, 1):
            peers.append(expert_at(x2, zh2, c2))
            places.append(here * 2 + c2)
            mine.append(seen * 2 + c)
            parts.append(here // 4)
            d2 = d if here < 4 else dbar
            row_peers.append((here, seen, expert_at(x2, zh2, c2), d2, x2 * 2 + c2))
    dps = [(d + k) % NDP for k in range(1, NDP)]

    partners = (
        [to(e2, d) for e2 in peers] + [to(e, d2) for d2 in dps]
        + [to(p[2], dbar) for p in row_peers if p[0] >= 4]
    )
    barrier = pltpu.get_barrier_semaphore()
    for dev in partners:
        pl.semaphore_signal(barrier, inc=1, device_id=dev, device_id_type=MESH)

    R = ids_ref.shape[1]
    loads = [
        pltpu.make_async_copy(
            ref.at[:, j * W : (j + 1) * W], dxc.at[j, a * R : (a + 1) * R], in_s.at[a, j]
        )
        for a, ref in ((0, x_hbm), (1, dy_hbm))
        for j in range(NDP)
    ]
    loads += [
        pltpu.make_async_copy(ref, weights.at[i], loc.at[3 + i])
        for i, ref in enumerate((wg_hbm, wu_hbm, wd_hbm))
    ]
    for copy in loads:
        copy.start()
    ids = ids_ref[...]
    onehot, rank = row_facts(ids, E)
    maps = slot_maps(ids, rank)
    for copy in loads[: 2 * NDP]:
        copy.wait()
    for a in (0, 1):
        for g, chunk in ((0, d), (1, dbar)):
            block = dxc[chunk, a * R : (a + 1) * R, :]
            s1[a, g] = jnp.dot(maps[g], block, preferred_element_type=f32).astype(bf16)
    pl.semaphore_wait(barrier, len(partners))

    rest = []

    def send(src, dst, ssem, rsem, dev):
        copy = pltpu.make_async_remote_copy(
            src, dst, ssem, rsem, device_id=dev, device_id_type=MESH
        )
        copy.start()
        rest.append(copy)

    def wait(ref, ssem, rsem):
        pltpu.make_async_remote_copy(
            ref, ref, ssem, rsem, device_id=sib, device_id_type=MESH
        ).wait_recv()

    def slots_at(n):
        return pl.ds(pl.multiple_of(n * SLOT, SLOT), SLOT)

    for a in (0, 1):
        for here, seen, e2, d2, q in row_peers:
            if a == 0 and here in (1, 2):
                continue
            pltpu.make_async_remote_copy(
                s1.at[a, here // 4, slots_at(q), :], cold.at[a, d2, slots_at(seen * 2 + c), :],
                st_s.at[a], st_r.at[a], device_id=to(e2, d2), device_id_type=MESH,
            ).start()
    def lay(j, _):
        got = jnp.dot(maps[2], dxc[j, 0:R, :], preferred_element_type=f32).astype(bf16)
        s2[0, j] = got[: 3 * SLOT]
        s3[j] = got[3 * SLOT :]
        got = jnp.dot(maps[2][: 3 * SLOT], dxc[j, R : 2 * R, :], preferred_element_type=f32)
        s2[1, j] = got.astype(bf16)
        return 0

    lax.fori_loop(0, NDP, lay, 0)
    send(s2.at[:, :, SLOT : 2 * SLOT, :], cold.at[:, :, slots_at(c), :], sib_s, sib_r, sib)

    def dp_piece(a, j, z, h):
        start = (3 if a == 0 else 1) * 2 * SLOT
        half = (ROWS - start) // 2
        rows = {None: (start, 2 * half), 0: (start, half), 1: (start + half, half)}[h]
        return cold.at[a, j * 2 + z, pl.ds(*rows), :]

    def ex_piece_of(core):
        def piece(a, j, z, h):
            chunks = {None: (0, NDP), 0: (0, NDP // 2), 1: (NDP // 2, NDP // 2)}[h]
            return extra.at[a, pl.ds(*chunks), slots_at(expert_at(j, z, core)), :]
        return piece

    ex_piece, ex_other = ex_piece_of(c), ex_piece_of(1 - c)
    dp = Gather(
        lambda a: dp_piece(a, y, zl, None), dp_piece, y, zl, right, left, pair, dp_s, dp_r
    )
    ex = Gather(
        lambda a: s2.at[a, :, 2 * SLOT :, :], ex_piece, x, zh, x_r_dev, x_l_dev, z_p, ex_s, ex_r
    )
    C = Scatter(
        lambda a, j, z: dxc.at[pl.ds(j * 2 + z, 1), pl.ds(a * HR, HR)],
        lambda ref, h: ref.at[:, pl.ds(h * (HR // 2), HR // 2)],
        y, zl, right, left, pair, c_refs,
    )
    X = Scatter(
        lambda a, j, z: hs.at[j * 2 + z, pl.ds(a * (NDP // 2), NDP // 2)],
        lambda ref, h: ref.at[pl.ds(h * (NDP // 4), NDP // 4)],
        x, zh, x_r_dev, x_l_dev, z_p, h_refs,
    )
    shares = []

    def share(a, j, z, src=None):
        i = len(shares)
        dst = ex_piece(a, j, z, None)
        send(dst if src is None else src, dst, xs_s.at[i], xs_r.at[i], sib)
        shares.append((a, j, z))

    def whole(a):
        ref = dp_piece(a, y, zl, None)
        return pltpu.make_async_remote_copy(
            ref, ref, st_s.at[a], st_r.at[a], device_id=sib, device_id_type=MESH
        )

    def cols(j):
        return pl.ds(pl.multiple_of(j * W, W), W)

    def forward_x(rows, t, at, n):
        def step(i, _):
            j = at(i)
            xj = rows[0, j]
            acc[t, 0] += nt(wg[:, cols(j)], xj)
            acc[t, 1] += nt(wu[:, cols(j)], xj)
            return 0

        lax.fori_loop(0, n, step, 0)

    def forward_dy(rows, t, at, n):
        def step(i, _):
            j = at(i)
            acc[t, 2] += nt(wd[:, cols(j)], rows[1, j])
            return 0

        lax.fori_loop(0, n, step, 0)

    def between(t):
        gate = gate_row(mr, t)
        pre, up, g = acc[t, 0], acc[t, 1], acc[t, 2]
        s = sigmoid(pre)
        active = pre * s
        hidden = (active * up).astype(bf16).astype(f32)
        gp[0:1, t * ROWS : (t + 1) * ROWS] = jnp.sum(hidden * g, axis=0, keepdims=True)
        gh = g * gate
        d_up = gh * active
        d_pre = gh * up * s * (1.0 + pre * (1.0 - s))
        lhs[t, 0] = d_pre.astype(bf16)
        lhs[t, 1] = d_up.astype(bf16)
        lhs[t, 2] = (hidden * gate).astype(bf16)
        rhs[t, :, 0:FFL] = d_pre.T.astype(bf16)
        rhs[t, :, FFL : 2 * FFL] = d_up.T.astype(bf16)

    def rows_back(t, out, at, n):
        def step(i, _):
            j = at(i)
            r = jnp.dot(rhs[t, :, 0:FFL], wg[:, cols(j)], preferred_element_type=f32)
            r += jnp.dot(rhs[t, :, FFL : 2 * FFL], wu[:, cols(j)], preferred_element_type=f32)
            out[j] = r.astype(bf16)
            return 0

        lax.fori_loop(0, n, step, 0)

    outs = (gg, gu, gd)

    def weights_back(first, sq):
        def step(j, sq):
            for i in range(3):
                v = jnp.dot(lhs[0, i], cold[i // 2, j], preferred_element_type=f32)
                v += jnp.dot(lhs[1, i], extra[i // 2, j], preferred_element_type=f32)
                outs[i][:, cols(j)] = v
                sq = sq + jnp.sum((v * v).reshape(-1, 8, W), axis=0)
            return sq

        return lax.fori_loop(first, first + 2, step, sq)

    ex.start(1)
    ex.start(0)
    for i, (x2, seen) in enumerate((((x + 1) % 4, 2), ((x + 3) % 4, 1))):
        for c2 in (0, 1):
            send(
                s3.at[:, pl.ds((i * 2 + c2) * SLOT, SLOT), :],
                cold.at[0, :, slots_at(seen * 2 + c), :],
                sd_s.at[i * 2 + c2], sd_r.at[(seen - 1) * 2 + c], to(expert_at(x2, zh, c2), d),
            )
    share(0, x, zh, s2.at[0, :, 2 * SLOT :, :])
    share(1, x, zh, s2.at[1, :, 2 * SLOT :, :])
    fill_meta(ms, ids, logits_ref[...], onehot, rank)
    meta_peers = row_peers + [(0, 0, expert_at(x, zh, 1 - c), d, 0)]
    for n, (_, seen, e2, d2, _) in enumerate(meta_peers):
        send(ms.at[e2], mr.at[seen * 2 + c], m_s.at[n], m_r.at[seen * 2 + c], to(e2, d2))
    own_in = [
        pltpu.make_async_copy(s2.at[:, :, 0:SLOT, :], cold.at[:, :, slots_at(c), :], loc.at[0]),
        pltpu.make_async_copy(s2.at[:, :, 2 * SLOT :, :], extra.at[:, :, slots_at(e), :], loc.at[1]),
        pltpu.make_async_copy(ms.at[e], mr.at[c], loc.at[2]),
    ]
    for copy in own_in:
        copy.start()
    acc[...] = jnp.zeros_like(acc)
    whole(0).wait_recv()
    dp.start(0)
    whole(1).wait_recv()
    dp.start(1)
    for copy in own_in + loads[2 * NDP :]:
        copy.wait()
    wait(cold.at[:, :, slots_at(1 - c), :], sib_s, sib_r)
    ex.s2()
    ex.s3()
    dp.s2()
    dp.s3()
    ex.s4()
    ex.s5()
    ex.s6()
    for a, j, z in ((0, ex.jl, zh), (0, ex.jr, zh), (1, x, 1 - zh), (1, ex.jl, zh), (1, ex.jr, zh)):
        share(a, j, z)
    dp.s4()
    dp.s5()
    dp.s6()
    ex.s7()
    ex.s8()
    share(0, ex.jd, zh)
    dp.s7()
    dp.s8()
    for i in range(4):
        wait(cold.at[0, :, pl.ds((2 + i) * SLOT, SLOT), :], sd_s.at[0], sd_r.at[i])
    forward_x(cold, 0, lambda i: d, 1)
    forward_dy(cold, 0, lambda i: d, 1)
    forward_x(cold, 0, lambda i: ((y + 1 + 2 * i) % 4) * 2 + zl, 2)
    ex.s9()
    ex.s10()
    share(1, ex.jl, 1 - zh)
    share(1, ex.jr, 1 - zh)
    dp.s9()
    dp.s10()
    forward_dy(cold, 0, lambda i: ((y + 1 + 2 * i) % 4) * 2 + zl, 2)
    forward_dy(cold, 0, lambda i: dbar, 1)
    dp.got("0oz", 0, y, 1 - zl, None)
    forward_x(cold, 0, lambda i: i * (dp.jd * 2 + zl) + (1 - i) * dbar, 2)
    ex.got("0oz", 0, x, 1 - zh, None)
    share(0, x, 1 - zh)
    ex.got("0lz", 0, ex.jl, 1 - zh, None)
    share(0, ex.jl, 1 - zh)
    ex.got("0rz", 0, ex.jr, 1 - zh, None)
    share(0, ex.jr, 1 - zh)
    ex.end_of_1_d()
    share(1, ex.jd, zh)
    ex.end_of_1_e()
    share(1, ex.jd, 1 - zh)
    ex.end_of_0_d()
    share(0, ex.jd, 1 - zh)
    forward_dy(cold, 0, lambda i: ((y + 1 + 2 * i) % 4) * 2 + 1 - zl, 2)
    for i in [1 - c] + list(range(2, E)):
        wait(mr.at[i], m_s.at[0], m_r.at[i])
    dp.end_of_1_d()
    forward_dy(cold, 0, lambda i: dp.jd * 2 + zl, 1)
    dp.got("0lz", 0, dp.jl, 1 - zl, None)
    dp.got("0rz", 0, dp.jr, 1 - zl, None)
    forward_x(cold, 0, lambda i: ((y + 1 + 2 * i) % 4) * 2 + 1 - zl, 2)
    dp.end_of_1_e()
    forward_dy(cold, 0, lambda i: dp.jd * 2 + 1 - zl, 1)
    dp.end_of_0_d()
    forward_x(cold, 0, lambda i: dp.jd * 2 + 1 - zl, 1)
    between(0)

    rows_back(0, dxc, lambda i: C.jd * 2 + i, 2)
    C.start0_far()
    C.start1("d")
    rows_back(0, dxc, lambda i: C.jr * 2 + i, 2)
    C.start0_right()
    C.start1("r")
    rows_back(0, dxc, lambda i: C.jl * 2 + i, 2)
    C.start0_left()
    C.start1("l")
    rows_back(0, dxc, lambda i: y * 2 + i, 2)
    C.start1("0")
    for i, where in enumerate(shares):
        wait(ex_other(*where, None), xs_s.at[i], xs_r.at[i])
    forward_x(extra, 1, lambda i: i, NDP)
    forward_dy(extra, 1, lambda i: i, NDP)
    between(1)
    C.relay0()
    C.relay1_far()
    far = [X.jd * 2, X.jd * 2 + 1, X.jr * 2, X.jl * 2, X.jr * 2 + 1, X.jl * 2 + 1, x * 2, x * 2 + 1]
    rows_back(1, dxh, lambda i: i, NDP)

    def h_rows(chip, core):
        return slots_at(chip * 2 + core)

    for i, chip in enumerate(far):
        send(dxh.at[:, h_rows(chip, 1 - c)], hin.at[chip], x_s.at[i], x_r.at[i], sib)
    C.relay1_near()
    for i, chip in enumerate(far):
        wait(hin.at[chip], x_s.at[i], x_r.at[i])
        add_into(hs.at[chip], dxh.at[:, h_rows(chip, c)], hin.at[chip])
        if i == 1:
            X.start0_far()
        if i == 5:
            X.start0_right()
            X.start0_left()
    for way in ("d", "r", "l", "0"):
        X.start1(way)
    C.pair0()
    C.relay1_last()
    sq = weights_back(0, jnp.zeros((8, W), f32))
    X.relay0()
    X.relay1_far()
    X.relay1_near()
    sq = weights_back(2, sq)
    X.relay1_last()
    X.pair0()
    sq = weights_back(4, sq)

    def give(a):
        for n, e2 in enumerate(peers):
            if parts[n] == a:
                send(
                    rc.at[0, slots_at(places[n]), :],
                    back.at[e], b_s.at[n], b_r.at[mine[n]], to(e2, d),
                )

    sq = weights_back(6, sq)
    total = jnp.sum(jnp.sum(sq, axis=0, keepdims=True), axis=1, keepdims=True)
    gp[0:1, 2 * ROWS :] = jnp.broadcast_to(total, (1, GW - 2 * ROWS))
    for k, d2 in enumerate(dps):
        send(gp, gall.at[d], g_s.at[k], g_r.at[k], to(e, d2))
    gall[d] = gp[...]
    C.end1(rc.at[:, pl.ds(HR, HR)])
    give(1)
    C.end0(rc.at[:, pl.ds(0, HR)])
    give(0)
    back[e] = rc[0, slots_at(c), :]
    X.end1(outh.at[pl.ds(NDP // 2, NDP // 2)])
    X.end0(outh.at[pl.ds(0, NDP // 2)])
    for k, d2 in enumerate(dps):
        send(outh.at[d2], hp.at[d], q_s.at[k], q_r.at[k], to(e, d2))
    hp[d] = outh[d]
    for k in range(NDP - 1):
        wait(gall.at[(d + NDP - 1 - k) % NDP], g_s.at[k], g_r.at[k])
    total = gall[0]
    for k in range(1, NDP):
        total = total + gall[k]
    gsum[...] = total
    gback[e] = total
    for n, e2 in enumerate(peers):
        send(gsum, gback.at[e], gb_s.at[n], gb_r.at[mine[n]], to(e2, d))
    for k in range(NDP - 1):
        wait(hp.at[(d + NDP - 1 - k) % NDP], q_s.at[k], q_r.at[k])
    total = hp[0].astype(f32)
    for k in range(1, NDP):
        total = total + hp[k].astype(f32)
    backh[...] = total.astype(bf16)

    for i in [1 - c] + list(range(2, E)):
        wait(back.at[0], b_s.at[0], b_r.at[i])
        wait(gback.at[0], gb_s.at[0], gb_r.at[i])
    whole(0).wait_send()
    whole(1).wait_send()
    for copy in rest:
        copy.wait_send()
    dp.drain()
    ex.drain()
    C.drain()
    X.drain()


def moe(ids, logits, x, dy, wg, wu, wd):
    FFL, width = wg.shape
    D = pltpu.SemaphoreType.DMA
    V = pltpu.VMEM
    return pl.pallas_call(
        moe_kernel,
        in_specs=[VM, VM] + [ANY] * 5,
        out_specs=[VM] * 7,
        out_shape=[
            pltpu.VMEM((E, SLOT, W), bf16),
            pltpu.VMEM((SLOT, W), bf16),
            pltpu.VMEM((E, 1, GW), f32),
            pltpu.VMEM((E, 8, 128), f32),
        ]
        + [pltpu.VMEM((FFL, width), f32)] * 3,
        scratch_shapes=Scatter.scratch(C_PIECE, C_HALF)
        + Scatter.scratch(H_PIECE, H_HALF)
        + [
            V((2, 2, ROWS // 2, W), bf16), V((2, NDP, 3 * SLOT, W), bf16),
            V((NDP, 4 * SLOT, W), bf16), V((E, 8, 128), f32), D((2, NDP)),
            V((2, NDP, ROWS, W), bf16), V((2, NDP, ROWS, W), bf16),
            V((3, FFL, width), bf16),
            V((2, 3, FFL, ROWS), f32), V((2, 3, FFL, ROWS), bf16), V((2, ROWS, 2 * FFL), bf16),
            V((NDP, ROWS, W), bf16), V((NDP, ROWS, W), bf16), V((1, GW), f32),
            V((1, ROWS, W), bf16),
            V((NDP, NDP, SLOT, W), bf16), V((NDP, NDP, SLOT, W), bf16),
            V((NDP, SLOT, W), bf16), V((NDP, SLOT, W), bf16),
            V((NDP, 1, GW), f32), V((1, GW), f32),
            D((2,)), D((2,)), D((4,)), D((4,)), D((15,)), D((16,)), D, D,
            D((18,)), D((18,)), D((18,)), D((18,)), D((16,)), D((16,)), D((6,)),
            D((7,)), D((7,)), D((15,)), D((16,)), D((15,)), D((16,)),
            D((8,)), D((8,)), D((7,)), D((7,)),
        ],
        compiler_params=pltpu.CompilerParams(
            collective_id=1, has_side_effects=True, vmem_limit_bytes=54 * 1024 * 1024
        ),
        name="moe",
    )(ids, logits, x, dy, wg, wu, wd)


def finish_kernel(
    ids_ref, logits_ref, back, backh, gback, mr, g1, g2, g3,
    rows_ref, gl_ref, norm_ref, o1, o2, o3, osem,
):
    stores = [
        pltpu.make_async_copy(g, o, osem.at[i])
        for i, (g, o) in enumerate(((g1, o1), (g2, o2), (g3, o3)))
    ]
    for copy in stores:
        copy.start()
    finish_rows(ids_ref, logits_ref, back, backh, gback, mr, rows_ref, gl_ref, norm_ref)
    for copy in stores:
        copy.wait()


def finish_rows(ids_ref, logits_ref, back, backh, gback, mr, rows_ref, gl_ref, norm_ref):
    e, _, x, zh, c, _, _ = place()
    ids = ids_ref[...]
    onehot, rank = row_facts(ids, E)
    probs = soft(logits_ref[...])
    n = ids.shape[1]
    first = rank < SLOT
    slot = lax.broadcasted_iota(jnp.int32, (ROWS, n), 0)
    pick = (slot == jnp.where(first, ids * SLOT + rank, -1)).astype(f32).astype(bf16)
    slot = lax.broadcasted_iota(jnp.int32, (SLOT, n), 0)
    pickh = (slot == rank - SLOT).astype(f32).astype(bf16)
    got = tn(pick, back[...].reshape(ROWS, W)) + tn(pickh, backh[...])
    rows_ref[...] = got.astype(bf16)
    rel = seen_from(ids, x, zh, c)
    lane = jnp.where(first, rel * SLOT + rank, ROWS + e * SLOT + rank - SLOT)
    slot = lax.broadcasted_iota(jnp.int32, (2 * ROWS, n), 0)
    here = (slot == lane).astype(f32).astype(bf16)
    found = jnp.dot(gback[:, 0, 0 : 2 * ROWS].astype(bf16), here, preferred_element_type=f32)
    dgate = jnp.sum(onehot * found, axis=0, keepdims=True)
    count = jnp.sum(mr[...], axis=0)[2:3, :]
    across = lax.broadcasted_iota(jnp.int32, (E, 128), 0)
    diag = across == lax.broadcasted_iota(jnp.int32, (E, 128), 1)
    column = jnp.sum(jnp.where(diag, jnp.broadcast_to(count, (E, 128)), 0.0), axis=1, keepdims=True)
    pulls = onehot * dgate + 1.0 * E * (column / (E * n))
    gl_ref[...] = probs * (pulls - jnp.sum(probs * pulls, axis=0, keepdims=True))
    norm_ref[...] = jnp.sqrt(jnp.sum(gback[:, 0, 2 * ROWS : 2 * ROWS + 128], axis=0, keepdims=True))


def finish(ids, logits, back, backh, gback, mr, *grads):
    n = ids.shape[1]
    return pl.pallas_call(
        finish_kernel,
        in_specs=[VM] * 9,
        out_specs=[VM] * 3 + [ANY] * 3,
        out_shape=[
            jax.ShapeDtypeStruct((n, W), bf16),
            jax.ShapeDtypeStruct((E, n), f32),
            jax.ShapeDtypeStruct((1, 128), f32),
        ]
        + [jax.ShapeDtypeStruct(g.shape, f32) for g in grads],
        scratch_shapes=[
            pltpu.SemaphoreType.DMA((3,)),
        ],
        compiler_params=pltpu.CompilerParams(vmem_limit_bytes=20 * 1024 * 1024),
        name="finish",
    )(ids, logits, back, backh, gback, mr, *grads)


def local(rows_x, rows_dy, router_logits, expert_of, w_gate, w_up, w_down):
    ids = expert_of.reshape(1, -1)
    logits = router_logits.T
    back, backh, gback, mr, gg, gu, gd = moe(
        ids, logits, rows_x, rows_dy, w_gate[0], w_up[0], w_down[0]
    )
    held = (back, backh, gback, mr, gg, gu, gd)
    held = [pltpu.with_memory_space_constraint(v, pltpu.VMEM) for v in held]
    grad_rows, grad_logits, norm, gg, gu, gd = finish(ids, logits, *held)
    return grad_rows, grad_logits.T, gg[None], gu[None], gd[None], norm[0, 0]


def solution(mesh):
    rows = P("expert", None)
    weights = P("expert", "dp", None)
    return jax.shard_map(
        local,
        mesh=mesh,
        in_specs=(rows, rows, rows, rows, weights, weights, weights),
        out_specs=(P("expert", "dp"), rows, weights, weights, weights, P()),
        check_vma=False,
    )
```
